128 devices in a mesh: fsdp: 8 (over x, z_lo), ctx: 2 (over z_hi), tp: 8 (over y, core).
Axes of the slice: x: 4, y: 4, z: 4 (z_hi: 2, z_lo: 2; z = z_hi * 2 + z_lo), core: 2. Of those that a mesh axis runs over, the one named last changes fastest.
Arguments:
- tokens: float32 [6144, 1024], P(('fsdp', 'ctx')), may hold values from -30 to 30
- cotangent: float32 [6144, 1024], P(('fsdp', 'ctx')), may hold values from -6 to 6
- segments: int32 [8, 768], P('fsdp'), may hold values from 0 to 3, never falling along the last dimension, each value on 1 to 384 neighbouring positions
- attention_norm_weight: float32 [2, 1024], replicated, may hold values from 0.25 to 1.75
- query_gain: float32 [2, 128], replicated, may hold values from 0.25 to 1.75
- key_gain: float32 [2, 128], replicated, may hold values from 0.25 to 1.75
- feedforward_gain: float32 [2, 1024], replicated, may hold values from 0.25 to 1.75
- query_weight: bfloat16 [2, 1024, 2048], P(None, ('fsdp', 'ctx'), 'tp'), may hold values from -0.1875 to 0.1875
- key_projection_matrix: bfloat16 [2, 1024, 1024], P(None, ('fsdp', 'ctx'), 'tp'), may hold values from -0.1875 to 0.1875
- value_projection_matrix: bfloat16 [2, 1024, 1024], P(None, ('fsdp', 'ctx'), 'tp'), may hold values from -0.1875 to 0.1875
- output_weight: bfloat16 [2, 1024, 2048], P(None, ('fsdp', 'ctx'), 'tp'), may hold values from -0.75 to 0.75
- gate_weight: bfloat16 [2, 1024, 3072], P(None, ('fsdp', 'ctx'), 'tp'), may hold values from -0.1875 to 0.1875
- up_weight: bfloat16 [2, 1024, 3072], P(None, ('fsdp', 'ctx'), 'tp'), may hold values from -0.1875 to 0.1875
- down_weight: bfloat16 [2, 1024, 3072], P(None, ('fsdp', 'ctx'), 'tp'), may hold values from -0.15625 to 0.15625
Outputs:
- block_output: float32 [6144, 1024], P(('fsdp', 'ctx'))
- token_grad: float32 [6144, 1024], P(('fsdp', 'ctx'))
- attention_gain_grad: float32 [2, 1024], replicated
- query_gain_grad: float32 [2, 128], replicated
- key_gain_grad: float32 [2, 128], replicated
- feedforward_gain_grad: float32 [2, 1024], replicated
- query_weight_grad: float32 [2, 1024, 2048], P(None, ('fsdp', 'ctx'), 'tp')
- key_weight_grad: float32 [2, 1024, 1024], P(None, ('fsdp', 'ctx'), 'tp')
- value_weight_grad: float32 [2, 1024, 1024], P(None, ('fsdp', 'ctx'), 'tp')
- output_weight_grad: float32 [2, 1024, 2048], P(None, ('fsdp', 'ctx'), 'tp')
- gate_weight_grad: float32 [2, 1024, 3072], P(None, ('fsdp', 'ctx'), 'tp')
- up_weight_grad: float32 [2, 1024, 3072], P(None, ('fsdp', 'ctx'), 'tp')
- down_weight_grad: float32 [2, 1024, 3072], P(None, ('fsdp', 'ctx'), 'tp')
The draws below stay inside these ranges and needn't reach their ends.
Inputs may be any that keep to these rules, and one draw needn't show every extreme that they name: `segments`: within each sequence the numbers never fall; each of the 4 documents has 1 to 384 tokens, one exactly 384.
All inputs are finite; a program needn't handle non-finite values.
Results may differ from the reference program's by a relative error of at most 0.04.
Values may be sent and summed in bfloat16 or wider, within the bound.
No kernel may reach another device: no remote copies, remote signals or barrier semaphores. Data moves between devices by JAX's collectives and lax.ppermute only.
A program may use at most 128 MiB of HBM per device.

```python
import math
import jax
import jax.numpy as jnp
import numpy as np
from jax import lax

MODEL_DIMENSION = 1024
HQ = 16
KEY_VALUE_HEADS = 8
HEAD_DIMENSION = 128
FF = 3072
DECODER_LAYERS = 2
LEN = 768
DOCS = 4
TOKENS = 6144
DOC_MOST = 384
N_FSDP = 8
N_TP = 8


def draw_tokens(key, part):
    row_key, column_key, base_key = jax.random.split(key, 3)
    row_factor = jnp.exp(jax.random.uniform(row_key, (TOKENS, 1), jnp.float32, -1.15, 1.15))
    column_factor = jnp.exp(jax.random.uniform(column_key, (1, MODEL_DIMENSION), jnp.float32, -1.15, 1.15))
    base = jnp.clip(jax.random.normal(base_key, (TOKENS, MODEL_DIMENSION), jnp.float32), -5.0, 5.0)
    return (0.3 * base * row_factor * column_factor).astype(jnp.float32)


def shard_levels(stream_key, dims, cuts, least, high):
    level = 1.0
    for position, parts in cuts:
        draws = jax.random.uniform(jax.random.fold_in(jax.random.fold_in(stream_key, 6), position), (parts,), jnp.float32, least / len(cuts), high / len(cuts))
        level = level * jnp.repeat(jnp.exp(draws), dims[position] // parts).reshape((-1,) + (1,) * (len(dims) - 1 - position))
    return level


def profile(count, total, limit, skew):
    portions = [(1 << 20) // math.isqrt(rank ** skew) + 1 for rank in range(2, count + 1)]
    spare, given = total - limit - (count - 1), [1] * (count - 1)
    while spare > 0:
        free = [i for i in range(count - 1) if given[i] < limit]
        mass, remaining = sum([portions[i] for i in free]), spare
        for i in free:
            extra = min(limit - given[i], max(1, remaining * portions[i] // mass), spare)
            given[i] = given[i] + extra
            spare = spare - extra
    return np.array([limit] + given)


def uneven(stream_key, number_of, total, most, slope):
    if number_of == 2:
        one = jax.random.randint(stream_key, (), max(1, total - most), min(most, total - 1) + 1)
        return jnp.stack([one, total - one])
    lengths = jnp.asarray(profile(number_of, total, most, slope), jnp.int32)
    pairs = (number_of - 1) // 2
    source_of, receiver = lengths[1:1 + 2 * pairs:2], lengths[2:2 + 2 * pairs:2]
    room = jnp.minimum(source_of - 1, most - receiver)
    shifted = jax.random.randint(jax.random.fold_in(stream_key, 1), (pairs,), 0, 1 << 20) % (room + 1)
    lengths = lengths.at[1:1 + 2 * pairs:2].set(source_of - shifted).at[2:2 + 2 * pairs:2].set(receiver + shifted)
    return lengths[jax.random.permutation(jax.random.fold_in(stream_key, 2), number_of)]


def bell_draw(rng, shape, width, reach, pieces=(), kind=jnp.bfloat16):
    factor_of = shard_levels(rng, shape, pieces, -0.22, 0.18) if pieces else 1.0
    values = jax.random.normal(rng, shape, jnp.float32) * width * factor_of
    return jnp.minimum(jnp.maximum(values, -reach), reach).astype(kind)


def setup_inputs(seed: int = 0) -> dict:
    key_of = jax.random.split(jax.random.key(seed), 15)
    tokens = draw_tokens(jax.random.fold_in(key_of[14], 71), 0)
    cotangent = bell_draw(key_of[1], (TOKENS, MODEL_DIMENSION), 1.0, 6.0, ((0, 16),), jnp.float32)
    segments = jax.vmap(lambda own: jnp.searchsorted(jnp.cumsum(uneven(own, DOCS, LEN, DOC_MOST, 0)), jnp.arange(LEN), side="right"))(jax.random.split(key_of[2], N_FSDP)).reshape((N_FSDP, LEN)).astype(jnp.int32)
    attention_norm_weight = jnp.clip(1.0 + 0.15 * jax.random.normal(key_of[3], (DECODER_LAYERS, MODEL_DIMENSION), jnp.float32), 0.25, 1.75)
    query_gain = jnp.clip(1.0 + 0.15 * jax.random.normal(key_of[4], (DECODER_LAYERS, HEAD_DIMENSION), jnp.float32), 0.25, 1.75)
    key_gain = jnp.clip(1.0 + 0.15 * jax.random.normal(key_of[5], (DECODER_LAYERS, HEAD_DIMENSION), jnp.float32), 0.25, 1.75)
    feedforward_gain = jnp.clip(1.0 + 0.15 * jax.random.normal(key_of[6], (DECODER_LAYERS, MODEL_DIMENSION), jnp.float32), 0.25, 1.75)
    query_weight = bell_draw(key_of[7], (DECODER_LAYERS, MODEL_DIMENSION, HQ * HEAD_DIMENSION), MODEL_DIMENSION ** -0.5, 0.1875, ((1, 16), (2, 8)))
    key_projection_matrix = bell_draw(key_of[8], (DECODER_LAYERS, MODEL_DIMENSION, KEY_VALUE_HEADS * HEAD_DIMENSION), MODEL_DIMENSION ** -0.5, 0.1875, ((1, 16), (2, 8)))
    value_projection_matrix = bell_draw(key_of[9], (DECODER_LAYERS, MODEL_DIMENSION, KEY_VALUE_HEADS * HEAD_DIMENSION), MODEL_DIMENSION ** -0.5, 0.1875, ((1, 16), (2, 8)))
    output_weight = bell_draw(key_of[10], (DECODER_LAYERS, MODEL_DIMENSION, HQ * HEAD_DIMENSION), (HQ * HEAD_DIMENSION // 32) ** -0.5, 0.75, ((1, 16), (2, 8)))
    gate_weight = bell_draw(key_of[11], (DECODER_LAYERS, MODEL_DIMENSION, FF), MODEL_DIMENSION ** -0.5, 0.1875, ((1, 16), (2, 8)))
    up_weight = bell_draw(key_of[12], (DECODER_LAYERS, MODEL_DIMENSION, FF), MODEL_DIMENSION ** -0.5, 0.1875, ((1, 16), (2, 8)))
    down_weight = bell_draw(key_of[13], (DECODER_LAYERS, MODEL_DIMENSION, FF), (FF // 2) ** -0.5, 0.15625, ((1, 16), (2, 8)))
    return dict(tokens=tokens, cotangent=cotangent, segments=segments, attention_norm_weight=attention_norm_weight, query_gain=query_gain, key_gain=key_gain, feedforward_gain=feedforward_gain, query_weight=query_weight, key_projection_matrix=key_projection_matrix, value_projection_matrix=value_projection_matrix, output_weight=output_weight, gate_weight=gate_weight, up_weight=up_weight, down_weight=down_weight)


eps = 1e-06
rope_base = 1000000.0

def row_scale(source):
    return lax.rsqrt(lax.optimization_barrier(jnp.mean(source * source, axis=-1, keepdims=True)) + eps)

def norm_back(grad_out, normalized, scaling, norm_gain):
    weighted = grad_out * norm_gain
    return scaling * (weighted - normalized * lax.optimization_barrier(jnp.mean(weighted * normalized, axis=-1, keepdims=True)))

def rotary_tables(positions, head_size):
    halfway = head_size // 2
    frequency = rope_base ** (-2.0 * jnp.arange(halfway, dtype=jnp.float32) / head_size)
    angles = positions.astype(jnp.float32)[:, None] * frequency[None, :]
    return (jnp.cos(angles)[:, None, :], jnp.sin(angles)[:, None, :])

def rotate(source, cosine_table, sine_table):
    halfway = source.shape[-1] // 2
    leading = source[..., :halfway]
    trailing = source[..., halfway:]
    return jnp.concatenate([leading * cosine_table - trailing * sine_table, trailing * cosine_table + leading * sine_table], axis=-1)

def narrowed(source):
    return lax.optimization_barrier(source.astype(jnp.bfloat16)).astype(jnp.float32)

def group_sum(pairs):
    left_parts = []
    right_parts = []
    for left_side, right_side in pairs:
        left_parts.append(left_side.astype(jnp.float32).reshape(left_side.shape[0], N_TP, -1))
        right_parts.append(right_side.astype(jnp.float32).reshape(right_side.shape[0], N_TP, -1))
    partials = jnp.einsum('tgk,dgk->gtd', jnp.concatenate(left_parts, axis=2), jnp.concatenate(right_parts, axis=2))
    return lax.optimization_barrier(jnp.sum(narrowed(partials), axis=0))

def attention_scores(query_groups, key_groups):
    head_size = key_groups.shape[-1]
    return jnp.einsum('qgrd,kgd->grqk', query_groups.astype(jnp.float32), key_groups.astype(jnp.float32)) * head_size ** (-0.5)

def forward_layer(source, allowed, cosine_table, sine_table, layer_params):
    attention_norm, query_norm, key_norm, feed_norm, query_full, key_full, value_full, output_full, gate_full, up_full, down_full = layer_params
    seq_length = source.shape[0]
    head_size = query_norm.shape[0]
    heads_all = query_full.shape[1] // head_size
    groups_all = key_full.shape[1] // head_size
    per_group = heads_all // groups_all
    scale_one = row_scale(source)
    normed = (source * scale_one * attention_norm).astype(jnp.bfloat16)
    query_raw = jnp.dot(normed, query_full, preferred_element_type=jnp.float32).reshape(seq_length, heads_all, head_size)
    key_raw = jnp.dot(normed, key_full, preferred_element_type=jnp.float32).reshape(seq_length, groups_all, head_size)
    values = jnp.dot(normed, value_full, preferred_element_type=jnp.float32).astype(jnp.bfloat16)
    query_scale = row_scale(query_raw)
    query_unit = query_raw * query_scale
    key_scale = row_scale(key_raw)
    key_unit = key_raw * key_scale
    queries = rotate(query_unit * query_norm, cosine_table, sine_table).astype(jnp.bfloat16)
    keys = rotate(key_unit * key_norm, cosine_table, sine_table).astype(jnp.bfloat16)
    query_groups = queries.reshape(seq_length, groups_all, per_group, head_size)
    value_groups = values.reshape(seq_length, groups_all, head_size)
    scores = attention_scores(query_groups, keys)
    exponent = jnp.where(allowed, jnp.exp(scores), 0.0)
    log_total = jnp.log(lax.optimization_barrier(jnp.sum(exponent, axis=-1, keepdims=True)))
    probs = jnp.where(allowed, jnp.exp(scores - log_total), 0.0).astype(jnp.bfloat16)
    attended = jnp.einsum('grqk,kgd->qgrd', probs.astype(jnp.float32), value_groups.astype(jnp.float32))
    attended = attended.astype(jnp.bfloat16).reshape(seq_length, heads_all * head_size)
    middle = source + group_sum([(attended, output_full)])
    scale_two = row_scale(middle)
    feed_normed = (middle * scale_two * feed_norm).astype(jnp.bfloat16)
    gate_linear = jnp.dot(feed_normed, gate_full, preferred_element_type=jnp.float32)
    up_linear = jnp.dot(feed_normed, up_full, preferred_element_type=jnp.float32)
    activated = (jax.nn.silu(gate_linear) * up_linear).astype(jnp.bfloat16)
    result = middle + group_sum([(activated, down_full)])
    stored = (source, scale_one, normed, query_unit, query_scale, key_unit, key_scale, query_groups, keys, value_groups, log_total, attended, middle, scale_two, feed_normed, gate_linear, up_linear, activated)
    return (stored, result)

def backward_layer(grad_in, allowed, cosine_table, sine_table, layer_params, stored):
    attention_norm, query_norm, key_norm, feed_norm, query_full, key_full, value_full, output_full, gate_full, up_full, down_full = layer_params
    source, scale_one, normed, query_unit, query_scale, key_unit, key_scale, query_groups, keys, value_groups, log_total, attended, middle, scale_two, feed_normed, gate_linear, up_linear, activated = stored
    seq_length = source.shape[0]
    head_size = query_norm.shape[0]
    heads_all = query_full.shape[1] // head_size
    groups_all = key_full.shape[1] // head_size
    per_group = heads_all // groups_all
    grad_half = grad_in.astype(jnp.bfloat16)
    down_grad = jnp.dot(grad_half.T, activated, preferred_element_type=jnp.float32)
    act_grad = jnp.dot(grad_half, down_full, preferred_element_type=jnp.float32)
    sigmoid_gate = jax.nn.sigmoid(gate_linear)
    gate_grad = (act_grad * up_linear * sigmoid_gate * (1.0 + gate_linear * (1.0 - sigmoid_gate))).astype(jnp.bfloat16)
    up_grad = (act_grad * jax.nn.silu(gate_linear)).astype(jnp.bfloat16)
    gate_weight_grad = jnp.dot(feed_normed.T, gate_grad, preferred_element_type=jnp.float32)
    up_weight_grad = jnp.dot(feed_normed.T, up_grad, preferred_element_type=jnp.float32)
    feed_grad = group_sum([(gate_grad, gate_full), (up_grad, up_full)])
    feed_unit = middle * scale_two
    feed_gain_grad = lax.optimization_barrier(jnp.sum(feed_grad * feed_unit, axis=0))
    middle_grad = grad_in + norm_back(feed_grad, feed_unit, scale_two, feed_norm)
    middle_half = middle_grad.astype(jnp.bfloat16)
    output_weight_grad = jnp.dot(middle_half.T, attended, preferred_element_type=jnp.float32)
    attended_grad = jnp.dot(middle_half, output_full, preferred_element_type=jnp.float32).astype(jnp.bfloat16)
    attended_grad = attended_grad.reshape(seq_length, groups_all, per_group, head_size).astype(jnp.float32)
    scores = attention_scores(query_groups, keys)
    exact = jnp.where(allowed, jnp.exp(scores - log_total), 0.0)
    half_probs = exact.astype(jnp.bfloat16).astype(jnp.float32)
    value_grad = jnp.einsum('grqk,qgrd->kgd', half_probs, attended_grad)
    prob_grad = jnp.einsum('qgrd,kgd->grqk', attended_grad, value_groups.astype(jnp.float32))
    row_delta = lax.optimization_barrier(jnp.sum(exact * prob_grad, axis=-1, keepdims=True))
    score_grad = (exact * (prob_grad - row_delta) * head_size ** (-0.5)).astype(jnp.bfloat16).astype(jnp.float32)
    query_grad = jnp.einsum('grqk,kgd->qgrd', score_grad, keys.astype(jnp.float32)).reshape(seq_length, heads_all, head_size)
    key_grad = jnp.einsum('grqk,qgrd->kgd', score_grad, query_groups.astype(jnp.float32))
    query_turned = rotate(query_grad, cosine_table, -sine_table)
    key_turned = rotate(key_grad, cosine_table, -sine_table)
    query_gain_grad = lax.optimization_barrier(jnp.sum(query_turned * query_unit, axis=(0, 1)))
    key_gain_grad = lax.optimization_barrier(jnp.sum(key_turned * key_unit, axis=(0, 1)))
    query_pre = norm_back(query_turned, query_unit, query_scale, query_norm).astype(jnp.bfloat16).reshape(seq_length, heads_all * head_size)
    key_pre = norm_back(key_turned, key_unit, key_scale, key_norm).astype(jnp.bfloat16).reshape(seq_length, groups_all * head_size)
    value_pre = value_grad.astype(jnp.bfloat16).reshape(seq_length, groups_all * head_size)
    query_weight_grad = jnp.dot(normed.T, query_pre, preferred_element_type=jnp.float32)
    key_weight_grad = jnp.dot(normed.T, key_pre, preferred_element_type=jnp.float32)
    value_weight_grad = jnp.dot(normed.T, value_pre, preferred_element_type=jnp.float32)
    normed_grad = group_sum([(query_pre, query_full), (key_pre, key_full), (value_pre, value_full)])
    source_unit = source * scale_one
    attention_gain_grad = lax.optimization_barrier(jnp.sum(normed_grad * source_unit, axis=0))
    source_grad = middle_grad + norm_back(normed_grad, source_unit, scale_one, attention_norm)
    gradients = (attention_gain_grad, query_gain_grad, key_gain_grad, feed_gain_grad, query_weight_grad, key_weight_grad, value_weight_grad, output_weight_grad, gate_weight_grad, up_weight_grad, down_grad)
    return (source_grad, gradients)

def sequence_pass(source, upstream, segment_row, params):
    seq_length = source.shape[0]
    head_size = params[1].shape[1]
    positions = jnp.arange(seq_length, dtype=jnp.int32)
    allowed = (segment_row[:, None] == segment_row[None, :]) & (positions[None, :] <= positions[:, None])
    cosine_table, sine_table = rotary_tables(positions, head_size)
    layer_count = params[0].shape[0]
    stored_layers = []
    hidden = source
    for layer_index in range(layer_count):
        layer_params = tuple((member[layer_index] for member in params))
        stored, hidden = forward_layer(hidden, allowed, cosine_table, sine_table, layer_params)
        stored_layers.append(stored)
    grad_flow = upstream
    per_layer = [None] * layer_count
    for layer_index in reversed(range(layer_count)):
        layer_params = tuple((member[layer_index] for member in params))
        grad_flow, gradients = backward_layer(grad_flow, allowed, cosine_table, sine_table, layer_params, stored_layers[layer_index])
        per_layer[layer_index] = gradients
    stacked = tuple((jnp.stack([per_layer[layer_index][which] for layer_index in range(layer_count)]) for which in range(len(params))))
    return (hidden, grad_flow, stacked)

def reference(tokens, cotangent, segments, attention_norm_weight, query_gain, key_gain, feedforward_gain, query_weight, key_projection_matrix, value_projection_matrix, output_weight, gate_weight, up_weight, down_weight):
    params = (attention_norm_weight, query_gain, key_gain, feedforward_gain, query_weight, key_projection_matrix, value_projection_matrix, output_weight, gate_weight, up_weight, down_weight)
    token_blocks = tokens.reshape(N_FSDP, LEN, MODEL_DIMENSION)
    upstream_blocks = cotangent.reshape(N_FSDP, LEN, MODEL_DIMENSION)
    initial = tuple((jnp.zeros(member.shape, jnp.float32) for member in params))

    def one_sequence(carry, inputs):
        source, upstream, segment_row = inputs
        output_rows, grad_rows, gradients = sequence_pass(source, upstream, segment_row, params)
        totals = tuple((total + piece for total, piece in zip(carry, gradients)))
        return (totals, (output_rows, grad_rows))
    totals, (outputs, token_grads) = lax.scan(one_sequence, initial, (token_blocks, upstream_blocks, segments))
    return (outputs.reshape(TOKENS, MODEL_DIMENSION), token_grads.reshape(TOKENS, MODEL_DIMENSION), totals[0], totals[1], totals[2], totals[3], totals[4], totals[5], totals[6], totals[7], totals[8], totals[9], totals[10])
```

```python
import jax
import jax.numpy as jnp
from jax import lax
from jax.sharding import PartitionSpec as P

eps = 1e-06
rope_base = 1000000.0


def contract_last(left_side, right_side):
    return lax.dot_general(
        left_side, right_side, (((1,), (1,)), ((), ())), preferred_element_type=jnp.float32
    )


def contract_first(left_side, right_side):
    return lax.dot_general(
        left_side, right_side, (((0,), (0,)), ((), ())), preferred_element_type=jnp.float32
    )


def row_scale(source):
    return lax.rsqrt(jnp.mean(source * source, axis=-1, keepdims=True) + eps)


def norm_back(grad_out, normalized, scaling, norm_gain):
    weighted = grad_out * norm_gain
    return scaling * (
        weighted - normalized * jnp.mean(weighted * normalized, axis=-1, keepdims=True)
    )


def rotary_tables(positions, head_size):
    halfway = head_size // 2
    frequency = rope_base ** (-2.0 * jnp.arange(halfway, dtype=jnp.float32) / head_size)
    angles = positions.astype(jnp.float32)[:, None] * frequency[None, :]
    return (jnp.cos(angles)[:, None, :], jnp.sin(angles)[:, None, :])


def rotate(source, cosine_table, sine_table):
    halfway = source.shape[-1] // 2
    leading = source[..., :halfway]
    trailing = source[..., halfway:]
    return jnp.concatenate(
        [
            leading * cosine_table - trailing * sine_table,
            trailing * cosine_table + leading * sine_table,
        ],
        axis=-1,
    )


def per_device(
    tokens,
    cotangent,
    segments,
    attention_norm_weight,
    query_gain,
    key_gain,
    feedforward_gain,
    query_weight,
    key_projection_matrix,
    value_projection_matrix,
    output_weight,
    gate_weight,
    up_weight,
    down_weight,
):
    row_count = tokens.shape[0]
    model_width = tokens.shape[1]
    head_size = query_gain.shape[1]
    local_heads = query_weight.shape[2] // head_size
    local_groups = key_projection_matrix.shape[2] // head_size
    per_group = local_heads // local_groups
    layer_count = query_weight.shape[0]
    seq_length = segments.shape[1]
    row_start = lax.axis_index("ctx") * row_count
    column_width = model_width // lax.axis_size("tp")
    column_start = lax.axis_index("tp") * column_width
    score_scale = head_size ** (-0.5)
    positions = row_start + jnp.arange(row_count, dtype=jnp.int32)
    segment_row = segments[0]
    query_ids = lax.dynamic_slice_in_dim(segment_row, row_start, row_count)
    key_positions = jnp.arange(seq_length, dtype=jnp.int32)
    allowed = (query_ids[:, None] == segment_row[None, :]) & (
        key_positions[None, :] <= positions[:, None]
    )
    cosine_table, sine_table = rotary_tables(positions, head_size)

    def column_share(grad_rows, normalized):
        gradient_portion = lax.dynamic_slice_in_dim(grad_rows, column_start, column_width, 1)
        unit_slice = lax.dynamic_slice_in_dim(normalized, column_start, column_width, 1)
        part_sum = jnp.sum(gradient_portion * unit_slice, axis=0)
        return lax.dynamic_update_slice_in_dim(
            jnp.zeros((model_width,), jnp.float32), part_sum, column_start, 0
        )

    def attention_scores(query_groups, key_groups):
        return (
            jnp.einsum(
                "qgrd,kgd->grqk", query_groups, key_groups, preferred_element_type=jnp.float32
            )
            * score_scale
        )

    weight_shards = (
        query_weight,
        key_projection_matrix,
        value_projection_matrix,
        output_weight,
        gate_weight,
        up_weight,
        down_weight,
    )
    widths = [member.shape[2] for member in weight_shards]
    edges = [0]
    for width in widths:
        edges.append(edges[-1] + width)

    def gather_layer(layer_index):
        joined = jnp.concatenate([member[layer_index] for member in weight_shards], axis=1)
        full = lax.all_gather(joined, ("fsdp", "ctx"), axis=0, tiled=True)
        return tuple(full[:, edges[k] : edges[k + 1]] for k in range(len(widths)))

    def scatter_layer(terms):
        joined = jnp.concatenate([term.astype(jnp.bfloat16) for term in terms], axis=1)
        owned = lax.psum_scatter(joined, ("fsdp", "ctx"), scatter_dimension=0, tiled=True)
        return tuple(
            owned[:, edges[k] : edges[k + 1]].astype(jnp.float32) for k in range(len(widths))
        )

    kept_weights = []
    stored_layers = []
    hidden = tokens
    for layer_index in range(layer_count):
        gathered = gather_layer(layer_index)
        kept_weights.append(gathered)
        (
            forward_query_full,
            forward_key_full,
            forward_value_full,
            forward_output_full,
            forward_gate_full,
            forward_up_full,
            forward_down_full,
        ) = gathered
        forward_scale_one = row_scale(hidden)
        forward_normed = (hidden * forward_scale_one * attention_norm_weight[layer_index]).astype(
            jnp.bfloat16
        )
        query_raw = jnp.dot(
            forward_normed, forward_query_full, preferred_element_type=jnp.float32
        ).reshape(row_count, local_heads, head_size)
        key_raw = jnp.dot(
            forward_normed, forward_key_full, preferred_element_type=jnp.float32
        ).reshape(row_count, local_groups, head_size)
        values = jnp.dot(
            forward_normed, forward_value_full, preferred_element_type=jnp.float32
        ).astype(jnp.bfloat16)
        forward_query_scale = row_scale(query_raw)
        forward_query_unit = query_raw * forward_query_scale
        forward_key_scale = row_scale(key_raw)
        forward_key_unit = key_raw * forward_key_scale
        queries = rotate(
            forward_query_unit * query_gain[layer_index], cosine_table, sine_table
        ).astype(jnp.bfloat16)
        keys = rotate(forward_key_unit * key_gain[layer_index], cosine_table, sine_table).astype(
            jnp.bfloat16
        )
        keys = keys.reshape(row_count, local_groups * head_size)
        all_keys = lax.all_gather(keys, "ctx", axis=0, tiled=True)
        all_values = lax.all_gather(values, "ctx", axis=0, tiled=True)
        forward_query_groups = queries.reshape(row_count, local_groups, per_group, head_size)
        forward_key_groups = all_keys.reshape(seq_length, local_groups, head_size)
        forward_value_groups = all_values.reshape(seq_length, local_groups, head_size)
        forward_scores = attention_scores(forward_query_groups, forward_key_groups)
        exponent = jnp.where(allowed, jnp.exp(forward_scores), 0.0)
        forward_log_total = jnp.log(jnp.sum(exponent, axis=-1, keepdims=True))
        attention_probs = jnp.where(
            allowed, jnp.exp(forward_scores - forward_log_total), 0.0
        ).astype(jnp.bfloat16)
        forward_attended = jnp.einsum(
            "grqk,kgd->qgrd",
            attention_probs,
            forward_value_groups,
            preferred_element_type=jnp.float32,
        )
        forward_attended = forward_attended.astype(jnp.bfloat16).reshape(
            row_count, local_heads * head_size
        )
        forward_middle = hidden + lax.psum(
            contract_last(forward_attended, forward_output_full).astype(jnp.bfloat16), "tp"
        ).astype(jnp.float32)
        forward_scale_two = row_scale(forward_middle)
        forward_feed_normed = (
            forward_middle * forward_scale_two * feedforward_gain[layer_index]
        ).astype(jnp.bfloat16)
        forward_gate_linear = jnp.dot(
            forward_feed_normed, forward_gate_full, preferred_element_type=jnp.float32
        )
        forward_up_linear = jnp.dot(
            forward_feed_normed, forward_up_full, preferred_element_type=jnp.float32
        )
        forward_activated = (jax.nn.silu(forward_gate_linear) * forward_up_linear).astype(
            jnp.bfloat16
        )
        result = forward_middle + lax.psum(
            contract_last(forward_activated, forward_down_full).astype(jnp.bfloat16), "tp"
        ).astype(jnp.float32)
        forward_stored = (
            hidden,
            forward_scale_one,
            forward_normed,
            forward_query_unit,
            forward_query_scale,
            forward_key_unit,
            forward_key_scale,
            forward_query_groups,
            forward_key_groups,
            forward_value_groups,
            forward_log_total,
            forward_attended,
            forward_middle,
            forward_scale_two,
            forward_feed_normed,
            forward_gate_linear,
            forward_up_linear,
            forward_activated,
        )
        hidden = result
        stored_layers.append(forward_stored)
    grad_flow = cotangent
    weight_sums = [None] * layer_count
    gain_parts = [None] * layer_count
    for layer_index in reversed(range(layer_count)):
        gathered = kept_weights[layer_index]
        backward_stored = stored_layers[layer_index]
        query_full, key_full, value_full, output_full, gate_full, up_full, down_full = gathered
        (
            source,
            scale_one,
            normed,
            query_unit,
            query_scale,
            key_unit,
            key_scale,
            backward_query_groups,
            backward_key_groups,
            value_groups,
            log_total,
            attended,
            middle,
            scale_two,
            feed_normed,
            gate_linear,
            up_linear,
            activated,
        ) = backward_stored
        grad_half = grad_flow.astype(jnp.bfloat16)
        down_grad = contract_first(grad_half, activated)
        act_grad = jnp.dot(grad_half, down_full, preferred_element_type=jnp.float32)
        sigmoid_gate = jax.nn.sigmoid(gate_linear)
        gate_grad = (
            act_grad * up_linear * sigmoid_gate * (1.0 + gate_linear * (1.0 - sigmoid_gate))
        ).astype(jnp.bfloat16)
        up_grad = (act_grad * jax.nn.silu(gate_linear)).astype(jnp.bfloat16)
        gate_weight_grad = contract_first(feed_normed, gate_grad)
        up_weight_grad = contract_first(feed_normed, up_grad)
        feed_part = contract_last(gate_grad, gate_full) + contract_last(up_grad, up_full)
        feed_grad = lax.psum(feed_part.astype(jnp.bfloat16), "tp").astype(jnp.float32)
        feed_unit = middle * scale_two
        feed_gain_grad = column_share(feed_grad, feed_unit)
        middle_grad = grad_flow + norm_back(
            feed_grad, feed_unit, scale_two, feedforward_gain[layer_index]
        )
        middle_half = middle_grad.astype(jnp.bfloat16)
        output_weight_grad = contract_first(middle_half, attended)
        attended_grad = jnp.dot(
            middle_half, output_full, preferred_element_type=jnp.float32
        ).astype(jnp.bfloat16)
        attended_grad = attended_grad.reshape(row_count, local_groups, per_group, head_size)
        scores = attention_scores(backward_query_groups, backward_key_groups)
        exact = jnp.where(allowed, jnp.exp(scores - log_total), 0.0)
        half_probs = exact.astype(jnp.bfloat16)
        value_grad = jnp.einsum(
            "grqk,qgrd->kgd", half_probs, attended_grad, preferred_element_type=jnp.float32
        )
        prob_grad = jnp.einsum(
            "qgrd,kgd->grqk", attended_grad, value_groups, preferred_element_type=jnp.float32
        )
        row_delta = jnp.sum(exact * prob_grad, axis=-1, keepdims=True)
        score_grad = (exact * (prob_grad - row_delta) * score_scale).astype(jnp.bfloat16)
        query_grad = jnp.einsum(
            "grqk,kgd->qgrd", score_grad, backward_key_groups, preferred_element_type=jnp.float32
        )
        query_grad = query_grad.reshape(row_count, local_heads, head_size)
        key_grad = jnp.einsum(
            "grqk,qgrd->kgd", score_grad, backward_query_groups, preferred_element_type=jnp.float32
        )
        key_own = lax.psum_scatter(
            key_grad.reshape(seq_length, local_groups * head_size).astype(jnp.bfloat16),
            "ctx",
            scatter_dimension=0,
            tiled=True,
        ).astype(jnp.float32)
        value_own = lax.psum_scatter(
            value_grad.reshape(seq_length, local_groups * head_size).astype(jnp.bfloat16),
            "ctx",
            scatter_dimension=0,
            tiled=True,
        )
        query_turned = rotate(query_grad, cosine_table, -sine_table)
        key_turned = rotate(
            key_own.reshape(row_count, local_groups, head_size), cosine_table, -sine_table
        )
        query_gain_grad = jnp.sum(query_turned * query_unit, axis=(0, 1))
        key_gain_grad = jnp.sum(key_turned * key_unit, axis=(0, 1))
        query_pre = norm_back(
            query_turned, query_unit, query_scale, query_gain[layer_index]
        ).astype(jnp.bfloat16)
        query_pre = query_pre.reshape(row_count, local_heads * head_size)
        key_pre = norm_back(key_turned, key_unit, key_scale, key_gain[layer_index]).astype(
            jnp.bfloat16
        )
        key_pre = key_pre.reshape(row_count, local_groups * head_size)
        query_weight_grad = contract_first(normed, query_pre)
        key_weight_grad = contract_first(normed, key_pre)
        value_weight_grad = contract_first(normed, value_own)
        attention_part = (
            contract_last(query_pre, query_full)
            + contract_last(key_pre, key_full)
            + contract_last(value_own, value_full)
        )
        normed_grad = lax.psum(attention_part.astype(jnp.bfloat16), "tp").astype(jnp.float32)
        source_unit = source * scale_one
        attention_gain_grad = column_share(normed_grad, source_unit)
        source_grad = middle_grad + norm_back(
            normed_grad, source_unit, scale_one, attention_norm_weight[layer_index]
        )
        weight_terms = (
            query_weight_grad,
            key_weight_grad,
            value_weight_grad,
            output_weight_grad,
            gate_weight_grad,
            up_weight_grad,
            down_grad,
        )
        gain_terms = (attention_gain_grad, query_gain_grad, key_gain_grad, feed_gain_grad)
        grad_flow, weight_terms, gain_terms = (source_grad, weight_terms, gain_terms)
        grad_query, grad_key, grad_value, grad_output, grad_gate, grad_up, grad_down = weight_terms
        weight_sums[layer_index] = scatter_layer(weight_terms)
        gain_parts[layer_index] = gain_terms
    gain_totals = lax.psum(
        (
            jnp.stack([member[0] for member in gain_parts]),
            jnp.stack([member[1] for member in gain_parts]),
            jnp.stack([member[2] for member in gain_parts]),
            jnp.stack([member[3] for member in gain_parts]),
        ),
        ("fsdp", "ctx", "tp"),
    )
    stacked = [jnp.stack([member[which] for member in weight_sums]) for which in range(7)]
    return (
        hidden,
        grad_flow,
        gain_totals[0],
        gain_totals[1],
        gain_totals[2],
        gain_totals[3],
        stacked[0],
        stacked[1],
        stacked[2],
        stacked[3],
        stacked[4],
        stacked[5],
        stacked[6],
    )


def solution(mesh):
    in_specs = (
        P(("fsdp", "ctx"), None),
        P(("fsdp", "ctx"), None),
        P("fsdp", None),
        P(),
        P(),
        P(),
        P(),
        P(None, ("fsdp", "ctx"), "tp"),
        P(None, ("fsdp", "ctx"), "tp"),
        P(None, ("fsdp", "ctx"), "tp"),
        P(None, ("fsdp", "ctx"), "tp"),
        P(None, ("fsdp", "ctx"), "tp"),
        P(None, ("fsdp", "ctx"), "tp"),
        P(None, ("fsdp", "ctx"), "tp"),
    )
    out_specs = (
        P(("fsdp", "ctx"), None),
        P(("fsdp", "ctx"), None),
        P(),
        P(),
        P(),
        P(),
        P(None, ("fsdp", "ctx"), "tp"),
        P(None, ("fsdp", "ctx"), "tp"),
        P(None, ("fsdp", "ctx"), "tp"),
        P(None, ("fsdp", "ctx"), "tp"),
        P(None, ("fsdp", "ctx"), "tp"),
        P(None, ("fsdp", "ctx"), "tp"),
        P(None, ("fsdp", "ctx"), "tp"),
    )
    return jax.shard_map(
        per_device, mesh=mesh, in_specs=in_specs, out_specs=out_specs, check_vma=False
    )
```

```python
import jax
import jax.numpy as jnp
from jax import lax
from jax.sharding import PartitionSpec as P

eps = 1e-06
rope_base = 1000000.0


def contract_last(left_side, right_side):
    return lax.dot_general(
        left_side, right_side, (((1,), (1,)), ((), ())), preferred_element_type=jnp.float32
    )


def contract_first(left_side, right_side):
    return lax.dot_general(
        left_side, right_side, (((0,), (0,)), ((), ())), preferred_element_type=jnp.float32
    )


def row_scale(source):
    return lax.rsqrt(jnp.mean(source * source, axis=-1, keepdims=True) + eps)


def norm_back(grad_out, normalized, scaling, norm_gain):
    weighted = grad_out * norm_gain
    return scaling * (
        weighted - normalized * jnp.mean(weighted * normalized, axis=-1, keepdims=True)
    )


def rotary_tables(positions, head_size):
    halfway = head_size // 2
    frequency = rope_base ** (-2.0 * jnp.arange(halfway, dtype=jnp.float32) / head_size)
    angles = positions.astype(jnp.float32)[:, None] * frequency[None, :]
    return (jnp.cos(angles)[:, None, :], jnp.sin(angles)[:, None, :])


def rotate(source, cosine_table, sine_table):
    halfway = source.shape[-1] // 2
    leading = source[..., :halfway]
    trailing = source[..., halfway:]
    return jnp.concatenate(
        [
            leading * cosine_table - trailing * sine_table,
            trailing * cosine_table + leading * sine_table,
        ],
        axis=-1,
    )


def tp_sum(term):
    tp_count = lax.axis_size("tp")
    tp_index = lax.axis_index("tp")
    current = term.astype(jnp.bfloat16)
    bits = []
    step = 1
    while step < tp_count:
        bits.append(step)
        step *= 2
    for step in bits:
        half = current.shape[0] // 2
        upper = (tp_index // step) % 2
        kept = lax.dynamic_slice_in_dim(current, upper * half, half, 0)
        sent = lax.dynamic_slice_in_dim(current, (1 - upper) * half, half, 0)
        pairs = [(device, device ^ step) for device in range(tp_count)]
        received = lax.ppermute(sent.astype(jnp.bfloat16), "tp", pairs)
        current = kept.astype(jnp.float32) + received.astype(jnp.float32)
    current = current.astype(jnp.bfloat16)
    for step in reversed(bits):
        upper = (tp_index // step) % 2
        pairs = [(device, device ^ step) for device in range(tp_count)]
        received = lax.ppermute(current, "tp", pairs)
        current = jnp.where(
            upper == 0,
            jnp.concatenate([current, received], axis=0),
            jnp.concatenate([received, current], axis=0),
        )
    return current.astype(jnp.float32)


def per_device(
    tokens,
    cotangent,
    segments,
    attention_norm_weight,
    query_gain,
    key_gain,
    feedforward_gain,
    query_weight,
    key_projection_matrix,
    value_projection_matrix,
    output_weight,
    gate_weight,
    up_weight,
    down_weight,
):
    row_count = tokens.shape[0]
    model_width = tokens.shape[1]
    head_size = query_gain.shape[1]
    local_heads = query_weight.shape[2] // head_size
    local_groups = key_projection_matrix.shape[2] // head_size
    per_group = local_heads // local_groups
    layer_count = query_weight.shape[0]
    seq_length = segments.shape[1]
    row_start = lax.axis_index("ctx") * row_count
    column_width = model_width // lax.axis_size("tp")
    column_start = lax.axis_index("tp") * column_width
    score_scale = head_size ** (-0.5)
    positions = row_start + jnp.arange(row_count, dtype=jnp.int32)
    segment_row = segments[0]
    query_ids = lax.dynamic_slice_in_dim(segment_row, row_start, row_count)
    key_positions = jnp.arange(seq_length, dtype=jnp.int32)
    allowed = (query_ids[:, None] == segment_row[None, :]) & (
        key_positions[None, :] <= positions[:, None]
    )
    cosine_table, sine_table = rotary_tables(positions, head_size)

    def column_share(grad_rows, normalized):
        gradient_portion = lax.dynamic_slice_in_dim(grad_rows, column_start, column_width, 1)
        unit_slice = lax.dynamic_slice_in_dim(normalized, column_start, column_width, 1)
        part_sum = jnp.sum(gradient_portion * unit_slice, axis=0)
        return lax.dynamic_update_slice_in_dim(
            jnp.zeros((model_width,), jnp.float32), part_sum, column_start, 0
        )

    def attention_scores(query_groups, key_groups):
        return (
            jnp.einsum(
                "qgrd,kgd->grqk", query_groups, key_groups, preferred_element_type=jnp.float32
            )
            * score_scale
        )

    weight_shards = (
        query_weight,
        key_projection_matrix,
        value_projection_matrix,
        output_weight,
        gate_weight,
        up_weight,
        down_weight,
    )
    widths = [member.shape[2] for member in weight_shards]
    edges = [0]
    for width in widths:
        edges.append(edges[-1] + width)

    def gather_layer(layer_index):
        joined = jnp.concatenate([member[layer_index] for member in weight_shards], axis=1)
        full = lax.all_gather(joined, ("fsdp", "ctx"), axis=0, tiled=True)
        return tuple(full[:, edges[k] : edges[k + 1]] for k in range(len(widths)))

    def scatter_layer(terms):
        joined = jnp.concatenate([term.astype(jnp.bfloat16) for term in terms], axis=1)
        owned = lax.psum_scatter(joined, ("fsdp", "ctx"), scatter_dimension=0, tiled=True)
        return tuple(
            owned[:, edges[k] : edges[k + 1]].astype(jnp.float32) for k in range(len(widths))
        )

    kept_weights = []
    stored_layers = []
    hidden = tokens
    for layer_index in range(layer_count):
        gathered = gather_layer(layer_index)
        kept_weights.append(gathered)
        (
            forward_query_full,
            forward_key_full,
            forward_value_full,
            forward_output_full,
            forward_gate_full,
            forward_up_full,
            forward_down_full,
        ) = gathered
        forward_scale_one = row_scale(hidden)
        forward_normed = (hidden * forward_scale_one * attention_norm_weight[layer_index]).astype(
            jnp.bfloat16
        )
        query_raw = jnp.dot(
            forward_normed, forward_query_full, preferred_element_type=jnp.float32
        ).reshape(row_count, local_heads, head_size)
        key_raw = jnp.dot(
            forward_normed, forward_key_full, preferred_element_type=jnp.float32
        ).reshape(row_count, local_groups, head_size)
        values = jnp.dot(
            forward_normed, forward_value_full, preferred_element_type=jnp.float32
        ).astype(jnp.bfloat16)
        forward_query_scale = row_scale(query_raw)
        forward_query_unit = query_raw * forward_query_scale
        forward_key_scale = row_scale(key_raw)
        forward_key_unit = key_raw * forward_key_scale
        queries = rotate(
            forward_query_unit * query_gain[layer_index], cosine_table, sine_table
        ).astype(jnp.bfloat16)
        keys = rotate(forward_key_unit * key_gain[layer_index], cosine_table, sine_table).astype(
            jnp.bfloat16
        )
        keys = keys.reshape(row_count, local_groups * head_size)
        all_keys = lax.all_gather(keys, "ctx", axis=0, tiled=True)
        all_values = lax.all_gather(values, "ctx", axis=0, tiled=True)
        forward_query_groups = queries.reshape(row_count, local_groups, per_group, head_size)
        forward_key_groups = all_keys.reshape(seq_length, local_groups, head_size)
        forward_value_groups = all_values.reshape(seq_length, local_groups, head_size)
        forward_scores = attention_scores(forward_query_groups, forward_key_groups)
        exponent = jnp.where(allowed, jnp.exp(forward_scores), 0.0)
        forward_log_total = jnp.log(jnp.sum(exponent, axis=-1, keepdims=True))
        attention_probs = jnp.where(
            allowed, jnp.exp(forward_scores - forward_log_total), 0.0
        ).astype(jnp.bfloat16)
        forward_attended = jnp.einsum(
            "grqk,kgd->qgrd",
            attention_probs,
            forward_value_groups,
            preferred_element_type=jnp.float32,
        )
        forward_attended = forward_attended.astype(jnp.bfloat16).reshape(
            row_count, local_heads * head_size
        )
        forward_middle = hidden + tp_sum(contract_last(forward_attended, forward_output_full))
        forward_scale_two = row_scale(forward_middle)
        forward_feed_normed = (
            forward_middle * forward_scale_two * feedforward_gain[layer_index]
        ).astype(jnp.bfloat16)
        forward_gate_linear = jnp.dot(
            forward_feed_normed, forward_gate_full, preferred_element_type=jnp.float32
        )
        forward_up_linear = jnp.dot(
            forward_feed_normed, forward_up_full, preferred_element_type=jnp.float32
        )
        forward_activated = (jax.nn.silu(forward_gate_linear) * forward_up_linear).astype(
            jnp.bfloat16
        )
        result = forward_middle + tp_sum(contract_last(forward_activated, forward_down_full))
        forward_stored = (
            hidden,
            forward_scale_one,
            forward_normed,
            forward_query_unit,
            forward_query_scale,
            forward_key_unit,
            forward_key_scale,
            forward_query_groups,
            forward_key_groups,
            forward_value_groups,
            forward_log_total,
            forward_attended,
            forward_middle,
            forward_scale_two,
            forward_feed_normed,
            forward_gate_linear,
            forward_up_linear,
            forward_activated,
        )
        hidden = result
        stored_layers.append(forward_stored)
    grad_flow = cotangent
    weight_sums = [None] * layer_count
    gain_parts = [None] * layer_count
    for layer_index in reversed(range(layer_count)):
        gathered = kept_weights[layer_index]
        backward_stored = stored_layers[layer_index]
        query_full, key_full, value_full, output_full, gate_full, up_full, down_full = gathered
        (
            source,
            scale_one,
            normed,
            query_unit,
            query_scale,
            key_unit,
            key_scale,
            backward_query_groups,
            backward_key_groups,
            value_groups,
            log_total,
            attended,
            middle,
            scale_two,
            feed_normed,
            gate_linear,
            up_linear,
            activated,
        ) = backward_stored
        grad_half = grad_flow.astype(jnp.bfloat16)
        down_grad = contract_first(grad_half, activated)
        act_grad = jnp.dot(grad_half, down_full, preferred_element_type=jnp.float32)
        sigmoid_gate = jax.nn.sigmoid(gate_linear)
        gate_grad = (
            act_grad * up_linear * sigmoid_gate * (1.0 + gate_linear * (1.0 - sigmoid_gate))
        ).astype(jnp.bfloat16)
        up_grad = (act_grad * jax.nn.silu(gate_linear)).astype(jnp.bfloat16)
        gate_weight_grad = contract_first(feed_normed, gate_grad)
        up_weight_grad = contract_first(feed_normed, up_grad)
        feed_part = contract_last(gate_grad, gate_full) + contract_last(up_grad, up_full)
        feed_grad = tp_sum(feed_part)
        feed_unit = middle * scale_two
        feed_gain_grad = column_share(feed_grad, feed_unit)
        middle_grad = grad_flow + norm_back(
            feed_grad, feed_unit, scale_two, feedforward_gain[layer_index]
        )
        middle_half = middle_grad.astype(jnp.bfloat16)
        output_weight_grad = contract_first(middle_half, attended)
        attended_grad = jnp.dot(
            middle_half, output_full, preferred_element_type=jnp.float32
        ).astype(jnp.bfloat16)
        attended_grad = attended_grad.reshape(row_count, local_groups, per_group, head_size)
        scores = attention_scores(backward_query_groups, backward_key_groups)
        exact = jnp.where(allowed, jnp.exp(scores - log_total), 0.0)
        half_probs = exact.astype(jnp.bfloat16)
        value_grad = jnp.einsum(
            "grqk,qgrd->kgd", half_probs, attended_grad, preferred_element_type=jnp.float32
        )
        prob_grad = jnp.einsum(
            "qgrd,kgd->grqk", attended_grad, value_groups, preferred_element_type=jnp.float32
        )
        row_delta = jnp.sum(exact * prob_grad, axis=-1, keepdims=True)
        score_grad = (exact * (prob_grad - row_delta) * score_scale).astype(jnp.bfloat16)
        query_grad = jnp.einsum(
            "grqk,kgd->qgrd", score_grad, backward_key_groups, preferred_element_type=jnp.float32
        )
        query_grad = query_grad.reshape(row_count, local_heads, head_size)
        key_grad = jnp.einsum(
            "grqk,qgrd->kgd", score_grad, backward_query_groups, preferred_element_type=jnp.float32
        )
        key_own = lax.psum_scatter(
            key_grad.reshape(seq_length, local_groups * head_size).astype(jnp.bfloat16),
            "ctx",
            scatter_dimension=0,
            tiled=True,
        ).astype(jnp.float32)
        value_own = lax.psum_scatter(
            value_grad.reshape(seq_length, local_groups * head_size).astype(jnp.bfloat16),
            "ctx",
            scatter_dimension=0,
            tiled=True,
        )
        query_turned = rotate(query_grad, cosine_table, -sine_table)
        key_turned = rotate(
            key_own.reshape(row_count, local_groups, head_size), cosine_table, -sine_table
        )
        query_gain_grad = jnp.sum(query_turned * query_unit, axis=(0, 1))
        key_gain_grad = jnp.sum(key_turned * key_unit, axis=(0, 1))
        query_pre = norm_back(
            query_turned, query_unit, query_scale, query_gain[layer_index]
        ).astype(jnp.bfloat16)
        query_pre = query_pre.reshape(row_count, local_heads * head_size)
        key_pre = norm_back(key_turned, key_unit, key_scale, key_gain[layer_index]).astype(
            jnp.bfloat16
        )
        key_pre = key_pre.reshape(row_count, local_groups * head_size)
        query_weight_grad = contract_first(normed, query_pre)
        key_weight_grad = contract_first(normed, key_pre)
        value_weight_grad = contract_first(normed, value_own)
        attention_part = (
            contract_last(query_pre, query_full)
            + contract_last(key_pre, key_full)
            + contract_last(value_own, value_full)
        )
        normed_grad = tp_sum(attention_part)
        source_unit = source * scale_one
        attention_gain_grad = column_share(normed_grad, source_unit)
        source_grad = middle_grad + norm_back(
            normed_grad, source_unit, scale_one, attention_norm_weight[layer_index]
        )
        weight_terms = (
            query_weight_grad,
            key_weight_grad,
            value_weight_grad,
            output_weight_grad,
            gate_weight_grad,
            up_weight_grad,
            down_grad,
        )
        gain_terms = (attention_gain_grad, query_gain_grad, key_gain_grad, feed_gain_grad)
        grad_flow, weight_terms, gain_terms = (source_grad, weight_terms, gain_terms)
        grad_query, grad_key, grad_value, grad_output, grad_gate, grad_up, grad_down = weight_terms
        weight_sums[layer_index] = scatter_layer(weight_terms)
        gain_parts[layer_index] = gain_terms
    gain_totals = lax.psum(
        (
            jnp.stack([member[0] for member in gain_parts]),
            jnp.stack([member[1] for member in gain_parts]),
            jnp.stack([member[2] for member in gain_parts]),
            jnp.stack([member[3] for member in gain_parts]),
        ),
        ("fsdp", "ctx", "tp"),
    )
    stacked = [jnp.stack([member[which] for member in weight_sums]) for which in range(7)]
    return (
        hidden,
        grad_flow,
        gain_totals[0],
        gain_totals[1],
        gain_totals[2],
        gain_totals[3],
        stacked[0],
        stacked[1],
        stacked[2],
        stacked[3],
        stacked[4],
        stacked[5],
        stacked[6],
    )


def solution(mesh):
    in_specs = (
        P(("fsdp", "ctx"), None),
        P(("fsdp", "ctx"), None),
        P("fsdp", None),
        P(),
        P(),
        P(),
        P(),
        P(None, ("fsdp", "ctx"), "tp"),
        P(None, ("fsdp", "ctx"), "tp"),
        P(None, ("fsdp", "ctx"), "tp"),
        P(None, ("fsdp", "ctx"), "tp"),
        P(None, ("fsdp", "ctx"), "tp"),
        P(None, ("fsdp", "ctx"), "tp"),
        P(None, ("fsdp", "ctx"), "tp"),
    )
    out_specs = (
        P(("fsdp", "ctx"), None),
        P(("fsdp", "ctx"), None),
        P(),
        P(),
        P(),
        P(),
        P(None, ("fsdp", "ctx"), "tp"),
        P(None, ("fsdp", "ctx"), "tp"),
        P(None, ("fsdp", "ctx"), "tp"),
        P(None, ("fsdp", "ctx"), "tp"),
        P(None, ("fsdp", "ctx"), "tp"),
        P(None, ("fsdp", "ctx"), "tp"),
        P(None, ("fsdp", "ctx"), "tp"),
    )
    return jax.shard_map(
        per_device, mesh=mesh, in_specs=in_specs, out_specs=out_specs, check_vma=False
    )
```

```python
import jax
import jax.numpy as jnp
from jax import lax
from jax.sharding import PartitionSpec as P

eps = 1e-06
rope_base = 1000000.0


def contract_last(left_side, right_side):
    return lax.dot_general(
        left_side, right_side, (((1,), (1,)), ((), ())), preferred_element_type=jnp.float32
    )


def contract_first(left_side, right_side):
    return lax.dot_general(
        left_side, right_side, (((0,), (0,)), ((), ())), preferred_element_type=jnp.float32
    )


def row_scale(source):
    return lax.rsqrt(jnp.mean(source * source, axis=-1, keepdims=True) + eps)


def norm_back(grad_out, normalized, scaling, norm_gain):
    weighted = grad_out * norm_gain
    return scaling * (
        weighted - normalized * jnp.mean(weighted * normalized, axis=-1, keepdims=True)
    )


def rotary_tables(positions, head_size):
    halfway = head_size // 2
    frequency = rope_base ** (-2.0 * jnp.arange(halfway, dtype=jnp.float32) / head_size)
    angles = positions.astype(jnp.float32)[:, None] * frequency[None, :]
    return (jnp.cos(angles)[:, None, :], jnp.sin(angles)[:, None, :])


def rotate(source, cosine_table, sine_table):
    halfway = source.shape[-1] // 2
    leading = source[..., :halfway]
    trailing = source[..., halfway:]
    return jnp.concatenate(
        [
            leading * cosine_table - trailing * sine_table,
            trailing * cosine_table + leading * sine_table,
        ],
        axis=-1,
    )


def tp_sum(term):
    tp_count = lax.axis_size("tp")
    tp_index = lax.axis_index("tp")
    current = term.astype(jnp.bfloat16)
    bits = []
    step = 1
    while step < tp_count:
        bits.append(step)
        step *= 2
    for step in bits:
        half = current.shape[0] // 2
        upper = (tp_index // step) % 2
        kept = lax.dynamic_slice_in_dim(current, upper * half, half, 0)
        sent = lax.dynamic_slice_in_dim(current, (1 - upper) * half, half, 0)
        pairs = [(device, device ^ step) for device in range(tp_count)]
        received = lax.ppermute(sent.astype(jnp.bfloat16), "tp", pairs)
        current = kept.astype(jnp.float32) + received.astype(jnp.float32)
    current = current.astype(jnp.bfloat16)
    for step in reversed(bits):
        upper = (tp_index // step) % 2
        pairs = [(device, device ^ step) for device in range(tp_count)]
        received = lax.ppermute(current, "tp", pairs)
        current = jnp.where(
            upper == 0,
            jnp.concatenate([current, received], axis=0),
            jnp.concatenate([received, current], axis=0),
        )
    return current.astype(jnp.float32)


def swap_halves(local, axis_name):
    return lax.ppermute(local, axis_name, [(0, 1), (1, 0)])


def ctx_gather(local):
    other = swap_halves(local, "ctx")
    first = lax.axis_index("ctx") == 0
    return jnp.where(
        first, jnp.concatenate([local, other], axis=0), jnp.concatenate([other, local], axis=0)
    )


def ctx_scatter(full):
    rows = full.shape[0] // 2
    place = lax.axis_index("ctx")
    kept = lax.dynamic_slice_in_dim(full, place * rows, rows, 0)
    sent = lax.dynamic_slice_in_dim(full, (1 - place) * rows, rows, 0)
    received = swap_halves(sent.astype(jnp.bfloat16), "ctx")
    return kept.astype(jnp.bfloat16).astype(jnp.float32) + received.astype(jnp.float32)


def all_sum(value):
    total = value
    for axis_name in ("tp", "ctx", "fsdp"):
        count = lax.axis_size(axis_name)
        step = 1
        while step < count:
            pairs = [(device, device ^ step) for device in range(count)]
            total = total + lax.ppermute(total, axis_name, pairs)
            step *= 2
    return total


def per_device(
    tokens,
    cotangent,
    segments,
    attention_norm_weight,
    query_gain,
    key_gain,
    feedforward_gain,
    query_weight,
    key_projection_matrix,
    value_projection_matrix,
    output_weight,
    gate_weight,
    up_weight,
    down_weight,
):
    row_count = tokens.shape[0]
    model_width = tokens.shape[1]
    head_size = query_gain.shape[1]
    local_heads = query_weight.shape[2] // head_size
    local_groups = key_projection_matrix.shape[2] // head_size
    per_group = local_heads // local_groups
    layer_count = query_weight.shape[0]
    seq_length = segments.shape[1]
    row_start = lax.axis_index("ctx") * row_count
    column_width = model_width // lax.axis_size("tp")
    column_start = lax.axis_index("tp") * column_width
    score_scale = head_size ** (-0.5)
    positions = row_start + jnp.arange(row_count, dtype=jnp.int32)
    segment_row = segments[0]
    query_ids = lax.dynamic_slice_in_dim(segment_row, row_start, row_count)
    key_positions = jnp.arange(seq_length, dtype=jnp.int32)
    allowed = (query_ids[:, None] == segment_row[None, :]) & (
        key_positions[None, :] <= positions[:, None]
    )
    cosine_table, sine_table = rotary_tables(positions, head_size)

    def column_share(grad_rows, normalized):
        gradient_portion = lax.dynamic_slice_in_dim(grad_rows, column_start, column_width, 1)
        unit_slice = lax.dynamic_slice_in_dim(normalized, column_start, column_width, 1)
        part_sum = jnp.sum(gradient_portion * unit_slice, axis=0)
        return lax.dynamic_update_slice_in_dim(
            jnp.zeros((model_width,), jnp.float32), part_sum, column_start, 0
        )

    def attention_scores(query_groups, key_groups):
        return (
            jnp.einsum(
                "qgrd,kgd->grqk", query_groups, key_groups, preferred_element_type=jnp.float32
            )
            * score_scale
        )

    weight_shards = (
        query_weight,
        key_projection_matrix,
        value_projection_matrix,
        output_weight,
        gate_weight,
        up_weight,
        down_weight,
    )
    widths = [member.shape[2] for member in weight_shards]
    edges = [0]
    for width in widths:
        edges.append(edges[-1] + width)

    def gather_layer(layer_index):
        joined = jnp.concatenate([member[layer_index] for member in weight_shards], axis=1)
        full = lax.all_gather(joined, ("fsdp", "ctx"), axis=0, tiled=True)
        return tuple(full[:, edges[k] : edges[k + 1]] for k in range(len(widths)))

    def scatter_terms(terms):
        joined = jnp.concatenate([term.astype(jnp.bfloat16) for term in terms], axis=1)
        owned = lax.psum_scatter(joined, ("fsdp", "ctx"), scatter_dimension=0, tiled=True)
        pieces = []
        start = 0
        for term in terms:
            pieces.append(owned[:, start : start + term.shape[1]].astype(jnp.float32))
            start += term.shape[1]
        return pieces

    def scatter_layer(terms):
        return tuple(scatter_terms(terms[:4]) + scatter_terms(terms[4:]))

    kept_weights = []
    stored_layers = []
    hidden = tokens
    for layer_index in range(layer_count):
        gathered = gather_layer(layer_index)
        kept_weights.append(gathered)
        (
            forward_query_full,
            forward_key_full,
            forward_value_full,
            forward_output_full,
            forward_gate_full,
            forward_up_full,
            forward_down_full,
        ) = gathered
        forward_scale_one = row_scale(hidden)
        forward_normed = (hidden * forward_scale_one * attention_norm_weight[layer_index]).astype(
            jnp.bfloat16
        )
        query_raw = jnp.dot(
            forward_normed, forward_query_full, preferred_element_type=jnp.float32
        ).reshape(row_count, local_heads, head_size)
        key_raw = jnp.dot(
            forward_normed, forward_key_full, preferred_element_type=jnp.float32
        ).reshape(row_count, local_groups, head_size)
        values = jnp.dot(
            forward_normed, forward_value_full, preferred_element_type=jnp.float32
        ).astype(jnp.bfloat16)
        forward_query_scale = row_scale(query_raw)
        forward_query_unit = query_raw * forward_query_scale
        forward_key_scale = row_scale(key_raw)
        forward_key_unit = key_raw * forward_key_scale
        queries = rotate(
            forward_query_unit * query_gain[layer_index], cosine_table, sine_table
        ).astype(jnp.bfloat16)
        keys = rotate(forward_key_unit * key_gain[layer_index], cosine_table, sine_table).astype(
            jnp.bfloat16
        )
        keys = keys.reshape(row_count, local_groups * head_size)
        all_keys = ctx_gather(keys)
        all_values = ctx_gather(values)
        forward_query_groups = queries.reshape(row_count, local_groups, per_group, head_size)
        forward_key_groups = all_keys.reshape(seq_length, local_groups, head_size)
        forward_value_groups = all_values.reshape(seq_length, local_groups, head_size)
        forward_scores = attention_scores(forward_query_groups, forward_key_groups)
        exponent = jnp.where(allowed, jnp.exp(forward_scores), 0.0)
        forward_log_total = jnp.log(jnp.sum(exponent, axis=-1, keepdims=True))
        attention_probs = jnp.where(
            allowed, jnp.exp(forward_scores - forward_log_total), 0.0
        ).astype(jnp.bfloat16)
        forward_attended = jnp.einsum(
            "grqk,kgd->qgrd",
            attention_probs,
            forward_value_groups,
            preferred_element_type=jnp.float32,
        )
        forward_attended = forward_attended.astype(jnp.bfloat16).reshape(
            row_count, local_heads * head_size
        )
        forward_middle = hidden + tp_sum(contract_last(forward_attended, forward_output_full))
        forward_scale_two = row_scale(forward_middle)
        forward_feed_normed = (
            forward_middle * forward_scale_two * feedforward_gain[layer_index]
        ).astype(jnp.bfloat16)
        forward_gate_linear = jnp.dot(
            forward_feed_normed, forward_gate_full, preferred_element_type=jnp.float32
        )
        forward_up_linear = jnp.dot(
            forward_feed_normed, forward_up_full, preferred_element_type=jnp.float32
        )
        forward_activated = (jax.nn.silu(forward_gate_linear) * forward_up_linear).astype(
            jnp.bfloat16
        )
        result = forward_middle + tp_sum(contract_last(forward_activated, forward_down_full))
        forward_stored = (
            hidden,
            forward_scale_one,
            forward_normed,
            forward_query_unit,
            forward_query_scale,
            forward_key_unit,
            forward_key_scale,
            forward_query_groups,
            forward_key_groups,
            forward_value_groups,
            forward_log_total,
            forward_attended,
            forward_middle,
            forward_scale_two,
            forward_feed_normed,
            forward_gate_linear,
            forward_up_linear,
            forward_activated,
        )
        hidden = result
        stored_layers.append(forward_stored)
    grad_flow = cotangent
    weight_sums = [None] * layer_count
    gain_parts = [None] * layer_count
    for layer_index in reversed(range(layer_count)):
        gathered = kept_weights[layer_index]
        backward_stored = stored_layers[layer_index]
        query_full, key_full, value_full, output_full, gate_full, up_full, down_full = gathered
        (
            source,
            scale_one,
            normed,
            query_unit,
            query_scale,
            key_unit,
            key_scale,
            backward_query_groups,
            backward_key_groups,
            value_groups,
            log_total,
            attended,
            middle,
            scale_two,
            feed_normed,
            gate_linear,
            up_linear,
            activated,
        ) = backward_stored
        grad_half = grad_flow.astype(jnp.bfloat16)
        down_grad = contract_first(grad_half, activated)
        act_grad = jnp.dot(grad_half, down_full, preferred_element_type=jnp.float32)
        sigmoid_gate = jax.nn.sigmoid(gate_linear)
        gate_grad = (
            act_grad * up_linear * sigmoid_gate * (1.0 + gate_linear * (1.0 - sigmoid_gate))
        ).astype(jnp.bfloat16)
        up_grad = (act_grad * jax.nn.silu(gate_linear)).astype(jnp.bfloat16)
        gate_weight_grad = contract_first(feed_normed, gate_grad)
        up_weight_grad = contract_first(feed_normed, up_grad)
        feed_part = contract_last(gate_grad, gate_full) + contract_last(up_grad, up_full)
        feed_grad = tp_sum(feed_part)
        feed_unit = middle * scale_two
        feed_gain_grad = column_share(feed_grad, feed_unit)
        middle_grad = grad_flow + norm_back(
            feed_grad, feed_unit, scale_two, feedforward_gain[layer_index]
        )
        middle_half = middle_grad.astype(jnp.bfloat16)
        output_weight_grad = contract_first(middle_half, attended)
        attended_grad = jnp.dot(
            middle_half, output_full, preferred_element_type=jnp.float32
        ).astype(jnp.bfloat16)
        attended_grad = attended_grad.reshape(row_count, local_groups, per_group, head_size)
        scores = attention_scores(backward_query_groups, backward_key_groups)
        exact = jnp.where(allowed, jnp.exp(scores - log_total), 0.0)
        half_probs = exact.astype(jnp.bfloat16)
        value_grad = jnp.einsum(
            "grqk,qgrd->kgd", half_probs, attended_grad, preferred_element_type=jnp.float32
        )
        prob_grad = jnp.einsum(
            "qgrd,kgd->grqk", attended_grad, value_groups, preferred_element_type=jnp.float32
        )
        row_delta = jnp.sum(exact * prob_grad, axis=-1, keepdims=True)
        score_grad = (exact * (prob_grad - row_delta) * score_scale).astype(jnp.bfloat16)
        query_grad = jnp.einsum(
            "grqk,kgd->qgrd", score_grad, backward_key_groups, preferred_element_type=jnp.float32
        )
        query_grad = query_grad.reshape(row_count, local_heads, head_size)
        key_grad = jnp.einsum(
            "grqk,qgrd->kgd", score_grad, backward_query_groups, preferred_element_type=jnp.float32
        )
        key_own = ctx_scatter(key_grad.reshape(seq_length, local_groups * head_size))
        value_own = ctx_scatter(value_grad.reshape(seq_length, local_groups * head_size)).astype(
            jnp.bfloat16
        )
        query_turned = rotate(query_grad, cosine_table, -sine_table)
        key_turned = rotate(
            key_own.reshape(row_count, local_groups, head_size), cosine_table, -sine_table
        )
        query_gain_grad = jnp.sum(query_turned * query_unit, axis=(0, 1))
        key_gain_grad = jnp.sum(key_turned * key_unit, axis=(0, 1))
        query_pre = norm_back(
            query_turned, query_unit, query_scale, query_gain[layer_index]
        ).astype(jnp.bfloat16)
        query_pre = query_pre.reshape(row_count, local_heads * head_size)
        key_pre = norm_back(key_turned, key_unit, key_scale, key_gain[layer_index]).astype(
            jnp.bfloat16
        )
        key_pre = key_pre.reshape(row_count, local_groups * head_size)
        query_weight_grad = contract_first(normed, query_pre)
        key_weight_grad = contract_first(normed, key_pre)
        value_weight_grad = contract_first(normed, value_own)
        attention_part = (
            contract_last(query_pre, query_full)
            + contract_last(key_pre, key_full)
            + contract_last(value_own, value_full)
        )
        normed_grad = tp_sum(attention_part)
        source_unit = source * scale_one
        attention_gain_grad = column_share(normed_grad, source_unit)
        source_grad = middle_grad + norm_back(
            normed_grad, source_unit, scale_one, attention_norm_weight[layer_index]
        )
        weight_terms = (
            query_weight_grad,
            key_weight_grad,
            value_weight_grad,
            output_weight_grad,
            gate_weight_grad,
            up_weight_grad,
            down_grad,
        )
        gain_terms = (attention_gain_grad, query_gain_grad, key_gain_grad, feed_gain_grad)
        grad_flow, weight_terms, gain_terms = (source_grad, weight_terms, gain_terms)
        grad_query, grad_key, grad_value, grad_output, grad_gate, grad_up, grad_down = weight_terms
        weight_sums[layer_index] = scatter_layer(weight_terms)
        gain_parts[layer_index] = gain_terms
    gain_stacks = [
        jnp.stack([member[which] for member in gain_parts]) for which in range(4)
    ]
    gain_edges = [0]
    for member in gain_stacks:
        gain_edges.append(gain_edges[-1] + member.shape[1])
    gain_joined = all_sum(jnp.concatenate(gain_stacks, axis=1))
    gain_totals = [
        gain_joined[:, gain_edges[which] : gain_edges[which + 1]] for which in range(4)
    ]
    stacked = [jnp.stack([member[which] for member in weight_sums]) for which in range(7)]
    return (
        hidden,
        grad_flow,
        gain_totals[0],
        gain_totals[1],
        gain_totals[2],
        gain_totals[3],
        stacked[0],
        stacked[1],
        stacked[2],
        stacked[3],
        stacked[4],
        stacked[5],
        stacked[6],
    )


def solution(mesh):
    in_specs = (
        P(("fsdp", "ctx"), None),
        P(("fsdp", "ctx"), None),
        P("fsdp", None),
        P(),
        P(),
        P(),
        P(),
        P(None, ("fsdp", "ctx"), "tp"),
        P(None, ("fsdp", "ctx"), "tp"),
        P(None, ("fsdp", "ctx"), "tp"),
        P(None, ("fsdp", "ctx"), "tp"),
        P(None, ("fsdp", "ctx"), "tp"),
        P(None, ("fsdp", "ctx"), "tp"),
        P(None, ("fsdp", "ctx"), "tp"),
    )
    out_specs = (
        P(("fsdp", "ctx"), None),
        P(("fsdp", "ctx"), None),
        P(),
        P(),
        P(),
        P(),
        P(None, ("fsdp", "ctx"), "tp"),
        P(None, ("fsdp", "ctx"), "tp"),
        P(None, ("fsdp", "ctx"), "tp"),
        P(None, ("fsdp", "ctx"), "tp"),
        P(None, ("fsdp", "ctx"), "tp"),
        P(None, ("fsdp", "ctx"), "tp"),
        P(None, ("fsdp", "ctx"), "tp"),
    )
    return jax.shard_map(
        per_device, mesh=mesh, in_specs=in_specs, out_specs=out_specs, check_vma=False
    )
```

```python
import jax
import jax.numpy as jnp
from jax import lax
from jax.sharding import PartitionSpec as P

eps = 1e-06
rope_base = 1000000.0


def contract_last(left_side, right_side):
    return lax.dot_general(
        left_side, right_side, (((1,), (1,)), ((), ())), preferred_element_type=jnp.float32
    )


def contract_first(left_side, right_side):
    return lax.dot_general(
        left_side, right_side, (((0,), (0,)), ((), ())), preferred_element_type=jnp.float32
    )


def row_scale(source):
    return lax.rsqrt(jnp.mean(source * source, axis=-1, keepdims=True) + eps)


def norm_back(grad_out, normalized, scaling, norm_gain):
    weighted = grad_out * norm_gain
    return scaling * (
        weighted - normalized * jnp.mean(weighted * normalized, axis=-1, keepdims=True)
    )


def rotary_tables(positions, head_size):
    halfway = head_size // 2
    frequency = rope_base ** (-2.0 * jnp.arange(halfway, dtype=jnp.float32) / head_size)
    angles = positions.astype(jnp.float32)[:, None] * frequency[None, :]
    return (jnp.cos(angles)[:, None, :], jnp.sin(angles)[:, None, :])


def rotate(source, cosine_table, sine_table):
    halfway = source.shape[-1] // 2
    leading = source[..., :halfway]
    trailing = source[..., halfway:]
    return jnp.concatenate(
        [
            leading * cosine_table - trailing * sine_table,
            trailing * cosine_table + leading * sine_table,
        ],
        axis=-1,
    )


def tp_sum(term):
    tp_count = lax.axis_size("tp")
    tp_index = lax.axis_index("tp")
    current = term.astype(jnp.bfloat16)
    bits = []
    step = 1
    while step < tp_count:
        bits.append(step)
        step *= 2
    for step in bits:
        half = current.shape[0] // 2
        upper = (tp_index // step) % 2
        kept = lax.dynamic_slice_in_dim(current, upper * half, half, 0)
        sent = lax.dynamic_slice_in_dim(current, (1 - upper) * half, half, 0)
        pairs = [(device, device ^ step) for device in range(tp_count)]
        received = lax.ppermute(sent.astype(jnp.bfloat16), "tp", pairs)
        current = kept.astype(jnp.float32) + received.astype(jnp.float32)
    current = current.astype(jnp.bfloat16)
    for step in reversed(bits):
        upper = (tp_index // step) % 2
        pairs = [(device, device ^ step) for device in range(tp_count)]
        received = lax.ppermute(current, "tp", pairs)
        current = jnp.where(
            upper == 0,
            jnp.concatenate([current, received], axis=0),
            jnp.concatenate([received, current], axis=0),
        )
    return current.astype(jnp.float32)


def swap_halves(local, axis_name):
    return lax.ppermute(local, axis_name, [(0, 1), (1, 0)])


def ctx_gather(local):
    other = swap_halves(local, "ctx")
    first = lax.axis_index("ctx") == 0
    return jnp.where(
        first, jnp.concatenate([local, other], axis=0), jnp.concatenate([other, local], axis=0)
    )


def ctx_scatter(full):
    rows = full.shape[0] // 2
    place = lax.axis_index("ctx")
    kept = lax.dynamic_slice_in_dim(full, place * rows, rows, 0)
    sent = lax.dynamic_slice_in_dim(full, (1 - place) * rows, rows, 0)
    received = swap_halves(sent.astype(jnp.bfloat16), "ctx")
    return kept.astype(jnp.bfloat16).astype(jnp.float32) + received.astype(jnp.float32)


def all_sum(value):
    total = value
    for axis_name in ("tp", "ctx", "fsdp"):
        count = lax.axis_size(axis_name)
        step = 1
        while step < count:
            pairs = [(device, device ^ step) for device in range(count)]
            total = total + lax.ppermute(total, axis_name, pairs)
            step *= 2
    return total


def shard_scatter(full):
    fsdp_count = lax.axis_size("fsdp")
    ctx_count = lax.axis_size("ctx")
    fsdp_bits = []
    step = 1
    while step < fsdp_count:
        fsdp_bits.append(step)
        step *= 2
    rows = full.shape[0] // (fsdp_count * ctx_count)
    current = full.astype(jnp.bfloat16).reshape((2,) * len(fsdp_bits) + (ctx_count, rows, -1))
    order = [("fsdp", 1), ("fsdp", 2), ("ctx", 1)] + [("fsdp", bit) for bit in fsdp_bits[2:]]
    for axis_name, bit in order:
        if axis_name == "fsdp":
            dim = len(fsdp_bits) - 1 - fsdp_bits.index(bit)
        else:
            dim = len(fsdp_bits)
        upper = (lax.axis_index(axis_name) // bit) % 2
        kept = lax.dynamic_slice_in_dim(current, upper, 1, dim)
        sent = lax.dynamic_slice_in_dim(current, 1 - upper, 1, dim)
        count = fsdp_count if axis_name == "fsdp" else ctx_count
        pairs = [(device, device ^ bit) for device in range(count)]
        received = lax.ppermute(sent.astype(jnp.bfloat16), axis_name, pairs)
        current = kept.astype(jnp.float32) + received.astype(jnp.float32)
    return current.reshape(rows, -1)


def per_device(
    tokens,
    cotangent,
    segments,
    attention_norm_weight,
    query_gain,
    key_gain,
    feedforward_gain,
    query_weight,
    key_projection_matrix,
    value_projection_matrix,
    output_weight,
    gate_weight,
    up_weight,
    down_weight,
):
    row_count = tokens.shape[0]
    model_width = tokens.shape[1]
    head_size = query_gain.shape[1]
    local_heads = query_weight.shape[2] // head_size
    local_groups = key_projection_matrix.shape[2] // head_size
    per_group = local_heads // local_groups
    layer_count = query_weight.shape[0]
    seq_length = segments.shape[1]
    row_start = lax.axis_index("ctx") * row_count
    column_width = model_width // lax.axis_size("tp")
    column_start = lax.axis_index("tp") * column_width
    score_scale = head_size ** (-0.5)
    positions = row_start + jnp.arange(row_count, dtype=jnp.int32)
    segment_row = segments[0]
    query_ids = lax.dynamic_slice_in_dim(segment_row, row_start, row_count)
    key_positions = jnp.arange(seq_length, dtype=jnp.int32)
    allowed = (query_ids[:, None] == segment_row[None, :]) & (
        key_positions[None, :] <= positions[:, None]
    )
    cosine_table, sine_table = rotary_tables(positions, head_size)

    def column_share(grad_rows, normalized):
        gradient_portion = lax.dynamic_slice_in_dim(grad_rows, column_start, column_width, 1)
        unit_slice = lax.dynamic_slice_in_dim(normalized, column_start, column_width, 1)
        part_sum = jnp.sum(gradient_portion * unit_slice, axis=0)
        return lax.dynamic_update_slice_in_dim(
            jnp.zeros((model_width,), jnp.float32), part_sum, column_start, 0
        )

    def attention_scores(query_groups, key_groups):
        return (
            jnp.einsum(
                "qgrd,kgd->grqk", query_groups, key_groups, preferred_element_type=jnp.float32
            )
            * score_scale
        )

    weight_shards = (
        query_weight,
        key_projection_matrix,
        value_projection_matrix,
        output_weight,
        gate_weight,
        up_weight,
        down_weight,
    )
    widths = [member.shape[2] for member in weight_shards]
    edges = [0]
    for width in widths:
        edges.append(edges[-1] + width)

    def gather_layer(layer_index):
        joined = jnp.concatenate([member[layer_index] for member in weight_shards], axis=1)
        full = lax.all_gather(joined, ("fsdp", "ctx"), axis=0, tiled=True)
        return tuple(full[:, edges[k] : edges[k + 1]] for k in range(len(widths)))

    def scatter_terms(terms):
        joined = jnp.concatenate([term.astype(jnp.bfloat16) for term in terms], axis=1)
        owned = lax.psum_scatter(joined, ("fsdp", "ctx"), scatter_dimension=0, tiled=True)
        pieces = []
        start = 0
        for term in terms:
            pieces.append(owned[:, start : start + term.shape[1]].astype(jnp.float32))
            start += term.shape[1]
        return pieces

    def scatter_layer(terms, layer_index):
        if layer_index > 0:
            return tuple(scatter_terms(terms))
        early = scatter_terms(terms[3:])
        joined = shard_scatter(
            jnp.concatenate([term.astype(jnp.bfloat16) for term in terms[:3]], axis=1)
        )
        late = []
        start = 0
        for term in terms[:3]:
            late.append(joined[:, start : start + term.shape[1]])
            start += term.shape[1]
        return tuple(late + early)

    kept_weights = []
    stored_layers = []
    hidden = tokens
    for layer_index in range(layer_count):
        gathered = gather_layer(layer_index)
        kept_weights.append(gathered)
        (
            forward_query_full,
            forward_key_full,
            forward_value_full,
            forward_output_full,
            forward_gate_full,
            forward_up_full,
            forward_down_full,
        ) = gathered
        forward_scale_one = row_scale(hidden)
        forward_normed = (hidden * forward_scale_one * attention_norm_weight[layer_index]).astype(
            jnp.bfloat16
        )
        query_raw = jnp.dot(
            forward_normed, forward_query_full, preferred_element_type=jnp.float32
        ).reshape(row_count, local_heads, head_size)
        key_raw = jnp.dot(
            forward_normed, forward_key_full, preferred_element_type=jnp.float32
        ).reshape(row_count, local_groups, head_size)
        values = jnp.dot(
            forward_normed, forward_value_full, preferred_element_type=jnp.float32
        ).astype(jnp.bfloat16)
        forward_query_scale = row_scale(query_raw)
        forward_query_unit = query_raw * forward_query_scale
        forward_key_scale = row_scale(key_raw)
        forward_key_unit = key_raw * forward_key_scale
        queries = rotate(
            forward_query_unit * query_gain[layer_index], cosine_table, sine_table
        ).astype(jnp.bfloat16)
        keys = rotate(forward_key_unit * key_gain[layer_index], cosine_table, sine_table).astype(
            jnp.bfloat16
        )
        keys = keys.reshape(row_count, local_groups * head_size)
        all_keys = ctx_gather(keys)
        all_values = ctx_gather(values)
        forward_query_groups = queries.reshape(row_count, local_groups, per_group, head_size)
        forward_key_groups = all_keys.reshape(seq_length, local_groups, head_size)
        forward_value_groups = all_values.reshape(seq_length, local_groups, head_size)
        forward_scores = attention_scores(forward_query_groups, forward_key_groups)
        exponent = jnp.where(allowed, jnp.exp(forward_scores), 0.0)
        forward_log_total = jnp.log(jnp.sum(exponent, axis=-1, keepdims=True))
        attention_probs = jnp.where(
            allowed, jnp.exp(forward_scores - forward_log_total), 0.0
        ).astype(jnp.bfloat16)
        forward_attended = jnp.einsum(
            "grqk,kgd->qgrd",
            attention_probs,
            forward_value_groups,
            preferred_element_type=jnp.float32,
        )
        forward_attended = forward_attended.astype(jnp.bfloat16).reshape(
            row_count, local_heads * head_size
        )
        forward_middle = hidden + tp_sum(contract_last(forward_attended, forward_output_full))
        forward_scale_two = row_scale(forward_middle)
        forward_feed_normed = (
            forward_middle * forward_scale_two * feedforward_gain[layer_index]
        ).astype(jnp.bfloat16)
        forward_gate_linear = jnp.dot(
            forward_feed_normed, forward_gate_full, preferred_element_type=jnp.float32
        )
        forward_up_linear = jnp.dot(
            forward_feed_normed, forward_up_full, preferred_element_type=jnp.float32
        )
        forward_activated = (jax.nn.silu(forward_gate_linear) * forward_up_linear).astype(
            jnp.bfloat16
        )
        result = forward_middle + tp_sum(contract_last(forward_activated, forward_down_full))
        forward_stored = (
            hidden,
            forward_scale_one,
            forward_normed,
            forward_query_unit,
            forward_query_scale,
            forward_key_unit,
            forward_key_scale,
            forward_query_groups,
            forward_key_groups,
            forward_value_groups,
            forward_log_total,
            forward_attended,
            forward_middle,
            forward_scale_two,
            forward_feed_normed,
            forward_gate_linear,
            forward_up_linear,
            forward_activated,
        )
        hidden = result
        stored_layers.append(forward_stored)
    grad_flow = cotangent
    weight_sums = [None] * layer_count
    gain_parts = [None] * layer_count
    for layer_index in reversed(range(layer_count)):
        gathered = kept_weights[layer_index]
        backward_stored = stored_layers[layer_index]
        query_full, key_full, value_full, output_full, gate_full, up_full, down_full = gathered
        (
            source,
            scale_one,
            normed,
            query_unit,
            query_scale,
            key_unit,
            key_scale,
            backward_query_groups,
            backward_key_groups,
            value_groups,
            log_total,
            attended,
            middle,
            scale_two,
            feed_normed,
            gate_linear,
            up_linear,
            activated,
        ) = backward_stored
        grad_half = grad_flow.astype(jnp.bfloat16)
        down_grad = contract_first(grad_half, activated)
        act_grad = jnp.dot(grad_half, down_full, preferred_element_type=jnp.float32)
        sigmoid_gate = jax.nn.sigmoid(gate_linear)
        gate_grad = (
            act_grad * up_linear * sigmoid_gate * (1.0 + gate_linear * (1.0 - sigmoid_gate))
        ).astype(jnp.bfloat16)
        up_grad = (act_grad * jax.nn.silu(gate_linear)).astype(jnp.bfloat16)
        gate_weight_grad = contract_first(feed_normed, gate_grad)
        up_weight_grad = contract_first(feed_normed, up_grad)
        feed_part = contract_last(gate_grad, gate_full) + contract_last(up_grad, up_full)
        feed_grad = tp_sum(feed_part)
        feed_unit = middle * scale_two
        feed_gain_grad = column_share(feed_grad, feed_unit)
        middle_grad = grad_flow + norm_back(
            feed_grad, feed_unit, scale_two, feedforward_gain[layer_index]
        )
        middle_half = middle_grad.astype(jnp.bfloat16)
        output_weight_grad = contract_first(middle_half, attended)
        attended_grad = jnp.dot(
            middle_half, output_full, preferred_element_type=jnp.float32
        ).astype(jnp.bfloat16)
        attended_grad = attended_grad.reshape(row_count, local_groups, per_group, head_size)
        scores = attention_scores(backward_query_groups, backward_key_groups)
        exact = jnp.where(allowed, jnp.exp(scores - log_total), 0.0)
        half_probs = exact.astype(jnp.bfloat16)
        value_grad = jnp.einsum(
            "grqk,qgrd->kgd", half_probs, attended_grad, preferred_element_type=jnp.float32
        )
        prob_grad = jnp.einsum(
            "qgrd,kgd->grqk", attended_grad, value_groups, preferred_element_type=jnp.float32
        )
        row_delta = jnp.sum(exact * prob_grad, axis=-1, keepdims=True)
        score_grad = (exact * (prob_grad - row_delta) * score_scale).astype(jnp.bfloat16)
        query_grad = jnp.einsum(
            "grqk,kgd->qgrd", score_grad, backward_key_groups, preferred_element_type=jnp.float32
        )
        query_grad = query_grad.reshape(row_count, local_heads, head_size)
        key_grad = jnp.einsum(
            "grqk,qgrd->kgd", score_grad, backward_query_groups, preferred_element_type=jnp.float32
        )
        key_own = ctx_scatter(key_grad.reshape(seq_length, local_groups * head_size))
        value_own = ctx_scatter(value_grad.reshape(seq_length, local_groups * head_size)).astype(
            jnp.bfloat16
        )
        query_turned = rotate(query_grad, cosine_table, -sine_table)
        key_turned = rotate(
            key_own.reshape(row_count, local_groups, head_size), cosine_table, -sine_table
        )
        query_gain_grad = jnp.sum(query_turned * query_unit, axis=(0, 1))
        key_gain_grad = jnp.sum(key_turned * key_unit, axis=(0, 1))
        query_pre = norm_back(
            query_turned, query_unit, query_scale, query_gain[layer_index]
        ).astype(jnp.bfloat16)
        query_pre = query_pre.reshape(row_count, local_heads * head_size)
        key_pre = norm_back(key_turned, key_unit, key_scale, key_gain[layer_index]).astype(
            jnp.bfloat16
        )
        key_pre = key_pre.reshape(row_count, local_groups * head_size)
        query_weight_grad = contract_first(normed, query_pre)
        key_weight_grad = contract_first(normed, key_pre)
        value_weight_grad = contract_first(normed, value_own)
        attention_part = (
            contract_last(query_pre, query_full)
            + contract_last(key_pre, key_full)
            + contract_last(value_own, value_full)
        )
        normed_grad = tp_sum(attention_part)
        source_unit = source * scale_one
        attention_gain_grad = column_share(normed_grad, source_unit)
        source_grad = middle_grad + norm_back(
            normed_grad, source_unit, scale_one, attention_norm_weight[layer_index]
        )
        weight_terms = (
            query_weight_grad,
            key_weight_grad,
            value_weight_grad,
            output_weight_grad,
            gate_weight_grad,
            up_weight_grad,
            down_grad,
        )
        gain_terms = (attention_gain_grad, query_gain_grad, key_gain_grad, feed_gain_grad)
        grad_flow, weight_terms, gain_terms = (source_grad, weight_terms, gain_terms)
        grad_query, grad_key, grad_value, grad_output, grad_gate, grad_up, grad_down = weight_terms
        weight_sums[layer_index] = scatter_layer(weight_terms, layer_index)
        gain_parts[layer_index] = gain_terms
    gain_stacks = [
        jnp.stack([member[which] for member in gain_parts]) for which in range(4)
    ]
    gain_edges = [0]
    for member in gain_stacks:
        gain_edges.append(gain_edges[-1] + member.shape[1])
    gain_joined = all_sum(jnp.concatenate(gain_stacks, axis=1))
    gain_totals = [
        gain_joined[:, gain_edges[which] : gain_edges[which + 1]] for which in range(4)
    ]
    stacked = [jnp.stack([member[which] for member in weight_sums]) for which in range(7)]
    return (
        hidden,
        grad_flow,
        gain_totals[0],
        gain_totals[1],
        gain_totals[2],
        gain_totals[3],
        stacked[0],
        stacked[1],
        stacked[2],
        stacked[3],
        stacked[4],
        stacked[5],
        stacked[6],
    )


def solution(mesh):
    in_specs = (
        P(("fsdp", "ctx"), None),
        P(("fsdp", "ctx"), None),
        P("fsdp", None),
        P(),
        P(),
        P(),
        P(),
        P(None, ("fsdp", "ctx"), "tp"),
        P(None, ("fsdp", "ctx"), "tp"),
        P(None, ("fsdp", "ctx"), "tp"),
        P(None, ("fsdp", "ctx"), "tp"),
        P(None, ("fsdp", "ctx"), "tp"),
        P(None, ("fsdp", "ctx"), "tp"),
        P(None, ("fsdp", "ctx"), "tp"),
    )
    out_specs = (
        P(("fsdp", "ctx"), None),
        P(("fsdp", "ctx"), None),
        P(),
        P(),
        P(),
        P(),
        P(None, ("fsdp", "ctx"), "tp"),
        P(None, ("fsdp", "ctx"), "tp"),
        P(None, ("fsdp", "ctx"), "tp"),
        P(None, ("fsdp", "ctx"), "tp"),
        P(None, ("fsdp", "ctx"), "tp"),
        P(None, ("fsdp", "ctx"), "tp"),
        P(None, ("fsdp", "ctx"), "tp"),
    )
    return jax.shard_map(
        per_device, mesh=mesh, in_specs=in_specs, out_specs=out_specs, check_vma=False
    )
```

```python
import jax
import jax.numpy as jnp
from jax import lax
from jax.sharding import PartitionSpec as P

eps = 1e-06
rope_base = 1000000.0


def contract_last(left_side, right_side):
    return lax.dot_general(
        left_side, right_side, (((1,), (1,)), ((), ())), preferred_element_type=jnp.float32
    )


def contract_first(left_side, right_side):
    return lax.dot_general(
        left_side, right_side, (((0,), (0,)), ((), ())), preferred_element_type=jnp.float32
    )


def row_scale(source):
    return lax.rsqrt(jnp.mean(source * source, axis=-1, keepdims=True) + eps)


def norm_back(grad_out, normalized, scaling, norm_gain):
    weighted = grad_out * norm_gain
    return scaling * (
        weighted - normalized * jnp.mean(weighted * normalized, axis=-1, keepdims=True)
    )


def rotary_tables(positions, head_size):
    halfway = head_size // 2
    frequency = rope_base ** (-2.0 * jnp.arange(halfway, dtype=jnp.float32) / head_size)
    angles = positions.astype(jnp.float32)[:, None] * frequency[None, :]
    return (jnp.cos(angles)[:, None, :], jnp.sin(angles)[:, None, :])


def rotate(source, cosine_table, sine_table):
    halfway = source.shape[-1] // 2
    leading = source[..., :halfway]
    trailing = source[..., halfway:]
    return jnp.concatenate(
        [
            leading * cosine_table - trailing * sine_table,
            trailing * cosine_table + leading * sine_table,
        ],
        axis=-1,
    )


def tp_sum(term):
    tp_count = lax.axis_size("tp")
    tp_index = lax.axis_index("tp")
    current = term.astype(jnp.bfloat16)
    half = current.shape[0] // 2
    upper = tp_index % 2
    core_pairs = [(device, device ^ 1) for device in range(tp_count)]
    kept = lax.dynamic_slice_in_dim(current, upper * half, half, 0)
    sent = lax.dynamic_slice_in_dim(current, (1 - upper) * half, half, 0)
    received = lax.ppermute(sent, "tp", core_pairs)
    total = kept.astype(jnp.float32) + received.astype(jnp.float32)
    step = 2
    while step < tp_count:
        mine = total.astype(jnp.bfloat16)
        pairs = [(device, device ^ step) for device in range(tp_count)]
        received = lax.ppermute(mine, "tp", pairs)
        total = mine.astype(jnp.float32) + received.astype(jnp.float32)
        step *= 2
    mine = total.astype(jnp.bfloat16)
    other = lax.ppermute(mine, "tp", core_pairs)
    joined = jnp.where(
        upper == 0,
        jnp.concatenate([mine, other], axis=0),
        jnp.concatenate([other, mine], axis=0),
    )
    return joined.astype(jnp.float32)


def swap_halves(local, axis_name):
    return lax.ppermute(local, axis_name, [(0, 1), (1, 0)])


def ctx_gather(local):
    other = swap_halves(local, "ctx")
    first = lax.axis_index("ctx") == 0
    return jnp.where(
        first, jnp.concatenate([local, other], axis=0), jnp.concatenate([other, local], axis=0)
    )


def ctx_scatter(full):
    rows = full.shape[0] // 2
    place = lax.axis_index("ctx")
    kept = lax.dynamic_slice_in_dim(full, place * rows, rows, 0)
    sent = lax.dynamic_slice_in_dim(full, (1 - place) * rows, rows, 0)
    received = swap_halves(sent.astype(jnp.bfloat16), "ctx")
    return kept.astype(jnp.bfloat16).astype(jnp.float32) + received.astype(jnp.float32)


def all_sum(value):
    total = value
    for axis_name in ("tp", "ctx", "fsdp"):
        count = lax.axis_size(axis_name)
        step = 1
        while step < count:
            pairs = [(device, device ^ step) for device in range(count)]
            total = total + lax.ppermute(total, axis_name, pairs)
            step *= 2
    return total


def shard_scatter(full):
    fsdp_count = lax.axis_size("fsdp")
    ctx_count = lax.axis_size("ctx")
    fsdp_bits = []
    step = 1
    while step < fsdp_count:
        fsdp_bits.append(step)
        step *= 2
    rows = full.shape[0] // (fsdp_count * ctx_count)
    current = full.astype(jnp.bfloat16).reshape((2,) * len(fsdp_bits) + (ctx_count, rows, -1))
    order = [("fsdp", 1), ("fsdp", 2), ("ctx", 1)] + [("fsdp", bit) for bit in fsdp_bits[2:]]
    for axis_name, bit in order:
        if axis_name == "fsdp":
            dim = len(fsdp_bits) - 1 - fsdp_bits.index(bit)
        else:
            dim = len(fsdp_bits)
        upper = (lax.axis_index(axis_name) // bit) % 2
        kept = lax.dynamic_slice_in_dim(current, upper, 1, dim)
        sent = lax.dynamic_slice_in_dim(current, 1 - upper, 1, dim)
        count = fsdp_count if axis_name == "fsdp" else ctx_count
        pairs = [(device, device ^ bit) for device in range(count)]
        received = lax.ppermute(sent.astype(jnp.bfloat16), axis_name, pairs)
        current = kept.astype(jnp.float32) + received.astype(jnp.float32)
    return current.reshape(rows, -1)


def per_device(
    tokens,
    cotangent,
    segments,
    attention_norm_weight,
    query_gain,
    key_gain,
    feedforward_gain,
    query_weight,
    key_projection_matrix,
    value_projection_matrix,
    output_weight,
    gate_weight,
    up_weight,
    down_weight,
):
    row_count = tokens.shape[0]
    model_width = tokens.shape[1]
    head_size = query_gain.shape[1]
    local_heads = query_weight.shape[2] // head_size
    local_groups = key_projection_matrix.shape[2] // head_size
    per_group = local_heads // local_groups
    layer_count = query_weight.shape[0]
    seq_length = segments.shape[1]
    row_start = lax.axis_index("ctx") * row_count
    column_width = model_width // lax.axis_size("tp")
    column_start = lax.axis_index("tp") * column_width
    score_scale = head_size ** (-0.5)
    positions = row_start + jnp.arange(row_count, dtype=jnp.int32)
    segment_row = segments[0]
    query_ids = lax.dynamic_slice_in_dim(segment_row, row_start, row_count)
    key_positions = jnp.arange(seq_length, dtype=jnp.int32)
    allowed = (query_ids[:, None] == segment_row[None, :]) & (
        key_positions[None, :] <= positions[:, None]
    )
    cosine_table, sine_table = rotary_tables(positions, head_size)

    def column_share(grad_rows, normalized):
        gradient_portion = lax.dynamic_slice_in_dim(grad_rows, column_start, column_width, 1)
        unit_slice = lax.dynamic_slice_in_dim(normalized, column_start, column_width, 1)
        part_sum = jnp.sum(gradient_portion * unit_slice, axis=0)
        return lax.dynamic_update_slice_in_dim(
            jnp.zeros((model_width,), jnp.float32), part_sum, column_start, 0
        )

    def attention_scores(query_groups, key_groups):
        return (
            jnp.einsum(
                "qgrd,kgd->grqk", query_groups, key_groups, preferred_element_type=jnp.float32
            )
            * score_scale
        )

    weight_shards = (
        query_weight,
        key_projection_matrix,
        value_projection_matrix,
        output_weight,
        gate_weight,
        up_weight,
        down_weight,
    )
    widths = [member.shape[2] for member in weight_shards]
    edges = [0]
    for width in widths:
        edges.append(edges[-1] + width)

    def gather_layer(layer_index):
        joined = jnp.concatenate([member[layer_index] for member in weight_shards], axis=1)
        full = lax.all_gather(joined, ("fsdp", "ctx"), axis=0, tiled=True)
        return tuple(full[:, edges[k] : edges[k + 1]] for k in range(len(widths)))

    def scatter_terms(terms):
        joined = jnp.concatenate([term.astype(jnp.bfloat16) for term in terms], axis=1)
        owned = lax.psum_scatter(joined, ("fsdp", "ctx"), scatter_dimension=0, tiled=True)
        pieces = []
        start = 0
        for term in terms:
            pieces.append(owned[:, start : start + term.shape[1]].astype(jnp.float32))
            start += term.shape[1]
        return pieces

    def scatter_layer(terms, layer_index):
        if layer_index > 0:
            return tuple(scatter_terms(terms))
        early = scatter_terms(terms[3:])
        joined = shard_scatter(
            jnp.concatenate([term.astype(jnp.bfloat16) for term in terms[:3]], axis=1)
        )
        late = []
        start = 0
        for term in terms[:3]:
            late.append(joined[:, start : start + term.shape[1]])
            start += term.shape[1]
        return tuple(late + early)

    kept_weights = []
    stored_layers = []
    hidden = tokens
    for layer_index in range(layer_count):
        gathered = gather_layer(layer_index)
        kept_weights.append(gathered)
        (
            forward_query_full,
            forward_key_full,
            forward_value_full,
            forward_output_full,
            forward_gate_full,
            forward_up_full,
            forward_down_full,
        ) = gathered
        forward_scale_one = row_scale(hidden)
        forward_normed = (hidden * forward_scale_one * attention_norm_weight[layer_index]).astype(
            jnp.bfloat16
        )
        query_raw = jnp.dot(
            forward_normed, forward_query_full, preferred_element_type=jnp.float32
        ).reshape(row_count, local_heads, head_size)
        key_raw = jnp.dot(
            forward_normed, forward_key_full, preferred_element_type=jnp.float32
        ).reshape(row_count, local_groups, head_size)
        values = jnp.dot(
            forward_normed, forward_value_full, preferred_element_type=jnp.float32
        ).astype(jnp.bfloat16)
        forward_query_scale = row_scale(query_raw)
        forward_query_unit = query_raw * forward_query_scale
        forward_key_scale = row_scale(key_raw)
        forward_key_unit = key_raw * forward_key_scale
        queries = rotate(
            forward_query_unit * query_gain[layer_index], cosine_table, sine_table
        ).astype(jnp.bfloat16)
        keys = rotate(forward_key_unit * key_gain[layer_index], cosine_table, sine_table).astype(
            jnp.bfloat16
        )
        keys = keys.reshape(row_count, local_groups * head_size)
        all_keys = ctx_gather(keys)
        all_values = ctx_gather(values)
        forward_query_groups = queries.reshape(row_count, local_groups, per_group, head_size)
        forward_key_groups = all_keys.reshape(seq_length, local_groups, head_size)
        forward_value_groups = all_values.reshape(seq_length, local_groups, head_size)
        forward_scores = attention_scores(forward_query_groups, forward_key_groups)
        exponent = jnp.where(allowed, jnp.exp(forward_scores), 0.0)
        forward_log_total = jnp.log(jnp.sum(exponent, axis=-1, keepdims=True))
        attention_probs = jnp.where(
            allowed, jnp.exp(forward_scores - forward_log_total), 0.0
        ).astype(jnp.bfloat16)
        forward_attended = jnp.einsum(
            "grqk,kgd->qgrd",
            attention_probs,
            forward_value_groups,
            preferred_element_type=jnp.float32,
        )
        forward_attended = forward_attended.astype(jnp.bfloat16).reshape(
            row_count, local_heads * head_size
        )
        forward_middle = hidden + tp_sum(contract_last(forward_attended, forward_output_full))
        forward_scale_two = row_scale(forward_middle)
        forward_feed_normed = (
            forward_middle * forward_scale_two * feedforward_gain[layer_index]
        ).astype(jnp.bfloat16)
        forward_gate_linear = jnp.dot(
            forward_feed_normed, forward_gate_full, preferred_element_type=jnp.float32
        )
        forward_up_linear = jnp.dot(
            forward_feed_normed, forward_up_full, preferred_element_type=jnp.float32
        )
        forward_activated = (jax.nn.silu(forward_gate_linear) * forward_up_linear).astype(
            jnp.bfloat16
        )
        result = forward_middle + tp_sum(contract_last(forward_activated, forward_down_full))
        forward_stored = (
            hidden,
            forward_scale_one,
            forward_normed,
            forward_query_unit,
            forward_query_scale,
            forward_key_unit,
            forward_key_scale,
            forward_query_groups,
            forward_key_groups,
            forward_value_groups,
            forward_log_total,
            forward_attended,
            forward_middle,
            forward_scale_two,
            forward_feed_normed,
            forward_gate_linear,
            forward_up_linear,
            forward_activated,
        )
        hidden = result
        stored_layers.append(forward_stored)
    grad_flow = cotangent
    weight_sums = [None] * layer_count
    gain_parts = [None] * layer_count
    for layer_index in reversed(range(layer_count)):
        gathered = kept_weights[layer_index]
        backward_stored = stored_layers[layer_index]
        query_full, key_full, value_full, output_full, gate_full, up_full, down_full = gathered
        (
            source,
            scale_one,
            normed,
            query_unit,
            query_scale,
            key_unit,
            key_scale,
            backward_query_groups,
            backward_key_groups,
            value_groups,
            log_total,
            attended,
            middle,
            scale_two,
            feed_normed,
            gate_linear,
            up_linear,
            activated,
        ) = backward_stored
        grad_half = grad_flow.astype(jnp.bfloat16)
        down_grad = contract_first(grad_half, activated)
        act_grad = jnp.dot(grad_half, down_full, preferred_element_type=jnp.float32)
        sigmoid_gate = jax.nn.sigmoid(gate_linear)
        gate_grad = (
            act_grad * up_linear * sigmoid_gate * (1.0 + gate_linear * (1.0 - sigmoid_gate))
        ).astype(jnp.bfloat16)
        up_grad = (act_grad * jax.nn.silu(gate_linear)).astype(jnp.bfloat16)
        gate_weight_grad = contract_first(feed_normed, gate_grad)
        up_weight_grad = contract_first(feed_normed, up_grad)
        feed_part = contract_last(gate_grad, gate_full) + contract_last(up_grad, up_full)
        feed_grad = tp_sum(feed_part)
        feed_unit = middle * scale_two
        feed_gain_grad = column_share(feed_grad, feed_unit)
        middle_grad = grad_flow + norm_back(
            feed_grad, feed_unit, scale_two, feedforward_gain[layer_index]
        )
        middle_half = middle_grad.astype(jnp.bfloat16)
        output_weight_grad = contract_first(middle_half, attended)
        attended_grad = jnp.dot(
            middle_half, output_full, preferred_element_type=jnp.float32
        ).astype(jnp.bfloat16)
        attended_grad = attended_grad.reshape(row_count, local_groups, per_group, head_size)
        scores = attention_scores(backward_query_groups, backward_key_groups)
        exact = jnp.where(allowed, jnp.exp(scores - log_total), 0.0)
        half_probs = exact.astype(jnp.bfloat16)
        value_grad = jnp.einsum(
            "grqk,qgrd->kgd", half_probs, attended_grad, preferred_element_type=jnp.float32
        )
        prob_grad = jnp.einsum(
            "qgrd,kgd->grqk", attended_grad, value_groups, preferred_element_type=jnp.float32
        )
        row_delta = jnp.sum(exact * prob_grad, axis=-1, keepdims=True)
        score_grad = (exact * (prob_grad - row_delta) * score_scale).astype(jnp.bfloat16)
        query_grad = jnp.einsum(
            "grqk,kgd->qgrd", score_grad, backward_key_groups, preferred_element_type=jnp.float32
        )
        query_grad = query_grad.reshape(row_count, local_heads, head_size)
        key_grad = jnp.einsum(
            "grqk,qgrd->kgd", score_grad, backward_query_groups, preferred_element_type=jnp.float32
        )
        key_own = ctx_scatter(key_grad.reshape(seq_length, local_groups * head_size))
        value_own = ctx_scatter(value_grad.reshape(seq_length, local_groups * head_size)).astype(
            jnp.bfloat16
        )
        query_turned = rotate(query_grad, cosine_table, -sine_table)
        key_turned = rotate(
            key_own.reshape(row_count, local_groups, head_size), cosine_table, -sine_table
        )
        query_gain_grad = jnp.sum(query_turned * query_unit, axis=(0, 1))
        key_gain_grad = jnp.sum(key_turned * key_unit, axis=(0, 1))
        query_pre = norm_back(
            query_turned, query_unit, query_scale, query_gain[layer_index]
        ).astype(jnp.bfloat16)
        query_pre = query_pre.reshape(row_count, local_heads * head_size)
        key_pre = norm_back(key_turned, key_unit, key_scale, key_gain[layer_index]).astype(
            jnp.bfloat16
        )
        key_pre = key_pre.reshape(row_count, local_groups * head_size)
        query_weight_grad = contract_first(normed, query_pre)
        key_weight_grad = contract_first(normed, key_pre)
        value_weight_grad = contract_first(normed, value_own)
        attention_part = (
            contract_last(query_pre, query_full)
            + contract_last(key_pre, key_full)
            + contract_last(value_own, value_full)
        )
        normed_grad = tp_sum(attention_part)
        source_unit = source * scale_one
        attention_gain_grad = column_share(normed_grad, source_unit)
        source_grad = middle_grad + norm_back(
            normed_grad, source_unit, scale_one, attention_norm_weight[layer_index]
        )
        weight_terms = (
            query_weight_grad,
            key_weight_grad,
            value_weight_grad,
            output_weight_grad,
            gate_weight_grad,
            up_weight_grad,
            down_grad,
        )
        gain_terms = (attention_gain_grad, query_gain_grad, key_gain_grad, feed_gain_grad)
        grad_flow, weight_terms, gain_terms = (source_grad, weight_terms, gain_terms)
        grad_query, grad_key, grad_value, grad_output, grad_gate, grad_up, grad_down = weight_terms
        weight_sums[layer_index] = scatter_layer(weight_terms, layer_index)
        gain_parts[layer_index] = gain_terms
    gain_stacks = [
        jnp.stack([member[which] for member in gain_parts]) for which in range(4)
    ]
    gain_edges = [0]
    for member in gain_stacks:
        gain_edges.append(gain_edges[-1] + member.shape[1])
    gain_joined = all_sum(jnp.concatenate(gain_stacks, axis=1))
    gain_totals = [
        gain_joined[:, gain_edges[which] : gain_edges[which + 1]] for which in range(4)
    ]
    stacked = [jnp.stack([member[which] for member in weight_sums]) for which in range(7)]
    return (
        hidden,
        grad_flow,
        gain_totals[0],
        gain_totals[1],
        gain_totals[2],
        gain_totals[3],
        stacked[0],
        stacked[1],
        stacked[2],
        stacked[3],
        stacked[4],
        stacked[5],
        stacked[6],
    )


def solution(mesh):
    in_specs = (
        P(("fsdp", "ctx"), None),
        P(("fsdp", "ctx"), None),
        P("fsdp", None),
        P(),
        P(),
        P(),
        P(),
        P(None, ("fsdp", "ctx"), "tp"),
        P(None, ("fsdp", "ctx"), "tp"),
        P(None, ("fsdp", "ctx"), "tp"),
        P(None, ("fsdp", "ctx"), "tp"),
        P(None, ("fsdp", "ctx"), "tp"),
        P(None, ("fsdp", "ctx"), "tp"),
        P(None, ("fsdp", "ctx"), "tp"),
    )
    out_specs = (
        P(("fsdp", "ctx"), None),
        P(("fsdp", "ctx"), None),
        P(),
        P(),
        P(),
        P(),
        P(None, ("fsdp", "ctx"), "tp"),
        P(None, ("fsdp", "ctx"), "tp"),
        P(None, ("fsdp", "ctx"), "tp"),
        P(None, ("fsdp", "ctx"), "tp"),
        P(None, ("fsdp", "ctx"), "tp"),
        P(None, ("fsdp", "ctx"), "tp"),
        P(None, ("fsdp", "ctx"), "tp"),
    )
    return jax.shard_map(
        per_device, mesh=mesh, in_specs=in_specs, out_specs=out_specs, check_vma=False
    )
```

```python
import jax
import jax.numpy as jnp
from jax import lax
from jax.sharding import PartitionSpec as P

eps = 1e-06
rope_base = 1000000.0


def contract_last(left_side, right_side):
    return lax.dot_general(
        left_side, right_side, (((1,), (1,)), ((), ())), preferred_element_type=jnp.float32
    )


def contract_first(left_side, right_side):
    return lax.dot_general(
        left_side, right_side, (((0,), (0,)), ((), ())), preferred_element_type=jnp.float32
    )


def row_scale(source):
    return lax.rsqrt(jnp.mean(source * source, axis=-1, keepdims=True) + eps)


def norm_back(grad_out, normalized, scaling, norm_gain):
    weighted = grad_out * norm_gain
    return scaling * (
        weighted - normalized * jnp.mean(weighted * normalized, axis=-1, keepdims=True)
    )


def rotary_tables(positions, head_size):
    halfway = head_size // 2
    frequency = rope_base ** (-2.0 * jnp.arange(halfway, dtype=jnp.float32) / head_size)
    angles = positions.astype(jnp.float32)[:, None] * frequency[None, :]
    return (jnp.cos(angles)[:, None, :], jnp.sin(angles)[:, None, :])


def rotate(source, cosine_table, sine_table):
    halfway = source.shape[-1] // 2
    leading = source[..., :halfway]
    trailing = source[..., halfway:]
    return jnp.concatenate(
        [
            leading * cosine_table - trailing * sine_table,
            trailing * cosine_table + leading * sine_table,
        ],
        axis=-1,
    )


def tp_sum(term):
    tp_count = lax.axis_size("tp")
    tp_index = lax.axis_index("tp")
    current = term.astype(jnp.bfloat16)
    half = current.shape[0] // 2
    upper = tp_index % 2
    core_pairs = [(device, device ^ 1) for device in range(tp_count)]
    kept = lax.dynamic_slice_in_dim(current, upper * half, half, 0)
    sent = lax.dynamic_slice_in_dim(current, (1 - upper) * half, half, 0)
    received = lax.ppermute(sent, "tp", core_pairs)
    total = kept.astype(jnp.float32) + received.astype(jnp.float32)
    step = 2
    while step < tp_count:
        mine = total.astype(jnp.bfloat16)
        pairs = [(device, device ^ step) for device in range(tp_count)]
        received = lax.ppermute(mine, "tp", pairs)
        total = mine.astype(jnp.float32) + received.astype(jnp.float32)
        step *= 2
    mine = total.astype(jnp.bfloat16)
    other = lax.ppermute(mine, "tp", core_pairs)
    joined = jnp.where(
        upper == 0,
        jnp.concatenate([mine, other], axis=0),
        jnp.concatenate([other, mine], axis=0),
    )
    return joined.astype(jnp.float32)


def swap_halves(local, axis_name):
    return lax.ppermute(local, axis_name, [(0, 1), (1, 0)])


def ctx_gather(local):
    other = swap_halves(local, "ctx")
    first = lax.axis_index("ctx") == 0
    return jnp.where(
        first, jnp.concatenate([local, other], axis=0), jnp.concatenate([other, local], axis=0)
    )


def ctx_scatter(full):
    rows = full.shape[0] // 2
    place = lax.axis_index("ctx")
    kept = lax.dynamic_slice_in_dim(full, place * rows, rows, 0)
    sent = lax.dynamic_slice_in_dim(full, (1 - place) * rows, rows, 0)
    received = swap_halves(sent.astype(jnp.bfloat16), "ctx")
    return kept.astype(jnp.bfloat16).astype(jnp.float32) + received.astype(jnp.float32)


def all_sum(value):
    total = value
    for axis_name in ("tp", "ctx", "fsdp"):
        count = lax.axis_size(axis_name)
        step = 1
        while step < count:
            pairs = [(device, device ^ step) for device in range(count)]
            total = total + lax.ppermute(total, axis_name, pairs)
            step *= 2
    return total


def shard_scatter(full):
    fsdp_count = lax.axis_size("fsdp")
    ctx_count = lax.axis_size("ctx")
    fsdp_bits = []
    step = 1
    while step < fsdp_count:
        fsdp_bits.append(step)
        step *= 2
    rows = full.shape[0] // (fsdp_count * ctx_count)
    current = full.astype(jnp.bfloat16).reshape((2,) * len(fsdp_bits) + (ctx_count, rows, -1))
    order = [("fsdp", 1), ("fsdp", 2), ("ctx", 1)] + [("fsdp", bit) for bit in fsdp_bits[2:]]
    for axis_name, bit in order:
        if axis_name == "fsdp":
            dim = len(fsdp_bits) - 1 - fsdp_bits.index(bit)
        else:
            dim = len(fsdp_bits)
        upper = (lax.axis_index(axis_name) // bit) % 2
        kept = lax.dynamic_slice_in_dim(current, upper, 1, dim)
        sent = lax.dynamic_slice_in_dim(current, 1 - upper, 1, dim)
        count = fsdp_count if axis_name == "fsdp" else ctx_count
        pairs = [(device, device ^ bit) for device in range(count)]
        received = lax.ppermute(sent.astype(jnp.bfloat16), axis_name, pairs)
        current = kept.astype(jnp.float32) + received.astype(jnp.float32)
    return current.reshape(rows, -1)


def shard_gather(local):
    fsdp_count = lax.axis_size("fsdp")
    ctx_count = lax.axis_size("ctx")
    fsdp_bits = []
    step = 1
    while step < fsdp_count:
        fsdp_bits.append(step)
        step *= 2
    current = local.reshape((1,) * (len(fsdp_bits) + 1) + local.shape)
    order = [("ctx", 1)] + [("fsdp", bit) for bit in fsdp_bits[2:]] + [("fsdp", 1), ("fsdp", 2)]
    for axis_name, bit in order:
        if axis_name == "fsdp":
            dim = len(fsdp_bits) - 1 - fsdp_bits.index(bit)
        else:
            dim = len(fsdp_bits)
        count = fsdp_count if axis_name == "fsdp" else ctx_count
        pairs = [(device, device ^ bit) for device in range(count)]
        received = lax.ppermute(current, axis_name, pairs)
        upper = (lax.axis_index(axis_name) // bit) % 2
        current = jnp.where(
            upper == 0,
            jnp.concatenate([current, received], axis=dim),
            jnp.concatenate([received, current], axis=dim),
        )
    return current.reshape(-1, local.shape[1])


def per_device(
    tokens,
    cotangent,
    segments,
    attention_norm_weight,
    query_gain,
    key_gain,
    feedforward_gain,
    query_weight,
    key_projection_matrix,
    value_projection_matrix,
    output_weight,
    gate_weight,
    up_weight,
    down_weight,
):
    row_count = tokens.shape[0]
    model_width = tokens.shape[1]
    head_size = query_gain.shape[1]
    local_heads = query_weight.shape[2] // head_size
    local_groups = key_projection_matrix.shape[2] // head_size
    per_group = local_heads // local_groups
    layer_count = query_weight.shape[0]
    seq_length = segments.shape[1]
    row_start = lax.axis_index("ctx") * row_count
    column_width = model_width // lax.axis_size("tp")
    column_start = lax.axis_index("tp") * column_width
    score_scale = head_size ** (-0.5)
    positions = row_start + jnp.arange(row_count, dtype=jnp.int32)
    segment_row = segments[0]
    query_ids = lax.dynamic_slice_in_dim(segment_row, row_start, row_count)
    key_positions = jnp.arange(seq_length, dtype=jnp.int32)
    allowed = (query_ids[:, None] == segment_row[None, :]) & (
        key_positions[None, :] <= positions[:, None]
    )
    cosine_table, sine_table = rotary_tables(positions, head_size)

    def column_share(grad_rows, normalized):
        gradient_portion = lax.dynamic_slice_in_dim(grad_rows, column_start, column_width, 1)
        unit_slice = lax.dynamic_slice_in_dim(normalized, column_start, column_width, 1)
        part_sum = jnp.sum(gradient_portion * unit_slice, axis=0)
        return lax.dynamic_update_slice_in_dim(
            jnp.zeros((model_width,), jnp.float32), part_sum, column_start, 0
        )

    def attention_scores(query_groups, key_groups):
        return (
            jnp.einsum(
                "qgrd,kgd->grqk", query_groups, key_groups, preferred_element_type=jnp.float32
            )
            * score_scale
        )

    weight_shards = (
        query_weight,
        key_projection_matrix,
        value_projection_matrix,
        output_weight,
        gate_weight,
        up_weight,
        down_weight,
    )
    widths = [member.shape[2] for member in weight_shards]
    edges = [0]
    for width in widths:
        edges.append(edges[-1] + width)

    def gather_layer(layer_index):
        early = jnp.concatenate([member[layer_index] for member in weight_shards[:3]], axis=1)
        early_full = shard_gather(early)
        late = jnp.concatenate([member[layer_index] for member in weight_shards[3:]], axis=1)
        late_full = lax.all_gather(late, ("fsdp", "ctx"), axis=0, tiled=True)
        pieces = []
        for k in range(len(widths)):
            if k < 3:
                pieces.append(early_full[:, edges[k] : edges[k + 1]])
            else:
                pieces.append(late_full[:, edges[k] - edges[3] : edges[k + 1] - edges[3]])
        return tuple(pieces)

    def scatter_terms(terms):
        joined = jnp.concatenate([term.astype(jnp.bfloat16) for term in terms], axis=1)
        owned = lax.psum_scatter(joined, ("fsdp", "ctx"), scatter_dimension=0, tiled=True)
        pieces = []
        start = 0
        for term in terms:
            pieces.append(owned[:, start : start + term.shape[1]].astype(jnp.float32))
            start += term.shape[1]
        return pieces

    def scatter_layer(terms, layer_index):
        if layer_index > 0:
            return tuple(scatter_terms(terms))
        early = scatter_terms(terms[3:])
        joined = shard_scatter(
            jnp.concatenate([term.astype(jnp.bfloat16) for term in terms[:3]], axis=1)
        )
        late = []
        start = 0
        for term in terms[:3]:
            late.append(joined[:, start : start + term.shape[1]])
            start += term.shape[1]
        return tuple(late + early)

    kept_weights = []
    stored_layers = []
    hidden = tokens
    for layer_index in range(layer_count):
        gathered = gather_layer(layer_index)
        kept_weights.append(gathered)
        (
            forward_query_full,
            forward_key_full,
            forward_value_full,
            forward_output_full,
            forward_gate_full,
            forward_up_full,
            forward_down_full,
        ) = gathered
        forward_scale_one = row_scale(hidden)
        forward_normed = (hidden * forward_scale_one * attention_norm_weight[layer_index]).astype(
            jnp.bfloat16
        )
        query_raw = jnp.dot(
            forward_normed, forward_query_full, preferred_element_type=jnp.float32
        ).reshape(row_count, local_heads, head_size)
        key_raw = jnp.dot(
            forward_normed, forward_key_full, preferred_element_type=jnp.float32
        ).reshape(row_count, local_groups, head_size)
        values = jnp.dot(
            forward_normed, forward_value_full, preferred_element_type=jnp.float32
        ).astype(jnp.bfloat16)
        forward_query_scale = row_scale(query_raw)
        forward_query_unit = query_raw * forward_query_scale
        forward_key_scale = row_scale(key_raw)
        forward_key_unit = key_raw * forward_key_scale
        queries = rotate(
            forward_query_unit * query_gain[layer_index], cosine_table, sine_table
        ).astype(jnp.bfloat16)
        keys = rotate(forward_key_unit * key_gain[layer_index], cosine_table, sine_table).astype(
            jnp.bfloat16
        )
        keys = keys.reshape(row_count, local_groups * head_size)
        all_keys = ctx_gather(keys)
        all_values = ctx_gather(values)
        forward_query_groups = queries.reshape(row_count, local_groups, per_group, head_size)
        forward_key_groups = all_keys.reshape(seq_length, local_groups, head_size)
        forward_value_groups = all_values.reshape(seq_length, local_groups, head_size)
        forward_scores = attention_scores(forward_query_groups, forward_key_groups)
        exponent = jnp.where(allowed, jnp.exp(forward_scores), 0.0)
        forward_log_total = jnp.log(jnp.sum(exponent, axis=-1, keepdims=True))
        attention_probs = jnp.where(
            allowed, jnp.exp(forward_scores - forward_log_total), 0.0
        ).astype(jnp.bfloat16)
        forward_attended = jnp.einsum(
            "grqk,kgd->qgrd",
            attention_probs,
            forward_value_groups,
            preferred_element_type=jnp.float32,
        )
        forward_attended = forward_attended.astype(jnp.bfloat16).reshape(
            row_count, local_heads * head_size
        )
        forward_middle = hidden + tp_sum(contract_last(forward_attended, forward_output_full))
        forward_scale_two = row_scale(forward_middle)
        forward_feed_normed = (
            forward_middle * forward_scale_two * feedforward_gain[layer_index]
        ).astype(jnp.bfloat16)
        forward_gate_linear = jnp.dot(
            forward_feed_normed, forward_gate_full, preferred_element_type=jnp.float32
        )
        forward_up_linear = jnp.dot(
            forward_feed_normed, forward_up_full, preferred_element_type=jnp.float32
        )
        forward_activated = (jax.nn.silu(forward_gate_linear) * forward_up_linear).astype(
            jnp.bfloat16
        )
        result = forward_middle + tp_sum(contract_last(forward_activated, forward_down_full))
        forward_stored = (
            hidden,
            forward_scale_one,
            forward_normed,
            forward_query_unit,
            forward_query_scale,
            forward_key_unit,
            forward_key_scale,
            forward_query_groups,
            forward_key_groups,
            forward_value_groups,
            forward_log_total,
            forward_attended,
            forward_middle,
            forward_scale_two,
            forward_feed_normed,
            forward_gate_linear,
            forward_up_linear,
            forward_activated,
        )
        hidden = result
        stored_layers.append(forward_stored)
    grad_flow = cotangent
    weight_sums = [None] * layer_count
    gain_parts = [None] * layer_count
    for layer_index in reversed(range(layer_count)):
        gathered = kept_weights[layer_index]
        backward_stored = stored_layers[layer_index]
        query_full, key_full, value_full, output_full, gate_full, up_full, down_full = gathered
        (
            source,
            scale_one,
            normed,
            query_unit,
            query_scale,
            key_unit,
            key_scale,
            backward_query_groups,
            backward_key_groups,
            value_groups,
            log_total,
            attended,
            middle,
            scale_two,
            feed_normed,
            gate_linear,
            up_linear,
            activated,
        ) = backward_stored
        grad_half = grad_flow.astype(jnp.bfloat16)
        down_grad = contract_first(grad_half, activated)
        act_grad = jnp.dot(grad_half, down_full, preferred_element_type=jnp.float32)
        sigmoid_gate = jax.nn.sigmoid(gate_linear)
        gate_grad = (
            act_grad * up_linear * sigmoid_gate * (1.0 + gate_linear * (1.0 - sigmoid_gate))
        ).astype(jnp.bfloat16)
        up_grad = (act_grad * jax.nn.silu(gate_linear)).astype(jnp.bfloat16)
        gate_weight_grad = contract_first(feed_normed, gate_grad)
        up_weight_grad = contract_first(feed_normed, up_grad)
        feed_part = contract_last(gate_grad, gate_full) + contract_last(up_grad, up_full)
        feed_grad = tp_sum(feed_part)
        feed_unit = middle * scale_two
        feed_gain_grad = column_share(feed_grad, feed_unit)
        middle_grad = grad_flow + norm_back(
            feed_grad, feed_unit, scale_two, feedforward_gain[layer_index]
        )
        middle_half = middle_grad.astype(jnp.bfloat16)
        output_weight_grad = contract_first(middle_half, attended)
        attended_grad = jnp.dot(
            middle_half, output_full, preferred_element_type=jnp.float32
        ).astype(jnp.bfloat16)
        attended_grad = attended_grad.reshape(row_count, local_groups, per_group, head_size)
        scores = attention_scores(backward_query_groups, backward_key_groups)
        exact = jnp.where(allowed, jnp.exp(scores - log_total), 0.0)
        half_probs = exact.astype(jnp.bfloat16)
        value_grad = jnp.einsum(
            "grqk,qgrd->kgd", half_probs, attended_grad, preferred_element_type=jnp.float32
        )
        prob_grad = jnp.einsum(
            "qgrd,kgd->grqk", attended_grad, value_groups, preferred_element_type=jnp.float32
        )
        row_delta = jnp.sum(exact * prob_grad, axis=-1, keepdims=True)
        score_grad = (exact * (prob_grad - row_delta) * score_scale).astype(jnp.bfloat16)
        query_grad = jnp.einsum(
            "grqk,kgd->qgrd", score_grad, backward_key_groups, preferred_element_type=jnp.float32
        )
        query_grad = query_grad.reshape(row_count, local_heads, head_size)
        key_grad = jnp.einsum(
            "grqk,qgrd->kgd", score_grad, backward_query_groups, preferred_element_type=jnp.float32
        )
        key_own = ctx_scatter(key_grad.reshape(seq_length, local_groups * head_size))
        value_own = ctx_scatter(value_grad.reshape(seq_length, local_groups * head_size)).astype(
            jnp.bfloat16
        )
        query_turned = rotate(query_grad, cosine_table, -sine_table)
        key_turned = rotate(
            key_own.reshape(row_count, local_groups, head_size), cosine_table, -sine_table
        )
        query_gain_grad = jnp.sum(query_turned * query_unit, axis=(0, 1))
        key_gain_grad = jnp.sum(key_turned * key_unit, axis=(0, 1))
        query_pre = norm_back(
            query_turned, query_unit, query_scale, query_gain[layer_index]
        ).astype(jnp.bfloat16)
        query_pre = query_pre.reshape(row_count, local_heads * head_size)
        key_pre = norm_back(key_turned, key_unit, key_scale, key_gain[layer_index]).astype(
            jnp.bfloat16
        )
        key_pre = key_pre.reshape(row_count, local_groups * head_size)
        query_weight_grad = contract_first(normed, query_pre)
        key_weight_grad = contract_first(normed, key_pre)
        value_weight_grad = contract_first(normed, value_own)
        attention_part = (
            contract_last(query_pre, query_full)
            + contract_last(key_pre, key_full)
            + contract_last(value_own, value_full)
        )
        normed_grad = tp_sum(attention_part)
        source_unit = source * scale_one
        attention_gain_grad = column_share(normed_grad, source_unit)
        source_grad = middle_grad + norm_back(
            normed_grad, source_unit, scale_one, attention_norm_weight[layer_index]
        )
        weight_terms = (
            query_weight_grad,
            key_weight_grad,
            value_weight_grad,
            output_weight_grad,
            gate_weight_grad,
            up_weight_grad,
            down_grad,
        )
        gain_terms = (attention_gain_grad, query_gain_grad, key_gain_grad, feed_gain_grad)
        grad_flow, weight_terms, gain_terms = (source_grad, weight_terms, gain_terms)
        grad_query, grad_key, grad_value, grad_output, grad_gate, grad_up, grad_down = weight_terms
        weight_sums[layer_index] = scatter_layer(weight_terms, layer_index)
        gain_parts[layer_index] = gain_terms
    gain_stacks = [
        jnp.stack([member[which] for member in gain_parts]) for which in range(4)
    ]
    gain_edges = [0]
    for member in gain_stacks:
        gain_edges.append(gain_edges[-1] + member.shape[1])
    gain_joined = all_sum(jnp.concatenate(gain_stacks, axis=1))
    gain_totals = [
        gain_joined[:, gain_edges[which] : gain_edges[which + 1]] for which in range(4)
    ]
    stacked = [jnp.stack([member[which] for member in weight_sums]) for which in range(7)]
    return (
        hidden,
        grad_flow,
        gain_totals[0],
        gain_totals[1],
        gain_totals[2],
        gain_totals[3],
        stacked[0],
        stacked[1],
        stacked[2],
        stacked[3],
        stacked[4],
        stacked[5],
        stacked[6],
    )


def solution(mesh):
    in_specs = (
        P(("fsdp", "ctx"), None),
        P(("fsdp", "ctx"), None),
        P("fsdp", None),
        P(),
        P(),
        P(),
        P(),
        P(None, ("fsdp", "ctx"), "tp"),
        P(None, ("fsdp", "ctx"), "tp"),
        P(None, ("fsdp", "ctx"), "tp"),
        P(None, ("fsdp", "ctx"), "tp"),
        P(None, ("fsdp", "ctx"), "tp"),
        P(None, ("fsdp", "ctx"), "tp"),
        P(None, ("fsdp", "ctx"), "tp"),
    )
    out_specs = (
        P(("fsdp", "ctx"), None),
        P(("fsdp", "ctx"), None),
        P(),
        P(),
        P(),
        P(),
        P(None, ("fsdp", "ctx"), "tp"),
        P(None, ("fsdp", "ctx"), "tp"),
        P(None, ("fsdp", "ctx"), "tp"),
        P(None, ("fsdp", "ctx"), "tp"),
        P(None, ("fsdp", "ctx"), "tp"),
        P(None, ("fsdp", "ctx"), "tp"),
        P(None, ("fsdp", "ctx"), "tp"),
    )
    return jax.shard_map(
        per_device, mesh=mesh, in_specs=in_specs, out_specs=out_specs, check_vma=False
    )
```

```python
import jax
import jax.numpy as jnp
from jax import lax
from jax.sharding import PartitionSpec as P

eps = 1e-06
rope_base = 1000000.0


def contract_last(left_side, right_side):
    return lax.dot_general(
        left_side, right_side, (((1,), (1,)), ((), ())), preferred_element_type=jnp.float32
    )


def contract_first(left_side, right_side):
    return lax.dot_general(
        left_side, right_side, (((0,), (0,)), ((), ())), preferred_element_type=jnp.float32
    )


def row_scale(source):
    return lax.rsqrt(jnp.mean(source * source, axis=-1, keepdims=True) + eps)


def norm_back(grad_out, normalized, scaling, norm_gain):
    weighted = grad_out * norm_gain
    return scaling * (
        weighted - normalized * jnp.mean(weighted * normalized, axis=-1, keepdims=True)
    )


def rotary_tables(positions, head_size):
    halfway = head_size // 2
    frequency = rope_base ** (-2.0 * jnp.arange(halfway, dtype=jnp.float32) / head_size)
    angles = positions.astype(jnp.float32)[:, None] * frequency[None, :]
    return (jnp.cos(angles)[:, None, :], jnp.sin(angles)[:, None, :])


def rotate(source, cosine_table, sine_table):
    halfway = source.shape[-1] // 2
    leading = source[..., :halfway]
    trailing = source[..., halfway:]
    return jnp.concatenate(
        [
            leading * cosine_table - trailing * sine_table,
            trailing * cosine_table + leading * sine_table,
        ],
        axis=-1,
    )


def tp_sum(term):
    tp_count = lax.axis_size("tp")
    tp_index = lax.axis_index("tp")
    current = term.astype(jnp.bfloat16)
    half = current.shape[0] // 2
    upper = tp_index % 2
    core_pairs = [(device, device ^ 1) for device in range(tp_count)]
    kept = lax.dynamic_slice_in_dim(current, upper * half, half, 0)
    sent = lax.dynamic_slice_in_dim(current, (1 - upper) * half, half, 0)
    received = lax.ppermute(sent, "tp", core_pairs)
    total = kept.astype(jnp.float32) + received.astype(jnp.float32)
    step = 2
    while step < tp_count:
        mine = total.astype(jnp.bfloat16)
        pairs = [(device, device ^ step) for device in range(tp_count)]
        received = lax.ppermute(mine, "tp", pairs)
        total = mine.astype(jnp.float32) + received.astype(jnp.float32)
        step *= 2
    mine = total.astype(jnp.bfloat16)
    other = lax.ppermute(mine, "tp", core_pairs)
    joined = jnp.where(
        upper == 0,
        jnp.concatenate([mine, other], axis=0),
        jnp.concatenate([other, mine], axis=0),
    )
    return joined.astype(jnp.float32)


def swap_halves(local, axis_name):
    return lax.ppermute(local, axis_name, [(0, 1), (1, 0)])


def ctx_gather(local):
    other = swap_halves(local, "ctx")
    first = lax.axis_index("ctx") == 0
    return jnp.where(
        first, jnp.concatenate([local, other], axis=0), jnp.concatenate([other, local], axis=0)
    )


def ctx_scatter(full):
    rows = full.shape[0] // 2
    place = lax.axis_index("ctx")
    kept = lax.dynamic_slice_in_dim(full, place * rows, rows, 0)
    sent = lax.dynamic_slice_in_dim(full, (1 - place) * rows, rows, 0)
    received = swap_halves(sent.astype(jnp.bfloat16), "ctx")
    return kept.astype(jnp.bfloat16).astype(jnp.float32) + received.astype(jnp.float32)


def all_sum(value):
    total = value
    for axis_name in ("tp", "ctx", "fsdp"):
        count = lax.axis_size(axis_name)
        step = 1
        while step < count:
            pairs = [(device, device ^ step) for device in range(count)]
            total = total + lax.ppermute(total, axis_name, pairs)
            step *= 2
    return total


def shard_scatter(full):
    fsdp_count = lax.axis_size("fsdp")
    ctx_count = lax.axis_size("ctx")
    fsdp_bits = []
    step = 1
    while step < fsdp_count:
        fsdp_bits.append(step)
        step *= 2
    rows = full.shape[0] // (fsdp_count * ctx_count)
    current = full.astype(jnp.bfloat16).reshape((2,) * len(fsdp_bits) + (ctx_count, rows, -1))
    order = [("fsdp", 1), ("fsdp", 2), ("ctx", 1)] + [("fsdp", bit) for bit in fsdp_bits[2:]]
    for axis_name, bit in order:
        if axis_name == "fsdp":
            dim = len(fsdp_bits) - 1 - fsdp_bits.index(bit)
        else:
            dim = len(fsdp_bits)
        upper = (lax.axis_index(axis_name) // bit) % 2
        kept = lax.dynamic_slice_in_dim(current, upper, 1, dim)
        sent = lax.dynamic_slice_in_dim(current, 1 - upper, 1, dim)
        count = fsdp_count if axis_name == "fsdp" else ctx_count
        pairs = [(device, device ^ bit) for device in range(count)]
        received = lax.ppermute(sent.astype(jnp.bfloat16), axis_name, pairs)
        current = kept.astype(jnp.float32) + received.astype(jnp.float32)
    return current.reshape(rows, -1)


def shard_gather(local):
    fsdp_count = lax.axis_size("fsdp")
    ctx_count = lax.axis_size("ctx")
    fsdp_bits = []
    step = 1
    while step < fsdp_count:
        fsdp_bits.append(step)
        step *= 2
    current = local.reshape((1,) * (len(fsdp_bits) + 1) + local.shape)
    order = [("ctx", 1)] + [("fsdp", bit) for bit in fsdp_bits[2:]] + [("fsdp", 1), ("fsdp", 2)]
    for axis_name, bit in order:
        if axis_name == "fsdp":
            dim = len(fsdp_bits) - 1 - fsdp_bits.index(bit)
        else:
            dim = len(fsdp_bits)
        count = fsdp_count if axis_name == "fsdp" else ctx_count
        pairs = [(device, device ^ bit) for device in range(count)]
        received = lax.ppermute(current, axis_name, pairs)
        upper = (lax.axis_index(axis_name) // bit) % 2
        current = jnp.where(
            upper == 0,
            jnp.concatenate([current, received], axis=dim),
            jnp.concatenate([received, current], axis=dim),
        )
    return current.reshape(-1, local.shape[1])


def per_device(
    tokens,
    cotangent,
    segments,
    attention_norm_weight,
    query_gain,
    key_gain,
    feedforward_gain,
    query_weight,
    key_projection_matrix,
    value_projection_matrix,
    output_weight,
    gate_weight,
    up_weight,
    down_weight,
):
    row_count = tokens.shape[0]
    model_width = tokens.shape[1]
    head_size = query_gain.shape[1]
    local_heads = query_weight.shape[2] // head_size
    local_groups = key_projection_matrix.shape[2] // head_size
    per_group = local_heads // local_groups
    layer_count = query_weight.shape[0]
    seq_length = segments.shape[1]
    row_start = lax.axis_index("ctx") * row_count
    column_width = model_width // lax.axis_size("tp")
    column_start = lax.axis_index("tp") * column_width
    score_scale = head_size ** (-0.5)
    positions = row_start + jnp.arange(row_count, dtype=jnp.int32)
    segment_row = segments[0]
    query_ids = lax.dynamic_slice_in_dim(segment_row, row_start, row_count)
    key_positions = jnp.arange(seq_length, dtype=jnp.int32)
    allowed = (query_ids[:, None] == segment_row[None, :]) & (
        key_positions[None, :] <= positions[:, None]
    )
    cosine_table, sine_table = rotary_tables(positions, head_size)

    def column_share(grad_rows, normalized):
        gradient_portion = lax.dynamic_slice_in_dim(grad_rows, column_start, column_width, 1)
        unit_slice = lax.dynamic_slice_in_dim(normalized, column_start, column_width, 1)
        part_sum = jnp.sum(gradient_portion * unit_slice, axis=0)
        return lax.dynamic_update_slice_in_dim(
            jnp.zeros((model_width,), jnp.float32), part_sum, column_start, 0
        )

    def attention_scores(query_groups, key_groups):
        return (
            jnp.einsum(
                "qgrd,kgd->grqk", query_groups, key_groups, preferred_element_type=jnp.float32
            )
            * score_scale
        )

    weight_shards = (
        query_weight,
        key_projection_matrix,
        value_projection_matrix,
        output_weight,
        gate_weight,
        up_weight,
        down_weight,
    )
    widths = [member.shape[2] for member in weight_shards]
    edges = [0]
    for width in widths:
        edges.append(edges[-1] + width)

    def gather_layer(layer_index):
        if layer_index > 0:
            joined = jnp.concatenate([member[layer_index] for member in weight_shards], axis=1)
            full = lax.all_gather(joined, ("fsdp", "ctx"), axis=0, tiled=True)
            return tuple(full[:, edges[k] : edges[k + 1]] for k in range(len(widths)))
        early = jnp.concatenate([member[layer_index] for member in weight_shards[:3]], axis=1)
        early_full = shard_gather(early)
        late = jnp.concatenate([member[layer_index] for member in weight_shards[3:]], axis=1)
        late_full = lax.all_gather(late, ("fsdp", "ctx"), axis=0, tiled=True)
        pieces = []
        for k in range(len(widths)):
            if k < 3:
                pieces.append(early_full[:, edges[k] : edges[k + 1]])
            else:
                pieces.append(late_full[:, edges[k] - edges[3] : edges[k + 1] - edges[3]])
        return tuple(pieces)

    def scatter_terms(terms):
        joined = jnp.concatenate([term.astype(jnp.bfloat16) for term in terms], axis=1)
        owned = lax.psum_scatter(joined, ("fsdp", "ctx"), scatter_dimension=0, tiled=True)
        pieces = []
        start = 0
        for term in terms:
            pieces.append(owned[:, start : start + term.shape[1]].astype(jnp.float32))
            start += term.shape[1]
        return pieces

    def scatter_layer(terms, layer_index):
        if layer_index > 0:
            return tuple(scatter_terms(terms))
        early = scatter_terms(terms[3:])
        joined = shard_scatter(
            jnp.concatenate([term.astype(jnp.bfloat16) for term in terms[:3]], axis=1)
        )
        late = []
        start = 0
        for term in terms[:3]:
            late.append(joined[:, start : start + term.shape[1]])
            start += term.shape[1]
        return tuple(late + early)

    kept_weights = []
    stored_layers = []
    hidden = tokens
    for layer_index in range(layer_count):
        gathered = gather_layer(layer_index)
        kept_weights.append(gathered)
        (
            forward_query_full,
            forward_key_full,
            forward_value_full,
            forward_output_full,
            forward_gate_full,
            forward_up_full,
            forward_down_full,
        ) = gathered
        forward_scale_one = row_scale(hidden)
        forward_normed = (hidden * forward_scale_one * attention_norm_weight[layer_index]).astype(
            jnp.bfloat16
        )
        query_raw = jnp.dot(
            forward_normed, forward_query_full, preferred_element_type=jnp.float32
        ).reshape(row_count, local_heads, head_size)
        key_raw = jnp.dot(
            forward_normed, forward_key_full, preferred_element_type=jnp.float32
        ).reshape(row_count, local_groups, head_size)
        values = jnp.dot(
            forward_normed, forward_value_full, preferred_element_type=jnp.float32
        ).astype(jnp.bfloat16)
        forward_query_scale = row_scale(query_raw)
        forward_query_unit = query_raw * forward_query_scale
        forward_key_scale = row_scale(key_raw)
        forward_key_unit = key_raw * forward_key_scale
        queries = rotate(
            forward_query_unit * query_gain[layer_index], cosine_table, sine_table
        ).astype(jnp.bfloat16)
        keys = rotate(forward_key_unit * key_gain[layer_index], cosine_table, sine_table).astype(
            jnp.bfloat16
        )
        keys = keys.reshape(row_count, local_groups * head_size)
        all_keys = ctx_gather(keys)
        all_values = ctx_gather(values)
        forward_query_groups = queries.reshape(row_count, local_groups, per_group, head_size)
        forward_key_groups = all_keys.reshape(seq_length, local_groups, head_size)
        forward_value_groups = all_values.reshape(seq_length, local_groups, head_size)
        forward_scores = attention_scores(forward_query_groups, forward_key_groups)
        exponent = jnp.where(allowed, jnp.exp(forward_scores), 0.0)
        forward_log_total = jnp.log(jnp.sum(exponent, axis=-1, keepdims=True))
        attention_probs = jnp.where(
            allowed, jnp.exp(forward_scores - forward_log_total), 0.0
        ).astype(jnp.bfloat16)
        forward_attended = jnp.einsum(
            "grqk,kgd->qgrd",
            attention_probs,
            forward_value_groups,
            preferred_element_type=jnp.float32,
        )
        forward_attended = forward_attended.astype(jnp.bfloat16).reshape(
            row_count, local_heads * head_size
        )
        forward_middle = hidden + tp_sum(contract_last(forward_attended, forward_output_full))
        forward_scale_two = row_scale(forward_middle)
        forward_feed_normed = (
            forward_middle * forward_scale_two * feedforward_gain[layer_index]
        ).astype(jnp.bfloat16)
        forward_gate_linear = jnp.dot(
            forward_feed_normed, forward_gate_full, preferred_element_type=jnp.float32
        )
        forward_up_linear = jnp.dot(
            forward_feed_normed, forward_up_full, preferred_element_type=jnp.float32
        )
        forward_activated = (jax.nn.silu(forward_gate_linear) * forward_up_linear).astype(
            jnp.bfloat16
        )
        result = forward_middle + tp_sum(contract_last(forward_activated, forward_down_full))
        forward_stored = (
            hidden,
            forward_scale_one,
            forward_normed,
            forward_query_unit,
            forward_query_scale,
            forward_key_unit,
            forward_key_scale,
            forward_query_groups,
            forward_key_groups,
            forward_value_groups,
            forward_log_total,
            forward_attended,
            forward_middle,
            forward_scale_two,
            forward_feed_normed,
            forward_gate_linear,
            forward_up_linear,
            forward_activated,
        )
        hidden = result
        stored_layers.append(forward_stored)
    grad_flow = cotangent
    weight_sums = [None] * layer_count
    gain_parts = [None] * layer_count
    for layer_index in reversed(range(layer_count)):
        gathered = kept_weights[layer_index]
        backward_stored = stored_layers[layer_index]
        query_full, key_full, value_full, output_full, gate_full, up_full, down_full = gathered
        (
            source,
            scale_one,
            normed,
            query_unit,
            query_scale,
            key_unit,
            key_scale,
            backward_query_groups,
            backward_key_groups,
            value_groups,
            log_total,
            attended,
            middle,
            scale_two,
            feed_normed,
            gate_linear,
            up_linear,
            activated,
        ) = backward_stored
        grad_half = grad_flow.astype(jnp.bfloat16)
        down_grad = contract_first(grad_half, activated)
        act_grad = jnp.dot(grad_half, down_full, preferred_element_type=jnp.float32)
        sigmoid_gate = jax.nn.sigmoid(gate_linear)
        gate_grad = (
            act_grad * up_linear * sigmoid_gate * (1.0 + gate_linear * (1.0 - sigmoid_gate))
        ).astype(jnp.bfloat16)
        up_grad = (act_grad * jax.nn.silu(gate_linear)).astype(jnp.bfloat16)
        gate_weight_grad = contract_first(feed_normed, gate_grad)
        up_weight_grad = contract_first(feed_normed, up_grad)
        feed_part = contract_last(gate_grad, gate_full) + contract_last(up_grad, up_full)
        feed_grad = tp_sum(feed_part)
        feed_unit = middle * scale_two
        feed_gain_grad = column_share(feed_grad, feed_unit)
        middle_grad = grad_flow + norm_back(
            feed_grad, feed_unit, scale_two, feedforward_gain[layer_index]
        )
        middle_half = middle_grad.astype(jnp.bfloat16)
        output_weight_grad = contract_first(middle_half, attended)
        attended_grad = jnp.dot(
            middle_half, output_full, preferred_element_type=jnp.float32
        ).astype(jnp.bfloat16)
        attended_grad = attended_grad.reshape(row_count, local_groups, per_group, head_size)
        scores = attention_scores(backward_query_groups, backward_key_groups)
        exact = jnp.where(allowed, jnp.exp(scores - log_total), 0.0)
        half_probs = exact.astype(jnp.bfloat16)
        value_grad = jnp.einsum(
            "grqk,qgrd->kgd", half_probs, attended_grad, preferred_element_type=jnp.float32
        )
        prob_grad = jnp.einsum(
            "qgrd,kgd->grqk", attended_grad, value_groups, preferred_element_type=jnp.float32
        )
        row_delta = jnp.sum(exact * prob_grad, axis=-1, keepdims=True)
        score_grad = (exact * (prob_grad - row_delta) * score_scale).astype(jnp.bfloat16)
        query_grad = jnp.einsum(
            "grqk,kgd->qgrd", score_grad, backward_key_groups, preferred_element_type=jnp.float32
        )
        query_grad = query_grad.reshape(row_count, local_heads, head_size)
        key_grad = jnp.einsum(
            "grqk,qgrd->kgd", score_grad, backward_query_groups, preferred_element_type=jnp.float32
        )
        key_own = ctx_scatter(key_grad.reshape(seq_length, local_groups * head_size))
        value_own = ctx_scatter(value_grad.reshape(seq_length, local_groups * head_size)).astype(
            jnp.bfloat16
        )
        query_turned = rotate(query_grad, cosine_table, -sine_table)
        key_turned = rotate(
            key_own.reshape(row_count, local_groups, head_size), cosine_table, -sine_table
        )
        query_gain_grad = jnp.sum(query_turned * query_unit, axis=(0, 1))
        key_gain_grad = jnp.sum(key_turned * key_unit, axis=(0, 1))
        query_pre = norm_back(
            query_turned, query_unit, query_scale, query_gain[layer_index]
        ).astype(jnp.bfloat16)
        query_pre = query_pre.reshape(row_count, local_heads * head_size)
        key_pre = norm_back(key_turned, key_unit, key_scale, key_gain[layer_index]).astype(
            jnp.bfloat16
        )
        key_pre = key_pre.reshape(row_count, local_groups * head_size)
        query_weight_grad = contract_first(normed, query_pre)
        key_weight_grad = contract_first(normed, key_pre)
        value_weight_grad = contract_first(normed, value_own)
        attention_part = (
            contract_last(query_pre, query_full)
            + contract_last(key_pre, key_full)
            + contract_last(value_own, value_full)
        )
        normed_grad = tp_sum(attention_part)
        source_unit = source * scale_one
        attention_gain_grad = column_share(normed_grad, source_unit)
        source_grad = middle_grad + norm_back(
            normed_grad, source_unit, scale_one, attention_norm_weight[layer_index]
        )
        weight_terms = (
            query_weight_grad,
            key_weight_grad,
            value_weight_grad,
            output_weight_grad,
            gate_weight_grad,
            up_weight_grad,
            down_grad,
        )
        gain_terms = (attention_gain_grad, query_gain_grad, key_gain_grad, feed_gain_grad)
        grad_flow, weight_terms, gain_terms = (source_grad, weight_terms, gain_terms)
        grad_query, grad_key, grad_value, grad_output, grad_gate, grad_up, grad_down = weight_terms
        weight_sums[layer_index] = scatter_layer(weight_terms, layer_index)
        gain_parts[layer_index] = gain_terms
    gain_stacks = [
        jnp.stack([member[which] for member in gain_parts]) for which in range(4)
    ]
    gain_edges = [0]
    for member in gain_stacks:
        gain_edges.append(gain_edges[-1] + member.shape[1])
    gain_joined = all_sum(jnp.concatenate(gain_stacks, axis=1))
    gain_totals = [
        gain_joined[:, gain_edges[which] : gain_edges[which + 1]] for which in range(4)
    ]
    stacked = [jnp.stack([member[which] for member in weight_sums]) for which in range(7)]
    return (
        hidden,
        grad_flow,
        gain_totals[0],
        gain_totals[1],
        gain_totals[2],
        gain_totals[3],
        stacked[0],
        stacked[1],
        stacked[2],
        stacked[3],
        stacked[4],
        stacked[5],
        stacked[6],
    )


def solution(mesh):
    in_specs = (
        P(("fsdp", "ctx"), None),
        P(("fsdp", "ctx"), None),
        P("fsdp", None),
        P(),
        P(),
        P(),
        P(),
        P(None, ("fsdp", "ctx"), "tp"),
        P(None, ("fsdp", "ctx"), "tp"),
        P(None, ("fsdp", "ctx"), "tp"),
        P(None, ("fsdp", "ctx"), "tp"),
        P(None, ("fsdp", "ctx"), "tp"),
        P(None, ("fsdp", "ctx"), "tp"),
        P(None, ("fsdp", "ctx"), "tp"),
    )
    out_specs = (
        P(("fsdp", "ctx"), None),
        P(("fsdp", "ctx"), None),
        P(),
        P(),
        P(),
        P(),
        P(None, ("fsdp", "ctx"), "tp"),
        P(None, ("fsdp", "ctx"), "tp"),
        P(None, ("fsdp", "ctx"), "tp"),
        P(None, ("fsdp", "ctx"), "tp"),
        P(None, ("fsdp", "ctx"), "tp"),
        P(None, ("fsdp", "ctx"), "tp"),
        P(None, ("fsdp", "ctx"), "tp"),
    )
    return jax.shard_map(
        per_device, mesh=mesh, in_specs=in_specs, out_specs=out_specs, check_vma=False
    )
```

```python
import jax
import jax.numpy as jnp
from jax import lax
from jax.experimental import pallas as pl
from jax.sharding import PartitionSpec as P
import functools

eps = 1e-06
rope_base = 1000000.0


def contract_last(left_side, right_side):
    return lax.dot_general(
        left_side, right_side, (((1,), (1,)), ((), ())), preferred_element_type=jnp.float32
    )


def contract_first(left_side, right_side):
    return lax.dot_general(
        left_side, right_side, (((0,), (0,)), ((), ())), preferred_element_type=jnp.float32
    )


def row_scale(source):
    return lax.rsqrt(jnp.mean(source * source, axis=-1, keepdims=True) + eps)


def norm_back(grad_out, normalized, scaling, norm_gain):
    weighted = grad_out * norm_gain
    return scaling * (
        weighted - normalized * jnp.mean(weighted * normalized, axis=-1, keepdims=True)
    )


def rotary_tables(positions, head_size):
    halfway = head_size // 2
    frequency = rope_base ** (-2.0 * jnp.arange(halfway, dtype=jnp.float32) / head_size)
    angles = positions.astype(jnp.float32)[:, None] * frequency[None, :]
    return (jnp.cos(angles)[:, None, :], jnp.sin(angles)[:, None, :])


def rotate(source, cosine_table, sine_table):
    halfway = source.shape[-1] // 2
    leading = source[..., :halfway]
    trailing = source[..., halfway:]
    return jnp.concatenate(
        [
            leading * cosine_table - trailing * sine_table,
            trailing * cosine_table + leading * sine_table,
        ],
        axis=-1,
    )


def attention_kernel(
    query_ref, key_ref, value_ref, query_ids_ref, key_ids_ref, position_ref,
    attended_ref, log_total_ref, *, groups, per_group, head_size, score_scale
):
    query_ids = query_ids_ref[...]
    key_ids = key_ids_ref[...]
    key_positions = lax.broadcasted_iota(jnp.int32, key_ids.shape, 1)
    allowed = (query_ids == key_ids) & (key_positions <= position_ref[...])
    for group in range(groups):
        key_block = key_ref[:, group * head_size : (group + 1) * head_size]
        value_block = value_ref[:, group * head_size : (group + 1) * head_size]
        for member in range(per_group):
            head = group * per_group + member
            query_block = query_ref[:, head * head_size : (head + 1) * head_size]
            scores = (
                lax.dot_general(
                    query_block, key_block, (((1,), (1,)), ((), ())),
                    preferred_element_type=jnp.float32,
                )
                * score_scale
            )
            exponent = jnp.where(allowed, jnp.exp(scores), 0.0)
            log_total = jnp.log(jnp.sum(exponent, axis=1, keepdims=True))
            probs = jnp.where(allowed, jnp.exp(scores - log_total), 0.0).astype(jnp.bfloat16)
            attended = jnp.dot(probs, value_block, preferred_element_type=jnp.float32)
            attended_ref[:, head * head_size : (head + 1) * head_size] = attended.astype(
                jnp.bfloat16
            )
            log_total_ref[head] = log_total


def fused_attention(queries, keys, values, query_ids, key_ids, positions, per_group, head_size):
    rows = queries.shape[0]
    heads = queries.shape[1] // head_size
    groups = heads // per_group
    keys_count = keys.shape[0]
    kernel = functools.partial(
        attention_kernel, groups=groups, per_group=per_group, head_size=head_size,
        score_scale=head_size ** (-0.5),
    )
    return pl.pallas_call(
        kernel,
        out_shape=(
            jax.ShapeDtypeStruct((rows, heads * head_size), jnp.bfloat16),
            jax.ShapeDtypeStruct((heads, rows, 1), jnp.float32),
        ),
        cost_estimate=pl.CostEstimate(
            flops=4 * heads * rows * keys_count * head_size,
            transcendentals=2 * heads * rows * keys_count,
            bytes_accessed=2 * (2 * rows * heads * head_size + 2 * keys_count * groups * head_size),
        ),
    )(
        queries, keys, values, query_ids.reshape(rows, 1), key_ids.reshape(1, keys_count),
        positions.reshape(rows, 1),
    )


def tp_sum(term):
    tp_count = lax.axis_size("tp")
    tp_index = lax.axis_index("tp")
    current = term.astype(jnp.bfloat16)
    half = current.shape[0] // 2
    upper = tp_index % 2
    core_pairs = [(device, device ^ 1) for device in range(tp_count)]
    kept = lax.dynamic_slice_in_dim(current, upper * half, half, 0)
    sent = lax.dynamic_slice_in_dim(current, (1 - upper) * half, half, 0)
    received = lax.ppermute(sent, "tp", core_pairs)
    total = kept.astype(jnp.float32) + received.astype(jnp.float32)
    step = 2
    while step < tp_count:
        mine = total.astype(jnp.bfloat16)
        pairs = [(device, device ^ step) for device in range(tp_count)]
        received = lax.ppermute(mine, "tp", pairs)
        total = mine.astype(jnp.float32) + received.astype(jnp.float32)
        step *= 2
    mine = total.astype(jnp.bfloat16)
    other = lax.ppermute(mine, "tp", core_pairs)
    joined = jnp.where(
        upper == 0,
        jnp.concatenate([mine, other], axis=0),
        jnp.concatenate([other, mine], axis=0),
    )
    return joined.astype(jnp.float32)


def swap_halves(local, axis_name):
    return lax.ppermute(local, axis_name, [(0, 1), (1, 0)])


def ctx_gather(local):
    other = swap_halves(local, "ctx")
    first = lax.axis_index("ctx") == 0
    return jnp.where(
        first, jnp.concatenate([local, other], axis=0), jnp.concatenate([other, local], axis=0)
    )


def ctx_scatter(full):
    rows = full.shape[0] // 2
    place = lax.axis_index("ctx")
    kept = lax.dynamic_slice_in_dim(full, place * rows, rows, 0)
    sent = lax.dynamic_slice_in_dim(full, (1 - place) * rows, rows, 0)
    received = swap_halves(sent.astype(jnp.bfloat16), "ctx")
    return kept.astype(jnp.bfloat16).astype(jnp.float32) + received.astype(jnp.float32)


def all_sum(value):
    total = value
    for axis_name in ("tp", "ctx", "fsdp"):
        count = lax.axis_size(axis_name)
        step = 1
        while step < count:
            pairs = [(device, device ^ step) for device in range(count)]
            total = total + lax.ppermute(total, axis_name, pairs)
            step *= 2
    return total


def shard_scatter(full):
    fsdp_count = lax.axis_size("fsdp")
    ctx_count = lax.axis_size("ctx")
    fsdp_bits = []
    step = 1
    while step < fsdp_count:
        fsdp_bits.append(step)
        step *= 2
    rows = full.shape[0] // (fsdp_count * ctx_count)
    current = full.astype(jnp.bfloat16).reshape((2,) * len(fsdp_bits) + (ctx_count, rows, -1))
    order = [("fsdp", 1), ("fsdp", 2), ("ctx", 1)] + [("fsdp", bit) for bit in fsdp_bits[2:]]
    for axis_name, bit in order:
        if axis_name == "fsdp":
            dim = len(fsdp_bits) - 1 - fsdp_bits.index(bit)
        else:
            dim = len(fsdp_bits)
        upper = (lax.axis_index(axis_name) // bit) % 2
        kept = lax.dynamic_slice_in_dim(current, upper, 1, dim)
        sent = lax.dynamic_slice_in_dim(current, 1 - upper, 1, dim)
        count = fsdp_count if axis_name == "fsdp" else ctx_count
        pairs = [(device, device ^ bit) for device in range(count)]
        received = lax.ppermute(sent.astype(jnp.bfloat16), axis_name, pairs)
        current = kept.astype(jnp.float32) + received.astype(jnp.float32)
    return current.reshape(rows, -1)


def shard_gather(local):
    fsdp_count = lax.axis_size("fsdp")
    ctx_count = lax.axis_size("ctx")
    fsdp_bits = []
    step = 1
    while step < fsdp_count:
        fsdp_bits.append(step)
        step *= 2
    current = local.reshape((1,) * (len(fsdp_bits) + 1) + local.shape)
    order = [("ctx", 1)] + [("fsdp", bit) for bit in fsdp_bits[2:]] + [("fsdp", 1), ("fsdp", 2)]
    for axis_name, bit in order:
        if axis_name == "fsdp":
            dim = len(fsdp_bits) - 1 - fsdp_bits.index(bit)
        else:
            dim = len(fsdp_bits)
        count = fsdp_count if axis_name == "fsdp" else ctx_count
        pairs = [(device, device ^ bit) for device in range(count)]
        received = lax.ppermute(current, axis_name, pairs)
        upper = (lax.axis_index(axis_name) // bit) % 2
        current = jnp.where(
            upper == 0,
            jnp.concatenate([current, received], axis=dim),
            jnp.concatenate([received, current], axis=dim),
        )
    return current.reshape(-1, local.shape[1])


def per_device(
    tokens,
    cotangent,
    segments,
    attention_norm_weight,
    query_gain,
    key_gain,
    feedforward_gain,
    query_weight,
    key_projection_matrix,
    value_projection_matrix,
    output_weight,
    gate_weight,
    up_weight,
    down_weight,
):
    row_count = tokens.shape[0]
    model_width = tokens.shape[1]
    head_size = query_gain.shape[1]
    local_heads = query_weight.shape[2] // head_size
    local_groups = key_projection_matrix.shape[2] // head_size
    per_group = local_heads // local_groups
    layer_count = query_weight.shape[0]
    seq_length = segments.shape[1]
    row_start = lax.axis_index("ctx") * row_count
    column_width = model_width // lax.axis_size("tp")
    column_start = lax.axis_index("tp") * column_width
    score_scale = head_size ** (-0.5)
    positions = row_start + jnp.arange(row_count, dtype=jnp.int32)
    segment_row = segments[0]
    query_ids = lax.dynamic_slice_in_dim(segment_row, row_start, row_count)
    key_positions = jnp.arange(seq_length, dtype=jnp.int32)
    allowed = (query_ids[:, None] == segment_row[None, :]) & (
        key_positions[None, :] <= positions[:, None]
    )
    cosine_table, sine_table = rotary_tables(positions, head_size)

    def column_share(grad_rows, normalized):
        gradient_portion = lax.dynamic_slice_in_dim(grad_rows, column_start, column_width, 1)
        unit_slice = lax.dynamic_slice_in_dim(normalized, column_start, column_width, 1)
        part_sum = jnp.sum(gradient_portion * unit_slice, axis=0)
        return lax.dynamic_update_slice_in_dim(
            jnp.zeros((model_width,), jnp.float32), part_sum, column_start, 0
        )

    def attention_scores(query_groups, key_groups):
        return (
            jnp.einsum(
                "qgrd,kgd->grqk", query_groups, key_groups, preferred_element_type=jnp.float32
            )
            * score_scale
        )

    weight_shards = (
        query_weight,
        key_projection_matrix,
        value_projection_matrix,
        output_weight,
        gate_weight,
        up_weight,
        down_weight,
    )
    widths = [member.shape[2] for member in weight_shards]
    edges = [0]
    for width in widths:
        edges.append(edges[-1] + width)

    def gather_layer(layer_index):
        if layer_index > 0:
            joined = jnp.concatenate([member[layer_index] for member in weight_shards], axis=1)
            full = lax.all_gather(joined, ("fsdp", "ctx"), axis=0, tiled=True)
            return tuple(full[:, edges[k] : edges[k + 1]] for k in range(len(widths)))
        early = jnp.concatenate([member[layer_index] for member in weight_shards[:3]], axis=1)
        early_full = shard_gather(early)
        late = jnp.concatenate([member[layer_index] for member in weight_shards[3:]], axis=1)
        late_full = lax.all_gather(late, ("fsdp", "ctx"), axis=0, tiled=True)
        pieces = []
        for k in range(len(widths)):
            if k < 3:
                pieces.append(early_full[:, edges[k] : edges[k + 1]])
            else:
                pieces.append(late_full[:, edges[k] - edges[3] : edges[k + 1] - edges[3]])
        return tuple(pieces)

    def scatter_terms(terms):
        joined = jnp.concatenate([term.astype(jnp.bfloat16) for term in terms], axis=1)
        owned = lax.psum_scatter(joined, ("fsdp", "ctx"), scatter_dimension=0, tiled=True)
        pieces = []
        start = 0
        for term in terms:
            pieces.append(owned[:, start : start + term.shape[1]].astype(jnp.float32))
            start += term.shape[1]
        return pieces

    def scatter_layer(terms, layer_index):
        if layer_index > 0:
            return tuple(scatter_terms(terms))
        early = scatter_terms(terms[3:])
        joined = shard_scatter(
            jnp.concatenate([term.astype(jnp.bfloat16) for term in terms[:3]], axis=1)
        )
        late = []
        start = 0
        for term in terms[:3]:
            late.append(joined[:, start : start + term.shape[1]])
            start += term.shape[1]
        return tuple(late + early)

    kept_weights = []
    stored_layers = []
    hidden = tokens
    for layer_index in range(layer_count):
        gathered = gather_layer(layer_index)
        kept_weights.append(gathered)
        (
            forward_query_full,
            forward_key_full,
            forward_value_full,
            forward_output_full,
            forward_gate_full,
            forward_up_full,
            forward_down_full,
        ) = gathered
        forward_scale_one = row_scale(hidden)
        forward_normed = (hidden * forward_scale_one * attention_norm_weight[layer_index]).astype(
            jnp.bfloat16
        )
        query_raw = jnp.dot(
            forward_normed, forward_query_full, preferred_element_type=jnp.float32
        ).reshape(row_count, local_heads, head_size)
        key_raw = jnp.dot(
            forward_normed, forward_key_full, preferred_element_type=jnp.float32
        ).reshape(row_count, local_groups, head_size)
        values = jnp.dot(
            forward_normed, forward_value_full, preferred_element_type=jnp.float32
        ).astype(jnp.bfloat16)
        forward_query_scale = row_scale(query_raw)
        forward_query_unit = query_raw * forward_query_scale
        forward_key_scale = row_scale(key_raw)
        forward_key_unit = key_raw * forward_key_scale
        queries = rotate(
            forward_query_unit * query_gain[layer_index], cosine_table, sine_table
        ).astype(jnp.bfloat16)
        keys = rotate(forward_key_unit * key_gain[layer_index], cosine_table, sine_table).astype(
            jnp.bfloat16
        )
        keys = keys.reshape(row_count, local_groups * head_size)
        all_keys = ctx_gather(keys)
        all_values = ctx_gather(values)
        forward_query_groups = queries.reshape(row_count, local_groups, per_group, head_size)
        forward_key_groups = all_keys.reshape(seq_length, local_groups, head_size)
        forward_value_groups = all_values.reshape(seq_length, local_groups, head_size)
        forward_attended, forward_log_total = fused_attention(
            queries.reshape(row_count, local_heads * head_size),
            all_keys,
            all_values,
            query_ids,
            segment_row,
            positions,
            per_group,
            head_size,
        )
        forward_log_total = forward_log_total.reshape(local_groups, per_group, row_count, 1)
        forward_middle = hidden + tp_sum(contract_last(forward_attended, forward_output_full))
        forward_scale_two = row_scale(forward_middle)
        forward_feed_normed = (
            forward_middle * forward_scale_two * feedforward_gain[layer_index]
        ).astype(jnp.bfloat16)
        forward_gate_linear = jnp.dot(
            forward_feed_normed, forward_gate_full, preferred_element_type=jnp.float32
        )
        forward_up_linear = jnp.dot(
            forward_feed_normed, forward_up_full, preferred_element_type=jnp.float32
        )
        forward_activated = (jax.nn.silu(forward_gate_linear) * forward_up_linear).astype(
            jnp.bfloat16
        )
        result = forward_middle + tp_sum(contract_last(forward_activated, forward_down_full))
        forward_stored = (
            hidden,
            forward_scale_one,
            forward_normed,
            forward_query_unit,
            forward_query_scale,
            forward_key_unit,
            forward_key_scale,
            forward_query_groups,
            forward_key_groups,
            forward_value_groups,
            forward_log_total,
            forward_attended,
            forward_middle,
            forward_scale_two,
            forward_feed_normed,
            forward_gate_linear,
            forward_up_linear,
            forward_activated,
        )
        hidden = result
        stored_layers.append(forward_stored)
    grad_flow = cotangent
    weight_sums = [None] * layer_count
    gain_parts = [None] * layer_count
    for layer_index in reversed(range(layer_count)):
        gathered = kept_weights[layer_index]
        backward_stored = stored_layers[layer_index]
        query_full, key_full, value_full, output_full, gate_full, up_full, down_full = gathered
        (
            source,
            scale_one,
            normed,
            query_unit,
            query_scale,
            key_unit,
            key_scale,
            backward_query_groups,
            backward_key_groups,
            value_groups,
            log_total,
            attended,
            middle,
            scale_two,
            feed_normed,
            gate_linear,
            up_linear,
            activated,
        ) = backward_stored
        grad_half = grad_flow.astype(jnp.bfloat16)
        down_grad = contract_first(grad_half, activated)
        act_grad = jnp.dot(grad_half, down_full, preferred_element_type=jnp.float32)
        sigmoid_gate = jax.nn.sigmoid(gate_linear)
        gate_grad = (
            act_grad * up_linear * sigmoid_gate * (1.0 + gate_linear * (1.0 - sigmoid_gate))
        ).astype(jnp.bfloat16)
        up_grad = (act_grad * jax.nn.silu(gate_linear)).astype(jnp.bfloat16)
        gate_weight_grad = contract_first(feed_normed, gate_grad)
        up_weight_grad = contract_first(feed_normed, up_grad)
        feed_part = contract_last(gate_grad, gate_full) + contract_last(up_grad, up_full)
        feed_grad = tp_sum(feed_part)
        feed_unit = middle * scale_two
        feed_gain_grad = column_share(feed_grad, feed_unit)
        middle_grad = grad_flow + norm_back(
            feed_grad, feed_unit, scale_two, feedforward_gain[layer_index]
        )
        middle_half = middle_grad.astype(jnp.bfloat16)
        output_weight_grad = contract_first(middle_half, attended)
        attended_grad = jnp.dot(
            middle_half, output_full, preferred_element_type=jnp.float32
        ).astype(jnp.bfloat16)
        attended_grad = attended_grad.reshape(row_count, local_groups, per_group, head_size)
        scores = attention_scores(backward_query_groups, backward_key_groups)
        exact = jnp.where(allowed, jnp.exp(scores - log_total), 0.0)
        half_probs = exact.astype(jnp.bfloat16)
        value_grad = jnp.einsum(
            "grqk,qgrd->kgd", half_probs, attended_grad, preferred_element_type=jnp.float32
        )
        prob_grad = jnp.einsum(
            "qgrd,kgd->grqk", attended_grad, value_groups, preferred_element_type=jnp.float32
        )
        row_delta = jnp.sum(exact * prob_grad, axis=-1, keepdims=True)
        score_grad = (exact * (prob_grad - row_delta) * score_scale).astype(jnp.bfloat16)
        query_grad = jnp.einsum(
            "grqk,kgd->qgrd", score_grad, backward_key_groups, preferred_element_type=jnp.float32
        )
        query_grad = query_grad.reshape(row_count, local_heads, head_size)
        key_grad = jnp.einsum(
            "grqk,qgrd->kgd", score_grad, backward_query_groups, preferred_element_type=jnp.float32
        )
        key_own = ctx_scatter(key_grad.reshape(seq_length, local_groups * head_size))
        value_own = ctx_scatter(value_grad.reshape(seq_length, local_groups * head_size)).astype(
            jnp.bfloat16
        )
        query_turned = rotate(query_grad, cosine_table, -sine_table)
        key_turned = rotate(
            key_own.reshape(row_count, local_groups, head_size), cosine_table, -sine_table
        )
        query_gain_grad = jnp.sum(query_turned * query_unit, axis=(0, 1))
        key_gain_grad = jnp.sum(key_turned * key_unit, axis=(0, 1))
        query_pre = norm_back(
            query_turned, query_unit, query_scale, query_gain[layer_index]
        ).astype(jnp.bfloat16)
        query_pre = query_pre.reshape(row_count, local_heads * head_size)
        key_pre = norm_back(key_turned, key_unit, key_scale, key_gain[layer_index]).astype(
            jnp.bfloat16
        )
        key_pre = key_pre.reshape(row_count, local_groups * head_size)
        query_weight_grad = contract_first(normed, query_pre)
        key_weight_grad = contract_first(normed, key_pre)
        value_weight_grad = contract_first(normed, value_own)
        attention_part = (
            contract_last(query_pre, query_full)
            + contract_last(key_pre, key_full)
            + contract_last(value_own, value_full)
        )
        normed_grad = tp_sum(attention_part)
        source_unit = source * scale_one
        attention_gain_grad = column_share(normed_grad, source_unit)
        source_grad = middle_grad + norm_back(
            normed_grad, source_unit, scale_one, attention_norm_weight[layer_index]
        )
        weight_terms = (
            query_weight_grad,
            key_weight_grad,
            value_weight_grad,
            output_weight_grad,
            gate_weight_grad,
            up_weight_grad,
            down_grad,
        )
        gain_terms = (attention_gain_grad, query_gain_grad, key_gain_grad, feed_gain_grad)
        grad_flow, weight_terms, gain_terms = (source_grad, weight_terms, gain_terms)
        grad_query, grad_key, grad_value, grad_output, grad_gate, grad_up, grad_down = weight_terms
        weight_sums[layer_index] = scatter_layer(weight_terms, layer_index)
        gain_parts[layer_index] = gain_terms
    gain_stacks = [
        jnp.stack([member[which] for member in gain_parts]) for which in range(4)
    ]
    gain_edges = [0]
    for member in gain_stacks:
        gain_edges.append(gain_edges[-1] + member.shape[1])
    gain_joined = all_sum(jnp.concatenate(gain_stacks, axis=1))
    gain_totals = [
        gain_joined[:, gain_edges[which] : gain_edges[which + 1]] for which in range(4)
    ]
    stacked = [jnp.stack([member[which] for member in weight_sums]) for which in range(7)]
    return (
        hidden,
        grad_flow,
        gain_totals[0],
        gain_totals[1],
        gain_totals[2],
        gain_totals[3],
        stacked[0],
        stacked[1],
        stacked[2],
        stacked[3],
        stacked[4],
        stacked[5],
        stacked[6],
    )


def solution(mesh):
    in_specs = (
        P(("fsdp", "ctx"), None),
        P(("fsdp", "ctx"), None),
        P("fsdp", None),
        P(),
        P(),
        P(),
        P(),
        P(None, ("fsdp", "ctx"), "tp"),
        P(None, ("fsdp", "ctx"), "tp"),
        P(None, ("fsdp", "ctx"), "tp"),
        P(None, ("fsdp", "ctx"), "tp"),
        P(None, ("fsdp", "ctx"), "tp"),
        P(None, ("fsdp", "ctx"), "tp"),
        P(None, ("fsdp", "ctx"), "tp"),
    )
    out_specs = (
        P(("fsdp", "ctx"), None),
        P(("fsdp", "ctx"), None),
        P(),
        P(),
        P(),
        P(),
        P(None, ("fsdp", "ctx"), "tp"),
        P(None, ("fsdp", "ctx"), "tp"),
        P(None, ("fsdp", "ctx"), "tp"),
        P(None, ("fsdp", "ctx"), "tp"),
        P(None, ("fsdp", "ctx"), "tp"),
        P(None, ("fsdp", "ctx"), "tp"),
        P(None, ("fsdp", "ctx"), "tp"),
    )
    return jax.shard_map(
        per_device, mesh=mesh, in_specs=in_specs, out_specs=out_specs, check_vma=False
    )
```

```python
import jax
import jax.numpy as jnp
from jax import lax
from jax.experimental import pallas as pl
from jax.sharding import PartitionSpec as P
import functools

eps = 1e-06
rope_base = 1000000.0


def contract_last(left_side, right_side):
    return lax.dot_general(
        left_side, right_side, (((1,), (1,)), ((), ())), preferred_element_type=jnp.float32
    )


def contract_first(left_side, right_side):
    return lax.dot_general(
        left_side, right_side, (((0,), (0,)), ((), ())), preferred_element_type=jnp.float32
    )


def row_scale(source):
    return lax.rsqrt(jnp.mean(source * source, axis=-1, keepdims=True) + eps)


def norm_back(grad_out, normalized, scaling, norm_gain):
    weighted = grad_out * norm_gain
    return scaling * (
        weighted - normalized * jnp.mean(weighted * normalized, axis=-1, keepdims=True)
    )


def rotary_tables(positions, head_size):
    halfway = head_size // 2
    frequency = rope_base ** (-2.0 * jnp.arange(halfway, dtype=jnp.float32) / head_size)
    angles = positions.astype(jnp.float32)[:, None] * frequency[None, :]
    return (jnp.cos(angles)[:, None, :], jnp.sin(angles)[:, None, :])


def rotate(source, cosine_table, sine_table):
    halfway = source.shape[-1] // 2
    leading = source[..., :halfway]
    trailing = source[..., halfway:]
    return jnp.concatenate(
        [
            leading * cosine_table - trailing * sine_table,
            trailing * cosine_table + leading * sine_table,
        ],
        axis=-1,
    )


def attention_kernel(
    query_ref, key_ref, value_ref, query_ids_ref, key_ids_ref, position_ref,
    attended_ref, log_total_ref, *, groups, per_group, head_size, score_scale
):
    query_ids = query_ids_ref[...]
    key_ids = key_ids_ref[...]
    key_positions = lax.broadcasted_iota(jnp.int32, key_ids.shape, 1)
    allowed = (query_ids == key_ids) & (key_positions <= position_ref[...])
    for group in range(groups):
        key_block = key_ref[:, group * head_size : (group + 1) * head_size]
        value_block = value_ref[:, group * head_size : (group + 1) * head_size]
        for member in range(per_group):
            head = group * per_group + member
            query_block = query_ref[:, head * head_size : (head + 1) * head_size]
            scores = (
                lax.dot_general(
                    query_block, key_block, (((1,), (1,)), ((), ())),
                    preferred_element_type=jnp.float32,
                )
                * score_scale
            )
            exponent = jnp.where(allowed, jnp.exp(scores), 0.0)
            log_total = jnp.log(jnp.sum(exponent, axis=1, keepdims=True))
            probs = jnp.where(allowed, jnp.exp(scores - log_total), 0.0).astype(jnp.bfloat16)
            attended = jnp.dot(probs, value_block, preferred_element_type=jnp.float32)
            attended_ref[:, head * head_size : (head + 1) * head_size] = attended.astype(
                jnp.bfloat16
            )
            log_total_ref[head] = log_total


def fused_attention(queries, keys, values, query_ids, key_ids, positions, per_group, head_size):
    rows = queries.shape[0]
    heads = queries.shape[1] // head_size
    groups = heads // per_group
    keys_count = keys.shape[0]
    kernel = functools.partial(
        attention_kernel, groups=groups, per_group=per_group, head_size=head_size,
        score_scale=head_size ** (-0.5),
    )
    return pl.pallas_call(
        kernel,
        out_shape=(
            jax.ShapeDtypeStruct((rows, heads * head_size), jnp.bfloat16),
            jax.ShapeDtypeStruct((heads, rows, 1), jnp.float32),
        ),
        cost_estimate=pl.CostEstimate(
            flops=4 * heads * rows * keys_count * head_size,
            transcendentals=2 * heads * rows * keys_count,
            bytes_accessed=2 * (2 * rows * heads * head_size + 2 * keys_count * groups * head_size),
        ),
    )(
        queries, keys, values, query_ids.reshape(rows, 1), key_ids.reshape(1, keys_count),
        positions.reshape(rows, 1),
    )


def tp_sum(term):
    tp_count = lax.axis_size("tp")
    tp_index = lax.axis_index("tp")
    current = term.astype(jnp.bfloat16)
    half = current.shape[0] // 2
    upper = tp_index % 2
    core_pairs = [(device, device ^ 1) for device in range(tp_count)]
    kept = lax.dynamic_slice_in_dim(current, upper * half, half, 0)
    sent = lax.dynamic_slice_in_dim(current, (1 - upper) * half, half, 0)
    received = lax.ppermute(sent, "tp", core_pairs)
    total = kept.astype(jnp.float32) + received.astype(jnp.float32)
    step = 2
    while step < tp_count:
        mine = total.astype(jnp.bfloat16)
        pairs = [(device, device ^ step) for device in range(tp_count)]
        received = lax.ppermute(mine, "tp", pairs)
        total = mine.astype(jnp.float32) + received.astype(jnp.float32)
        step *= 2
    mine = total.astype(jnp.bfloat16)
    other = lax.ppermute(mine, "tp", core_pairs)
    joined = jnp.where(
        upper == 0,
        jnp.concatenate([mine, other], axis=0),
        jnp.concatenate([other, mine], axis=0),
    )
    return joined.astype(jnp.float32)


def swap_halves(local, axis_name):
    return lax.ppermute(local, axis_name, [(0, 1), (1, 0)])


def ctx_gather(local):
    other = swap_halves(local, "ctx")
    first = lax.axis_index("ctx") == 0
    return jnp.where(
        first, jnp.concatenate([local, other], axis=0), jnp.concatenate([other, local], axis=0)
    )


def ctx_scatter(full):
    rows = full.shape[0] // 2
    place = lax.axis_index("ctx")
    kept = lax.dynamic_slice_in_dim(full, place * rows, rows, 0)
    sent = lax.dynamic_slice_in_dim(full, (1 - place) * rows, rows, 0)
    received = swap_halves(sent.astype(jnp.bfloat16), "ctx")
    return kept.astype(jnp.bfloat16).astype(jnp.float32) + received.astype(jnp.float32)


def all_sum(value):
    total = value
    for axis_name in ("tp", "ctx", "fsdp"):
        count = lax.axis_size(axis_name)
        step = 1
        while step < count:
            pairs = [(device, device ^ step) for device in range(count)]
            total = total + lax.ppermute(total, axis_name, pairs)
            step *= 2
    return total


def shard_scatter(full):
    fsdp_count = lax.axis_size("fsdp")
    ctx_count = lax.axis_size("ctx")
    fsdp_bits = []
    step = 1
    while step < fsdp_count:
        fsdp_bits.append(step)
        step *= 2
    rows = full.shape[0] // (fsdp_count * ctx_count)
    current = full.astype(jnp.bfloat16).reshape((2,) * len(fsdp_bits) + (ctx_count, rows, -1))
    order = [("fsdp", 1), ("fsdp", 2), ("ctx", 1)] + [("fsdp", bit) for bit in fsdp_bits[2:]]
    for axis_name, bit in order:
        if axis_name == "fsdp":
            dim = len(fsdp_bits) - 1 - fsdp_bits.index(bit)
        else:
            dim = len(fsdp_bits)
        upper = (lax.axis_index(axis_name) // bit) % 2
        kept = lax.dynamic_slice_in_dim(current, upper, 1, dim)
        sent = lax.dynamic_slice_in_dim(current, 1 - upper, 1, dim)
        count = fsdp_count if axis_name == "fsdp" else ctx_count
        pairs = [(device, device ^ bit) for device in range(count)]
        received = lax.ppermute(sent.astype(jnp.bfloat16), axis_name, pairs)
        current = kept.astype(jnp.float32) + received.astype(jnp.float32)
    return current.reshape(rows, -1)


def shard_gather(local):
    fsdp_count = lax.axis_size("fsdp")
    ctx_count = lax.axis_size("ctx")
    fsdp_bits = []
    step = 1
    while step < fsdp_count:
        fsdp_bits.append(step)
        step *= 2
    current = local.reshape((1,) * (len(fsdp_bits) + 1) + local.shape)
    order = [("ctx", 1)] + [("fsdp", bit) for bit in fsdp_bits[2:]] + [("fsdp", 1), ("fsdp", 2)]
    for axis_name, bit in order:
        if axis_name == "fsdp":
            dim = len(fsdp_bits) - 1 - fsdp_bits.index(bit)
        else:
            dim = len(fsdp_bits)
        count = fsdp_count if axis_name == "fsdp" else ctx_count
        pairs = [(device, device ^ bit) for device in range(count)]
        received = lax.ppermute(current, axis_name, pairs)
        upper = (lax.axis_index(axis_name) // bit) % 2
        current = jnp.where(
            upper == 0,
            jnp.concatenate([current, received], axis=dim),
            jnp.concatenate([received, current], axis=dim),
        )
    return current.reshape(-1, local.shape[1])


def per_device(
    tokens,
    cotangent,
    segments,
    attention_norm_weight,
    query_gain,
    key_gain,
    feedforward_gain,
    query_weight,
    key_projection_matrix,
    value_projection_matrix,
    output_weight,
    gate_weight,
    up_weight,
    down_weight,
):
    row_count = tokens.shape[0]
    model_width = tokens.shape[1]
    head_size = query_gain.shape[1]
    local_heads = query_weight.shape[2] // head_size
    local_groups = key_projection_matrix.shape[2] // head_size
    per_group = local_heads // local_groups
    layer_count = query_weight.shape[0]
    seq_length = segments.shape[1]
    row_start = lax.axis_index("ctx") * row_count
    column_width = model_width // lax.axis_size("tp")
    column_start = lax.axis_index("tp") * column_width
    score_scale = head_size ** (-0.5)
    positions = row_start + jnp.arange(row_count, dtype=jnp.int32)
    segment_row = segments[0]
    query_ids = lax.dynamic_slice_in_dim(segment_row, row_start, row_count)
    key_positions = jnp.arange(seq_length, dtype=jnp.int32)
    allowed = (query_ids[:, None] == segment_row[None, :]) & (
        key_positions[None, :] <= positions[:, None]
    )
    cosine_table, sine_table = rotary_tables(positions, head_size)

    def column_share(grad_rows, normalized):
        gradient_portion = lax.dynamic_slice_in_dim(grad_rows, column_start, column_width, 1)
        unit_slice = lax.dynamic_slice_in_dim(normalized, column_start, column_width, 1)
        part_sum = jnp.sum(gradient_portion * unit_slice, axis=0)
        return lax.dynamic_update_slice_in_dim(
            jnp.zeros((model_width,), jnp.float32), part_sum, column_start, 0
        )

    def attention_scores(query_groups, key_groups):
        return (
            jnp.einsum(
                "qgrd,kgd->grqk", query_groups, key_groups, preferred_element_type=jnp.float32
            )
            * score_scale
        )

    weight_shards = (
        query_weight,
        key_projection_matrix,
        value_projection_matrix,
        output_weight,
        gate_weight,
        up_weight,
        down_weight,
    )
    widths = [member.shape[2] for member in weight_shards]
    edges = [0]
    for width in widths:
        edges.append(edges[-1] + width)

    def gather_early(layer_index):
        early = jnp.concatenate([member[layer_index] for member in weight_shards[:3]], axis=1)
        return shard_gather(early)

    def gather_layer(layer_index, early_full):
        late = jnp.concatenate([member[layer_index] for member in weight_shards[3:]], axis=1)
        late_full = lax.all_gather(late, ("fsdp", "ctx"), axis=0, tiled=True)
        pieces = []
        for k in range(len(widths)):
            if k < 3:
                pieces.append(early_full[:, edges[k] : edges[k + 1]])
            else:
                pieces.append(late_full[:, edges[k] - edges[3] : edges[k + 1] - edges[3]])
        return tuple(pieces)

    def scatter_terms(terms):
        joined = jnp.concatenate([term.astype(jnp.bfloat16) for term in terms], axis=1)
        owned = lax.psum_scatter(joined, ("fsdp", "ctx"), scatter_dimension=0, tiled=True)
        pieces = []
        start = 0
        for term in terms:
            pieces.append(owned[:, start : start + term.shape[1]].astype(jnp.float32))
            start += term.shape[1]
        return pieces

    def scatter_layer(terms, layer_index):
        early = scatter_terms(terms[3:])
        joined = shard_scatter(
            jnp.concatenate([term.astype(jnp.bfloat16) for term in terms[:3]], axis=1)
        )
        late = []
        start = 0
        for term in terms[:3]:
            late.append(joined[:, start : start + term.shape[1]])
            start += term.shape[1]
        return tuple(late + early)

    kept_weights = []
    early_gathered = [gather_early(layer_index) for layer_index in range(layer_count)]
    stored_layers = []
    hidden = tokens
    for layer_index in range(layer_count):
        gathered = gather_layer(layer_index, early_gathered[layer_index])
        kept_weights.append(gathered)
        (
            forward_query_full,
            forward_key_full,
            forward_value_full,
            forward_output_full,
            forward_gate_full,
            forward_up_full,
            forward_down_full,
        ) = gathered
        forward_scale_one = row_scale(hidden)
        forward_normed = (hidden * forward_scale_one * attention_norm_weight[layer_index]).astype(
            jnp.bfloat16
        )
        query_raw = jnp.dot(
            forward_normed, forward_query_full, preferred_element_type=jnp.float32
        ).reshape(row_count, local_heads, head_size)
        key_raw = jnp.dot(
            forward_normed, forward_key_full, preferred_element_type=jnp.float32
        ).reshape(row_count, local_groups, head_size)
        values = jnp.dot(
            forward_normed, forward_value_full, preferred_element_type=jnp.float32
        ).astype(jnp.bfloat16)
        forward_query_scale = row_scale(query_raw)
        forward_query_unit = query_raw * forward_query_scale
        forward_key_scale = row_scale(key_raw)
        forward_key_unit = key_raw * forward_key_scale
        queries = rotate(
            forward_query_unit * query_gain[layer_index], cosine_table, sine_table
        ).astype(jnp.bfloat16)
        keys = rotate(forward_key_unit * key_gain[layer_index], cosine_table, sine_table).astype(
            jnp.bfloat16
        )
        keys = keys.reshape(row_count, local_groups * head_size)
        all_keys = ctx_gather(keys)
        all_values = ctx_gather(values)
        forward_query_groups = queries.reshape(row_count, local_groups, per_group, head_size)
        forward_key_groups = all_keys.reshape(seq_length, local_groups, head_size)
        forward_value_groups = all_values.reshape(seq_length, local_groups, head_size)
        forward_attended, forward_log_total = fused_attention(
            queries.reshape(row_count, local_heads * head_size),
            all_keys,
            all_values,
            query_ids,
            segment_row,
            positions,
            per_group,
            head_size,
        )
        forward_log_total = forward_log_total.reshape(local_groups, per_group, row_count, 1)
        forward_middle = hidden + tp_sum(contract_last(forward_attended, forward_output_full))
        if layer_index + 1 < layer_count:
            forward_middle, early_gathered[layer_index + 1] = lax.optimization_barrier(
                (forward_middle, early_gathered[layer_index + 1])
            )
        forward_scale_two = row_scale(forward_middle)
        forward_feed_normed = (
            forward_middle * forward_scale_two * feedforward_gain[layer_index]
        ).astype(jnp.bfloat16)
        forward_gate_linear = jnp.dot(
            forward_feed_normed, forward_gate_full, preferred_element_type=jnp.float32
        )
        forward_up_linear = jnp.dot(
            forward_feed_normed, forward_up_full, preferred_element_type=jnp.float32
        )
        forward_activated = (jax.nn.silu(forward_gate_linear) * forward_up_linear).astype(
            jnp.bfloat16
        )
        result = forward_middle + tp_sum(contract_last(forward_activated, forward_down_full))
        forward_stored = (
            hidden,
            forward_scale_one,
            forward_normed,
            forward_query_unit,
            forward_query_scale,
            forward_key_unit,
            forward_key_scale,
            forward_query_groups,
            forward_key_groups,
            forward_value_groups,
            forward_log_total,
            forward_attended,
            forward_middle,
            forward_scale_two,
            forward_feed_normed,
            forward_gate_linear,
            forward_up_linear,
            forward_activated,
        )
        hidden = result
        stored_layers.append(forward_stored)
    grad_flow = cotangent
    weight_sums = [None] * layer_count
    gain_parts = [None] * layer_count
    for layer_index in reversed(range(layer_count)):
        gathered = kept_weights[layer_index]
        backward_stored = stored_layers[layer_index]
        query_full, key_full, value_full, output_full, gate_full, up_full, down_full = gathered
        (
            source,
            scale_one,
            normed,
            query_unit,
            query_scale,
            key_unit,
            key_scale,
            backward_query_groups,
            backward_key_groups,
            value_groups,
            log_total,
            attended,
            middle,
            scale_two,
            feed_normed,
            gate_linear,
            up_linear,
            activated,
        ) = backward_stored
        grad_half = grad_flow.astype(jnp.bfloat16)
        down_grad = contract_first(grad_half, activated)
        act_grad = jnp.dot(grad_half, down_full, preferred_element_type=jnp.float32)
        sigmoid_gate = jax.nn.sigmoid(gate_linear)
        gate_grad = (
            act_grad * up_linear * sigmoid_gate * (1.0 + gate_linear * (1.0 - sigmoid_gate))
        ).astype(jnp.bfloat16)
        up_grad = (act_grad * jax.nn.silu(gate_linear)).astype(jnp.bfloat16)
        gate_weight_grad = contract_first(feed_normed, gate_grad)
        up_weight_grad = contract_first(feed_normed, up_grad)
        feed_part = contract_last(gate_grad, gate_full) + contract_last(up_grad, up_full)
        feed_grad = tp_sum(feed_part)
        feed_unit = middle * scale_two
        feed_gain_grad = column_share(feed_grad, feed_unit)
        middle_grad = grad_flow + norm_back(
            feed_grad, feed_unit, scale_two, feedforward_gain[layer_index]
        )
        middle_half = middle_grad.astype(jnp.bfloat16)
        output_weight_grad = contract_first(middle_half, attended)
        attended_grad = jnp.dot(
            middle_half, output_full, preferred_element_type=jnp.float32
        ).astype(jnp.bfloat16)
        attended_grad = attended_grad.reshape(row_count, local_groups, per_group, head_size)
        scores = attention_scores(backward_query_groups, backward_key_groups)
        exact = jnp.where(allowed, jnp.exp(scores - log_total), 0.0)
        half_probs = exact.astype(jnp.bfloat16)
        value_grad = jnp.einsum(
            "grqk,qgrd->kgd", half_probs, attended_grad, preferred_element_type=jnp.float32
        )
        prob_grad = jnp.einsum(
            "qgrd,kgd->grqk", attended_grad, value_groups, preferred_element_type=jnp.float32
        )
        row_delta = jnp.sum(exact * prob_grad, axis=-1, keepdims=True)
        score_grad = (exact * (prob_grad - row_delta) * score_scale).astype(jnp.bfloat16)
        query_grad = jnp.einsum(
            "grqk,kgd->qgrd", score_grad, backward_key_groups, preferred_element_type=jnp.float32
        )
        query_grad = query_grad.reshape(row_count, local_heads, head_size)
        key_grad = jnp.einsum(
            "grqk,qgrd->kgd", score_grad, backward_query_groups, preferred_element_type=jnp.float32
        )
        key_own = ctx_scatter(key_grad.reshape(seq_length, local_groups * head_size))
        value_own = ctx_scatter(value_grad.reshape(seq_length, local_groups * head_size)).astype(
            jnp.bfloat16
        )
        query_turned = rotate(query_grad, cosine_table, -sine_table)
        key_turned = rotate(
            key_own.reshape(row_count, local_groups, head_size), cosine_table, -sine_table
        )
        query_gain_grad = jnp.sum(query_turned * query_unit, axis=(0, 1))
        key_gain_grad = jnp.sum(key_turned * key_unit, axis=(0, 1))
        query_pre = norm_back(
            query_turned, query_unit, query_scale, query_gain[layer_index]
        ).astype(jnp.bfloat16)
        query_pre = query_pre.reshape(row_count, local_heads * head_size)
        key_pre = norm_back(key_turned, key_unit, key_scale, key_gain[layer_index]).astype(
            jnp.bfloat16
        )
        key_pre = key_pre.reshape(row_count, local_groups * head_size)
        query_weight_grad = contract_first(normed, query_pre)
        key_weight_grad = contract_first(normed, key_pre)
        value_weight_grad = contract_first(normed, value_own)
        attention_part = (
            contract_last(query_pre, query_full)
            + contract_last(key_pre, key_full)
            + contract_last(value_own, value_full)
        )
        normed_grad = tp_sum(attention_part)
        source_unit = source * scale_one
        attention_gain_grad = column_share(normed_grad, source_unit)
        source_grad = middle_grad + norm_back(
            normed_grad, source_unit, scale_one, attention_norm_weight[layer_index]
        )
        weight_terms = (
            query_weight_grad,
            key_weight_grad,
            value_weight_grad,
            output_weight_grad,
            gate_weight_grad,
            up_weight_grad,
            down_grad,
        )
        gain_terms = (attention_gain_grad, query_gain_grad, key_gain_grad, feed_gain_grad)
        grad_flow, weight_terms, gain_terms = (source_grad, weight_terms, gain_terms)
        grad_query, grad_key, grad_value, grad_output, grad_gate, grad_up, grad_down = weight_terms
        weight_sums[layer_index] = scatter_layer(weight_terms, layer_index)
        gain_parts[layer_index] = gain_terms
    gain_stacks = [
        jnp.stack([member[which] for member in gain_parts]) for which in range(4)
    ]
    gain_edges = [0]
    for member in gain_stacks:
        gain_edges.append(gain_edges[-1] + member.shape[1])
    gain_joined = all_sum(jnp.concatenate(gain_stacks, axis=1))
    gain_totals = [
        gain_joined[:, gain_edges[which] : gain_edges[which + 1]] for which in range(4)
    ]
    stacked = [jnp.stack([member[which] for member in weight_sums]) for which in range(7)]
    return (
        hidden,
        grad_flow,
        gain_totals[0],
        gain_totals[1],
        gain_totals[2],
        gain_totals[3],
        stacked[0],
        stacked[1],
        stacked[2],
        stacked[3],
        stacked[4],
        stacked[5],
        stacked[6],
    )


def solution(mesh):
    in_specs = (
        P(("fsdp", "ctx"), None),
        P(("fsdp", "ctx"), None),
        P("fsdp", None),
        P(),
        P(),
        P(),
        P(),
        P(None, ("fsdp", "ctx"), "tp"),
        P(None, ("fsdp", "ctx"), "tp"),
        P(None, ("fsdp", "ctx"), "tp"),
        P(None, ("fsdp", "ctx"), "tp"),
        P(None, ("fsdp", "ctx"), "tp"),
        P(None, ("fsdp", "ctx"), "tp"),
        P(None, ("fsdp", "ctx"), "tp"),
    )
    out_specs = (
        P(("fsdp", "ctx"), None),
        P(("fsdp", "ctx"), None),
        P(),
        P(),
        P(),
        P(),
        P(None, ("fsdp", "ctx"), "tp"),
        P(None, ("fsdp", "ctx"), "tp"),
        P(None, ("fsdp", "ctx"), "tp"),
        P(None, ("fsdp", "ctx"), "tp"),
        P(None, ("fsdp", "ctx"), "tp"),
        P(None, ("fsdp", "ctx"), "tp"),
        P(None, ("fsdp", "ctx"), "tp"),
    )
    return jax.shard_map(
        per_device, mesh=mesh, in_specs=in_specs, out_specs=out_specs, check_vma=False
    )
```

```python
import jax
import jax.numpy as jnp
from jax import lax
from jax.sharding import PartitionSpec as P

eps = 1e-06
rope_base = 1000000.0


def contract_last(left_side, right_side):
    return lax.dot_general(
        left_side, right_side, (((1,), (1,)), ((), ())), preferred_element_type=jnp.float32
    )


def contract_first(left_side, right_side):
    return lax.dot_general(
        left_side, right_side, (((0,), (0,)), ((), ())), preferred_element_type=jnp.float32
    )


def row_scale(source):
    return lax.rsqrt(jnp.mean(source * source, axis=-1, keepdims=True) + eps)


def norm_back(grad_out, normalized, scaling, norm_gain):
    weighted = grad_out * norm_gain
    return scaling * (
        weighted - normalized * jnp.mean(weighted * normalized, axis=-1, keepdims=True)
    )


def rotary_tables(positions, head_size):
    halfway = head_size // 2
    frequency = rope_base ** (-2.0 * jnp.arange(halfway, dtype=jnp.float32) / head_size)
    angles = positions.astype(jnp.float32)[:, None] * frequency[None, :]
    return (jnp.cos(angles)[:, None, :], jnp.sin(angles)[:, None, :])


def rotate(source, cosine_table, sine_table):
    halfway = source.shape[-1] // 2
    leading = source[..., :halfway]
    trailing = source[..., halfway:]
    return jnp.concatenate(
        [
            leading * cosine_table - trailing * sine_table,
            trailing * cosine_table + leading * sine_table,
        ],
        axis=-1,
    )


def tp_sum(term):
    tp_count = lax.axis_size("tp")
    tp_index = lax.axis_index("tp")
    current = term.astype(jnp.bfloat16)
    half = current.shape[0] // 2
    upper = tp_index % 2
    core_pairs = [(device, device ^ 1) for device in range(tp_count)]
    kept = lax.dynamic_slice_in_dim(current, upper * half, half, 0)
    sent = lax.dynamic_slice_in_dim(current, (1 - upper) * half, half, 0)
    received = lax.ppermute(sent, "tp", core_pairs)
    total = kept.astype(jnp.float32) + received.astype(jnp.float32)
    step = 2
    while step < tp_count:
        mine = total.astype(jnp.bfloat16)
        pairs = [(device, device ^ step) for device in range(tp_count)]
        received = lax.ppermute(mine, "tp", pairs)
        total = mine.astype(jnp.float32) + received.astype(jnp.float32)
        step *= 2
    mine = total.astype(jnp.bfloat16)
    other = lax.ppermute(mine, "tp", core_pairs)
    joined = jnp.where(
        upper == 0,
        jnp.concatenate([mine, other], axis=0),
        jnp.concatenate([other, mine], axis=0),
    )
    return joined.astype(jnp.float32)


def swap_halves(local, axis_name):
    return lax.ppermute(local, axis_name, [(0, 1), (1, 0)])


def ctx_gather(local):
    other = swap_halves(local, "ctx")
    first = lax.axis_index("ctx") == 0
    return jnp.where(
        first, jnp.concatenate([local, other], axis=0), jnp.concatenate([other, local], axis=0)
    )


def ctx_scatter(full):
    rows = full.shape[0] // 2
    place = lax.axis_index("ctx")
    kept = lax.dynamic_slice_in_dim(full, place * rows, rows, 0)
    sent = lax.dynamic_slice_in_dim(full, (1 - place) * rows, rows, 0)
    received = swap_halves(sent.astype(jnp.bfloat16), "ctx")
    return kept.astype(jnp.bfloat16).astype(jnp.float32) + received.astype(jnp.float32)


def all_sum(value):
    total = value
    for axis_name in ("tp", "ctx", "fsdp"):
        count = lax.axis_size(axis_name)
        step = 1
        while step < count:
            pairs = [(device, device ^ step) for device in range(count)]
            total = total + lax.ppermute(total, axis_name, pairs)
            step *= 2
    return total


def shard_scatter(full):
    fsdp_count = lax.axis_size("fsdp")
    ctx_count = lax.axis_size("ctx")
    fsdp_bits = []
    step = 1
    while step < fsdp_count:
        fsdp_bits.append(step)
        step *= 2
    rows = full.shape[0] // (fsdp_count * ctx_count)
    current = full.astype(jnp.bfloat16).reshape((2,) * len(fsdp_bits) + (ctx_count, rows, -1))
    order = [("fsdp", 1), ("fsdp", 2), ("ctx", 1)] + [("fsdp", bit) for bit in fsdp_bits[2:]]
    for axis_name, bit in order:
        if axis_name == "fsdp":
            dim = len(fsdp_bits) - 1 - fsdp_bits.index(bit)
        else:
            dim = len(fsdp_bits)
        upper = (lax.axis_index(axis_name) // bit) % 2
        kept = lax.dynamic_slice_in_dim(current, upper, 1, dim)
        sent = lax.dynamic_slice_in_dim(current, 1 - upper, 1, dim)
        count = fsdp_count if axis_name == "fsdp" else ctx_count
        pairs = [(device, device ^ bit) for device in range(count)]
        received = lax.ppermute(sent.astype(jnp.bfloat16), axis_name, pairs)
        current = kept.astype(jnp.float32) + received.astype(jnp.float32)
    return current.reshape(rows, -1)


def shard_gather(local):
    fsdp_count = lax.axis_size("fsdp")
    ctx_count = lax.axis_size("ctx")
    fsdp_bits = []
    step = 1
    while step < fsdp_count:
        fsdp_bits.append(step)
        step *= 2
    current = local.reshape((1,) * (len(fsdp_bits) + 1) + local.shape)
    order = [("ctx", 1)] + [("fsdp", bit) for bit in fsdp_bits[2:]] + [("fsdp", 1), ("fsdp", 2)]
    for axis_name, bit in order:
        if axis_name == "fsdp":
            dim = len(fsdp_bits) - 1 - fsdp_bits.index(bit)
        else:
            dim = len(fsdp_bits)
        count = fsdp_count if axis_name == "fsdp" else ctx_count
        pairs = [(device, device ^ bit) for device in range(count)]
        received = lax.ppermute(current, axis_name, pairs)
        upper = (lax.axis_index(axis_name) // bit) % 2
        current = jnp.where(
            upper == 0,
            jnp.concatenate([current, received], axis=dim),
            jnp.concatenate([received, current], axis=dim),
        )
    return current.reshape(-1, local.shape[1])


def per_device(
    tokens,
    cotangent,
    segments,
    attention_norm_weight,
    query_gain,
    key_gain,
    feedforward_gain,
    query_weight,
    key_projection_matrix,
    value_projection_matrix,
    output_weight,
    gate_weight,
    up_weight,
    down_weight,
):
    row_count = tokens.shape[0]
    model_width = tokens.shape[1]
    head_size = query_gain.shape[1]
    local_heads = query_weight.shape[2] // head_size
    local_groups = key_projection_matrix.shape[2] // head_size
    per_group = local_heads // local_groups
    layer_count = query_weight.shape[0]
    seq_length = segments.shape[1]
    row_start = lax.axis_index("ctx") * row_count
    column_width = model_width // lax.axis_size("tp")
    column_start = lax.axis_index("tp") * column_width
    score_scale = head_size ** (-0.5)
    positions = row_start + jnp.arange(row_count, dtype=jnp.int32)
    segment_row = segments[0]
    query_ids = lax.dynamic_slice_in_dim(segment_row, row_start, row_count)
    key_positions = jnp.arange(seq_length, dtype=jnp.int32)
    allowed = (query_ids[:, None] == segment_row[None, :]) & (
        key_positions[None, :] <= positions[:, None]
    )
    cosine_table, sine_table = rotary_tables(positions, head_size)

    def column_share(grad_rows, normalized):
        gradient_portion = lax.dynamic_slice_in_dim(grad_rows, column_start, column_width, 1)
        unit_slice = lax.dynamic_slice_in_dim(normalized, column_start, column_width, 1)
        part_sum = jnp.sum(gradient_portion * unit_slice, axis=0)
        return lax.dynamic_update_slice_in_dim(
            jnp.zeros((model_width,), jnp.float32), part_sum, column_start, 0
        )

    def attention_scores(query_groups, key_groups):
        return (
            jnp.einsum(
                "qgrd,kgd->grqk", query_groups, key_groups, preferred_element_type=jnp.float32
            )
            * score_scale
        )

    weight_shards = (
        query_weight,
        key_projection_matrix,
        value_projection_matrix,
        output_weight,
        gate_weight,
        up_weight,
        down_weight,
    )
    widths = [member.shape[2] for member in weight_shards]
    edges = [0]
    for width in widths:
        edges.append(edges[-1] + width)

    def gather_layer(layer_index):
        if layer_index > 0:
            joined = jnp.concatenate([member[layer_index] for member in weight_shards], axis=1)
            full = lax.all_gather(joined, ("fsdp", "ctx"), axis=0, tiled=True)
            return tuple(full[:, edges[k] : edges[k + 1]] for k in range(len(widths)))
        early = jnp.concatenate([member[layer_index] for member in weight_shards[:3]], axis=1)
        early_full = shard_gather(early)
        late = jnp.concatenate([member[layer_index] for member in weight_shards[3:]], axis=1)
        late_full = lax.all_gather(late, ("fsdp", "ctx"), axis=0, tiled=True)
        pieces = []
        for k in range(len(widths)):
            if k < 3:
                pieces.append(early_full[:, edges[k] : edges[k + 1]])
            else:
                pieces.append(late_full[:, edges[k] - edges[3] : edges[k + 1] - edges[3]])
        return tuple(pieces)

    def scatter_terms(terms):
        joined = jnp.concatenate([term.astype(jnp.bfloat16) for term in terms], axis=1)
        owned = lax.psum_scatter(joined, ("fsdp", "ctx"), scatter_dimension=0, tiled=True)
        pieces = []
        start = 0
        for term in terms:
            pieces.append(owned[:, start : start + term.shape[1]].astype(jnp.float32))
            start += term.shape[1]
        return pieces

    def scatter_chain(layer_terms):
        results = [None] * len(layer_terms)
        pending = []
        for layer_index in reversed(range(len(layer_terms))):
            terms = layer_terms[layer_index]
            owned = scatter_terms(pending + list(terms[3:]))
            if pending:
                results[layer_index + 1] = tuple(owned[:3]) + results[layer_index + 1]
            results[layer_index] = tuple(owned[len(pending) :])
            pending = list(terms[:3])
        joined = shard_scatter(
            jnp.concatenate([term.astype(jnp.bfloat16) for term in pending], axis=1)
        )
        late = []
        start = 0
        for term in pending:
            late.append(joined[:, start : start + term.shape[1]])
            start += term.shape[1]
        results[0] = tuple(late) + results[0]
        return results

    def scatter_layer(terms, layer_index):
        if layer_index > 0:
            return tuple(scatter_terms(terms))
        early = scatter_terms(terms[3:])
        joined = shard_scatter(
            jnp.concatenate([term.astype(jnp.bfloat16) for term in terms[:3]], axis=1)
        )
        late = []
        start = 0
        for term in terms[:3]:
            late.append(joined[:, start : start + term.shape[1]])
            start += term.shape[1]
        return tuple(late + early)

    kept_weights = []
    stored_layers = []
    hidden = tokens
    for layer_index in range(layer_count):
        gathered = gather_layer(layer_index)
        kept_weights.append(gathered)
        (
            forward_query_full,
            forward_key_full,
            forward_value_full,
            forward_output_full,
            forward_gate_full,
            forward_up_full,
            forward_down_full,
        ) = gathered
        forward_scale_one = row_scale(hidden)
        forward_normed = (hidden * forward_scale_one * attention_norm_weight[layer_index]).astype(
            jnp.bfloat16
        )
        query_raw = jnp.dot(
            forward_normed, forward_query_full, preferred_element_type=jnp.float32
        ).reshape(row_count, local_heads, head_size)
        key_raw = jnp.dot(
            forward_normed, forward_key_full, preferred_element_type=jnp.float32
        ).reshape(row_count, local_groups, head_size)
        values = jnp.dot(
            forward_normed, forward_value_full, preferred_element_type=jnp.float32
        ).astype(jnp.bfloat16)
        forward_query_scale = row_scale(query_raw)
        forward_query_unit = query_raw * forward_query_scale
        forward_key_scale = row_scale(key_raw)
        forward_key_unit = key_raw * forward_key_scale
        queries = rotate(
            forward_query_unit * query_gain[layer_index], cosine_table, sine_table
        ).astype(jnp.bfloat16)
        keys = rotate(forward_key_unit * key_gain[layer_index], cosine_table, sine_table).astype(
            jnp.bfloat16
        )
        keys = keys.reshape(row_count, local_groups * head_size)
        all_keys = ctx_gather(keys)
        all_values = ctx_gather(values)
        forward_query_groups = queries.reshape(row_count, local_groups, per_group, head_size)
        forward_key_groups = all_keys.reshape(seq_length, local_groups, head_size)
        forward_value_groups = all_values.reshape(seq_length, local_groups, head_size)
        forward_scores = attention_scores(forward_query_groups, forward_key_groups)
        exponent = jnp.where(allowed, jnp.exp(forward_scores), 0.0)
        forward_log_total = jnp.log(jnp.sum(exponent, axis=-1, keepdims=True))
        attention_probs = jnp.where(
            allowed, jnp.exp(forward_scores - forward_log_total), 0.0
        ).astype(jnp.bfloat16)
        forward_attended = jnp.einsum(
            "grqk,kgd->qgrd",
            attention_probs,
            forward_value_groups,
            preferred_element_type=jnp.float32,
        )
        forward_attended = forward_attended.astype(jnp.bfloat16).reshape(
            row_count, local_heads * head_size
        )
        forward_middle = hidden + tp_sum(contract_last(forward_attended, forward_output_full))
        forward_scale_two = row_scale(forward_middle)
        forward_feed_normed = (
            forward_middle * forward_scale_two * feedforward_gain[layer_index]
        ).astype(jnp.bfloat16)
        forward_gate_linear = jnp.dot(
            forward_feed_normed, forward_gate_full, preferred_element_type=jnp.float32
        )
        forward_up_linear = jnp.dot(
            forward_feed_normed, forward_up_full, preferred_element_type=jnp.float32
        )
        forward_activated = (jax.nn.silu(forward_gate_linear) * forward_up_linear).astype(
            jnp.bfloat16
        )
        result = forward_middle + tp_sum(contract_last(forward_activated, forward_down_full))
        forward_stored = (
            hidden,
            forward_scale_one,
            forward_normed,
            forward_query_unit,
            forward_query_scale,
            forward_key_unit,
            forward_key_scale,
            forward_query_groups,
            forward_key_groups,
            forward_value_groups,
            forward_log_total,
            forward_attended,
            forward_middle,
            forward_scale_two,
            forward_feed_normed,
            forward_gate_linear,
            forward_up_linear,
            forward_activated,
        )
        hidden = result
        stored_layers.append(forward_stored)
    grad_flow = cotangent
    weight_sums = [None] * layer_count
    gain_parts = [None] * layer_count
    for layer_index in reversed(range(layer_count)):
        gathered = kept_weights[layer_index]
        backward_stored = stored_layers[layer_index]
        query_full, key_full, value_full, output_full, gate_full, up_full, down_full = gathered
        (
            source,
            scale_one,
            normed,
            query_unit,
            query_scale,
            key_unit,
            key_scale,
            backward_query_groups,
            backward_key_groups,
            value_groups,
            log_total,
            attended,
            middle,
            scale_two,
            feed_normed,
            gate_linear,
            up_linear,
            activated,
        ) = backward_stored
        grad_half = grad_flow.astype(jnp.bfloat16)
        down_grad = contract_first(grad_half, activated)
        act_grad = jnp.dot(grad_half, down_full, preferred_element_type=jnp.float32)
        sigmoid_gate = jax.nn.sigmoid(gate_linear)
        gate_grad = (
            act_grad * up_linear * sigmoid_gate * (1.0 + gate_linear * (1.0 - sigmoid_gate))
        ).astype(jnp.bfloat16)
        up_grad = (act_grad * jax.nn.silu(gate_linear)).astype(jnp.bfloat16)
        gate_weight_grad = contract_first(feed_normed, gate_grad)
        up_weight_grad = contract_first(feed_normed, up_grad)
        feed_part = contract_last(gate_grad, gate_full) + contract_last(up_grad, up_full)
        feed_grad = tp_sum(feed_part)
        feed_unit = middle * scale_two
        feed_gain_grad = column_share(feed_grad, feed_unit)
        middle_grad = grad_flow + norm_back(
            feed_grad, feed_unit, scale_two, feedforward_gain[layer_index]
        )
        middle_half = middle_grad.astype(jnp.bfloat16)
        output_weight_grad = contract_first(middle_half, attended)
        attended_grad = jnp.dot(
            middle_half, output_full, preferred_element_type=jnp.float32
        ).astype(jnp.bfloat16)
        attended_grad = attended_grad.reshape(row_count, local_groups, per_group, head_size)
        scores = attention_scores(backward_query_groups, backward_key_groups)
        exact = jnp.where(allowed, jnp.exp(scores - log_total), 0.0)
        half_probs = exact.astype(jnp.bfloat16)
        value_grad = jnp.einsum(
            "grqk,qgrd->kgd", half_probs, attended_grad, preferred_element_type=jnp.float32
        )
        prob_grad = jnp.einsum(
            "qgrd,kgd->grqk", attended_grad, value_groups, preferred_element_type=jnp.float32
        )
        row_delta = jnp.sum(exact * prob_grad, axis=-1, keepdims=True)
        score_grad = (exact * (prob_grad - row_delta) * score_scale).astype(jnp.bfloat16)
        query_grad = jnp.einsum(
            "grqk,kgd->qgrd", score_grad, backward_key_groups, preferred_element_type=jnp.float32
        )
        query_grad = query_grad.reshape(row_count, local_heads, head_size)
        key_grad = jnp.einsum(
            "grqk,qgrd->kgd", score_grad, backward_query_groups, preferred_element_type=jnp.float32
        )
        key_own = ctx_scatter(key_grad.reshape(seq_length, local_groups * head_size))
        value_own = ctx_scatter(value_grad.reshape(seq_length, local_groups * head_size)).astype(
            jnp.bfloat16
        )
        query_turned = rotate(query_grad, cosine_table, -sine_table)
        key_turned = rotate(
            key_own.reshape(row_count, local_groups, head_size), cosine_table, -sine_table
        )
        query_gain_grad = jnp.sum(query_turned * query_unit, axis=(0, 1))
        key_gain_grad = jnp.sum(key_turned * key_unit, axis=(0, 1))
        query_pre = norm_back(
            query_turned, query_unit, query_scale, query_gain[layer_index]
        ).astype(jnp.bfloat16)
        query_pre = query_pre.reshape(row_count, local_heads * head_size)
        key_pre = norm_back(key_turned, key_unit, key_scale, key_gain[layer_index]).astype(
            jnp.bfloat16
        )
        key_pre = key_pre.reshape(row_count, local_groups * head_size)
        query_weight_grad = contract_first(normed, query_pre)
        key_weight_grad = contract_first(normed, key_pre)
        value_weight_grad = contract_first(normed, value_own)
        attention_part = (
            contract_last(query_pre, query_full)
            + contract_last(key_pre, key_full)
            + contract_last(value_own, value_full)
        )
        normed_grad = tp_sum(attention_part)
        source_unit = source * scale_one
        attention_gain_grad = column_share(normed_grad, source_unit)
        source_grad = middle_grad + norm_back(
            normed_grad, source_unit, scale_one, attention_norm_weight[layer_index]
        )
        weight_terms = (
            query_weight_grad,
            key_weight_grad,
            value_weight_grad,
            output_weight_grad,
            gate_weight_grad,
            up_weight_grad,
            down_grad,
        )
        gain_terms = (attention_gain_grad, query_gain_grad, key_gain_grad, feed_gain_grad)
        grad_flow, weight_terms, gain_terms = (source_grad, weight_terms, gain_terms)
        grad_query, grad_key, grad_value, grad_output, grad_gate, grad_up, grad_down = weight_terms
        weight_sums[layer_index] = weight_terms
        gain_parts[layer_index] = gain_terms
    weight_sums = scatter_chain(weight_sums)
    gain_stacks = [
        jnp.stack([member[which] for member in gain_parts]) for which in range(4)
    ]
    gain_edges = [0]
    for member in gain_stacks:
        gain_edges.append(gain_edges[-1] + member.shape[1])
    gain_joined = all_sum(jnp.concatenate(gain_stacks, axis=1))
    gain_totals = [
        gain_joined[:, gain_edges[which] : gain_edges[which + 1]] for which in range(4)
    ]
    stacked = [jnp.stack([member[which] for member in weight_sums]) for which in range(7)]
    return (
        hidden,
        grad_flow,
        gain_totals[0],
        gain_totals[1],
        gain_totals[2],
        gain_totals[3],
        stacked[0],
        stacked[1],
        stacked[2],
        stacked[3],
        stacked[4],
        stacked[5],
        stacked[6],
    )


def solution(mesh):
    in_specs = (
        P(("fsdp", "ctx"), None),
        P(("fsdp", "ctx"), None),
        P("fsdp", None),
        P(),
        P(),
        P(),
        P(),
        P(None, ("fsdp", "ctx"), "tp"),
        P(None, ("fsdp", "ctx"), "tp"),
        P(None, ("fsdp", "ctx"), "tp"),
        P(None, ("fsdp", "ctx"), "tp"),
        P(None, ("fsdp", "ctx"), "tp"),
        P(None, ("fsdp", "ctx"), "tp"),
        P(None, ("fsdp", "ctx"), "tp"),
    )
    out_specs = (
        P(("fsdp", "ctx"), None),
        P(("fsdp", "ctx"), None),
        P(),
        P(),
        P(),
        P(),
        P(None, ("fsdp", "ctx"), "tp"),
        P(None, ("fsdp", "ctx"), "tp"),
        P(None, ("fsdp", "ctx"), "tp"),
        P(None, ("fsdp", "ctx"), "tp"),
        P(None, ("fsdp", "ctx"), "tp"),
        P(None, ("fsdp", "ctx"), "tp"),
        P(None, ("fsdp", "ctx"), "tp"),
    )
    return jax.shard_map(
        per_device, mesh=mesh, in_specs=in_specs, out_specs=out_specs, check_vma=False
    )
```

```python
import jax
import jax.numpy as jnp
from jax import lax
from jax.sharding import PartitionSpec as P

eps = 1e-06
rope_base = 1000000.0


def contract_last(left_side, right_side):
    return lax.dot_general(
        left_side, right_side, (((1,), (1,)), ((), ())), preferred_element_type=jnp.float32
    )


def contract_first(left_side, right_side):
    return lax.dot_general(
        left_side, right_side, (((0,), (0,)), ((), ())), preferred_element_type=jnp.float32
    )


def row_scale(source):
    return lax.rsqrt(jnp.mean(source * source, axis=-1, keepdims=True) + eps)


def norm_back(grad_out, normalized, scaling, norm_gain):
    weighted = grad_out * norm_gain
    return scaling * (
        weighted - normalized * jnp.mean(weighted * normalized, axis=-1, keepdims=True)
    )


def rotary_tables(positions, head_size):
    halfway = head_size // 2
    frequency = rope_base ** (-2.0 * jnp.arange(halfway, dtype=jnp.float32) / head_size)
    angles = positions.astype(jnp.float32)[:, None] * frequency[None, :]
    return (jnp.cos(angles)[:, None, :], jnp.sin(angles)[:, None, :])


def rotate(source, cosine_table, sine_table):
    halfway = source.shape[-1] // 2
    leading = source[..., :halfway]
    trailing = source[..., halfway:]
    return jnp.concatenate(
        [
            leading * cosine_table - trailing * sine_table,
            trailing * cosine_table + leading * sine_table,
        ],
        axis=-1,
    )


def tp_sum(term):
    tp_count = lax.axis_size("tp")
    tp_index = lax.axis_index("tp")
    current = term.astype(jnp.bfloat16)
    half = current.shape[0] // 2
    upper = tp_index % 2
    core_pairs = [(device, device ^ 1) for device in range(tp_count)]
    kept = lax.dynamic_slice_in_dim(current, upper * half, half, 0)
    sent = lax.dynamic_slice_in_dim(current, (1 - upper) * half, half, 0)
    received = lax.ppermute(sent, "tp", core_pairs)
    total = kept.astype(jnp.float32) + received.astype(jnp.float32)
    step = 2
    while step < tp_count:
        mine = total.astype(jnp.bfloat16)
        pairs = [(device, device ^ step) for device in range(tp_count)]
        received = lax.ppermute(mine, "tp", pairs)
        total = mine.astype(jnp.float32) + received.astype(jnp.float32)
        step *= 2
    mine = total.astype(jnp.bfloat16)
    other = lax.ppermute(mine, "tp", core_pairs)
    joined = jnp.where(
        upper == 0,
        jnp.concatenate([mine, other], axis=0),
        jnp.concatenate([other, mine], axis=0),
    )
    return joined.astype(jnp.float32)


def swap_halves(local, axis_name):
    return lax.ppermute(local, axis_name, [(0, 1), (1, 0)])


def ctx_gather(local):
    other = swap_halves(local, "ctx")
    first = lax.axis_index("ctx") == 0
    return jnp.where(
        first, jnp.concatenate([local, other], axis=0), jnp.concatenate([other, local], axis=0)
    )


def ctx_scatter(full):
    rows = full.shape[0] // 2
    place = lax.axis_index("ctx")
    kept = lax.dynamic_slice_in_dim(full, place * rows, rows, 0)
    sent = lax.dynamic_slice_in_dim(full, (1 - place) * rows, rows, 0)
    received = swap_halves(sent.astype(jnp.bfloat16), "ctx")
    return kept.astype(jnp.bfloat16).astype(jnp.float32) + received.astype(jnp.float32)


def all_sum(value):
    total = value
    for axis_name in ("tp", "ctx", "fsdp"):
        count = lax.axis_size(axis_name)
        step = 1
        while step < count:
            pairs = [(device, device ^ step) for device in range(count)]
            total = total + lax.ppermute(total, axis_name, pairs)
            step *= 2
    return total


def shard_scatter(full):
    fsdp_count = lax.axis_size("fsdp")
    ctx_count = lax.axis_size("ctx")
    fsdp_bits = []
    step = 1
    while step < fsdp_count:
        fsdp_bits.append(step)
        step *= 2
    rows = full.shape[0] // (fsdp_count * ctx_count)
    current = full.astype(jnp.bfloat16).reshape((2,) * len(fsdp_bits) + (ctx_count, rows, -1))
    order = [("fsdp", 1), ("fsdp", 2), ("ctx", 1)] + [("fsdp", bit) for bit in fsdp_bits[2:]]
    for axis_name, bit in order:
        if axis_name == "fsdp":
            dim = len(fsdp_bits) - 1 - fsdp_bits.index(bit)
        else:
            dim = len(fsdp_bits)
        upper = (lax.axis_index(axis_name) // bit) % 2
        kept = lax.dynamic_slice_in_dim(current, upper, 1, dim)
        sent = lax.dynamic_slice_in_dim(current, 1 - upper, 1, dim)
        count = fsdp_count if axis_name == "fsdp" else ctx_count
        pairs = [(device, device ^ bit) for device in range(count)]
        received = lax.ppermute(sent.astype(jnp.bfloat16), axis_name, pairs)
        current = kept.astype(jnp.float32) + received.astype(jnp.float32)
    return current.reshape(rows, -1)


def shard_gather(local):
    fsdp_count = lax.axis_size("fsdp")
    ctx_count = lax.axis_size("ctx")
    fsdp_bits = []
    step = 1
    while step < fsdp_count:
        fsdp_bits.append(step)
        step *= 2
    current = local.reshape((1,) * (len(fsdp_bits) + 1) + local.shape)
    order = [("ctx", 1)] + [("fsdp", bit) for bit in fsdp_bits[2:]] + [("fsdp", 1), ("fsdp", 2)]
    for axis_name, bit in order:
        if axis_name == "fsdp":
            dim = len(fsdp_bits) - 1 - fsdp_bits.index(bit)
        else:
            dim = len(fsdp_bits)
        count = fsdp_count if axis_name == "fsdp" else ctx_count
        pairs = [(device, device ^ bit) for device in range(count)]
        received = lax.ppermute(current, axis_name, pairs)
        upper = (lax.axis_index(axis_name) // bit) % 2
        current = jnp.where(
            upper == 0,
            jnp.concatenate([current, received], axis=dim),
            jnp.concatenate([received, current], axis=dim),
        )
    return current.reshape(-1, local.shape[1])


def per_device(
    tokens,
    cotangent,
    segments,
    attention_norm_weight,
    query_gain,
    key_gain,
    feedforward_gain,
    query_weight,
    key_projection_matrix,
    value_projection_matrix,
    output_weight,
    gate_weight,
    up_weight,
    down_weight,
):
    row_count = tokens.shape[0]
    model_width = tokens.shape[1]
    head_size = query_gain.shape[1]
    local_heads = query_weight.shape[2] // head_size
    local_groups = key_projection_matrix.shape[2] // head_size
    per_group = local_heads // local_groups
    layer_count = query_weight.shape[0]
    seq_length = segments.shape[1]
    row_start = lax.axis_index("ctx") * row_count
    column_width = model_width // lax.axis_size("tp")
    column_start = lax.axis_index("tp") * column_width
    score_scale = head_size ** (-0.5)
    positions = row_start + jnp.arange(row_count, dtype=jnp.int32)
    segment_row = segments[0]
    query_ids = lax.dynamic_slice_in_dim(segment_row, row_start, row_count)
    key_positions = jnp.arange(seq_length, dtype=jnp.int32)
    allowed = (query_ids[:, None] == segment_row[None, :]) & (
        key_positions[None, :] <= positions[:, None]
    )
    cosine_table, sine_table = rotary_tables(positions, head_size)

    def column_share(grad_rows, normalized):
        gradient_portion = lax.dynamic_slice_in_dim(grad_rows, column_start, column_width, 1)
        unit_slice = lax.dynamic_slice_in_dim(normalized, column_start, column_width, 1)
        part_sum = jnp.sum(gradient_portion * unit_slice, axis=0)
        return lax.dynamic_update_slice_in_dim(
            jnp.zeros((model_width,), jnp.float32), part_sum, column_start, 0
        )

    def attention_scores(query_groups, key_groups):
        return (
            jnp.einsum(
                "qgrd,kgd->grqk", query_groups, key_groups, preferred_element_type=jnp.float32
            )
            * score_scale
        )

    weight_shards = (
        query_weight,
        key_projection_matrix,
        value_projection_matrix,
        output_weight,
        gate_weight,
        up_weight,
        down_weight,
    )
    widths = [member.shape[2] for member in weight_shards]
    edges = [0]
    for width in widths:
        edges.append(edges[-1] + width)

    early_width = edges[3]
    early_all = shard_gather(
        jnp.concatenate(
            [member[layer_index] for layer_index in range(query_weight.shape[0])
             for member in weight_shards[:3]],
            axis=1,
        )
    )

    def gather_layer(layer_index):
        early_full = early_all[:, layer_index * early_width : (layer_index + 1) * early_width]
        late = jnp.concatenate([member[layer_index] for member in weight_shards[3:]], axis=1)
        late_full = lax.all_gather(late, ("fsdp", "ctx"), axis=0, tiled=True)
        pieces = []
        for k in range(len(widths)):
            if k < 3:
                pieces.append(early_full[:, edges[k] : edges[k + 1]])
            else:
                pieces.append(late_full[:, edges[k] - edges[3] : edges[k + 1] - edges[3]])
        return tuple(pieces)

    def scatter_terms(terms):
        joined = jnp.concatenate([term.astype(jnp.bfloat16) for term in terms], axis=1)
        owned = lax.psum_scatter(joined, ("fsdp", "ctx"), scatter_dimension=0, tiled=True)
        pieces = []
        start = 0
        for term in terms:
            pieces.append(owned[:, start : start + term.shape[1]].astype(jnp.float32))
            start += term.shape[1]
        return pieces

    def scatter_layer(terms, layer_index):
        if layer_index > 0:
            return tuple(scatter_terms(terms))
        early = scatter_terms(terms[3:])
        joined = shard_scatter(
            jnp.concatenate([term.astype(jnp.bfloat16) for term in terms[:3]], axis=1)
        )
        late = []
        start = 0
        for term in terms[:3]:
            late.append(joined[:, start : start + term.shape[1]])
            start += term.shape[1]
        return tuple(late + early)

    kept_weights = []
    stored_layers = []
    hidden = tokens
    for layer_index in range(layer_count):
        gathered = gather_layer(layer_index)
        kept_weights.append(gathered)
        (
            forward_query_full,
            forward_key_full,
            forward_value_full,
            forward_output_full,
            forward_gate_full,
            forward_up_full,
            forward_down_full,
        ) = gathered
        forward_scale_one = row_scale(hidden)
        forward_normed = (hidden * forward_scale_one * attention_norm_weight[layer_index]).astype(
            jnp.bfloat16
        )
        query_raw = jnp.dot(
            forward_normed, forward_query_full, preferred_element_type=jnp.float32
        ).reshape(row_count, local_heads, head_size)
        key_raw = jnp.dot(
            forward_normed, forward_key_full, preferred_element_type=jnp.float32
        ).reshape(row_count, local_groups, head_size)
        values = jnp.dot(
            forward_normed, forward_value_full, preferred_element_type=jnp.float32
        ).astype(jnp.bfloat16)
        forward_query_scale = row_scale(query_raw)
        forward_query_unit = query_raw * forward_query_scale
        forward_key_scale = row_scale(key_raw)
        forward_key_unit = key_raw * forward_key_scale
        queries = rotate(
            forward_query_unit * query_gain[layer_index], cosine_table, sine_table
        ).astype(jnp.bfloat16)
        keys = rotate(forward_key_unit * key_gain[layer_index], cosine_table, sine_table).astype(
            jnp.bfloat16
        )
        keys = keys.reshape(row_count, local_groups * head_size)
        all_keys = ctx_gather(keys)
        all_values = ctx_gather(values)
        forward_query_groups = queries.reshape(row_count, local_groups, per_group, head_size)
        forward_key_groups = all_keys.reshape(seq_length, local_groups, head_size)
        forward_value_groups = all_values.reshape(seq_length, local_groups, head_size)
        forward_scores = attention_scores(forward_query_groups, forward_key_groups)
        exponent = jnp.where(allowed, jnp.exp(forward_scores), 0.0)
        forward_log_total = jnp.log(jnp.sum(exponent, axis=-1, keepdims=True))
        attention_probs = jnp.where(
            allowed, jnp.exp(forward_scores - forward_log_total), 0.0
        ).astype(jnp.bfloat16)
        forward_attended = jnp.einsum(
            "grqk,kgd->qgrd",
            attention_probs,
            forward_value_groups,
            preferred_element_type=jnp.float32,
        )
        forward_attended = forward_attended.astype(jnp.bfloat16).reshape(
            row_count, local_heads * head_size
        )
        forward_middle = hidden + tp_sum(contract_last(forward_attended, forward_output_full))
        forward_scale_two = row_scale(forward_middle)
        forward_feed_normed = (
            forward_middle * forward_scale_two * feedforward_gain[layer_index]
        ).astype(jnp.bfloat16)
        forward_gate_linear = jnp.dot(
            forward_feed_normed, forward_gate_full, preferred_element_type=jnp.float32
        )
        forward_up_linear = jnp.dot(
            forward_feed_normed, forward_up_full, preferred_element_type=jnp.float32
        )
        forward_activated = (jax.nn.silu(forward_gate_linear) * forward_up_linear).astype(
            jnp.bfloat16
        )
        result = forward_middle + tp_sum(contract_last(forward_activated, forward_down_full))
        forward_stored = (
            hidden,
            forward_scale_one,
            forward_normed,
            forward_query_unit,
            forward_query_scale,
            forward_key_unit,
            forward_key_scale,
            forward_query_groups,
            forward_key_groups,
            forward_value_groups,
            forward_log_total,
            forward_attended,
            forward_middle,
            forward_scale_two,
            forward_feed_normed,
            forward_gate_linear,
            forward_up_linear,
            forward_activated,
        )
        hidden = result
        stored_layers.append(forward_stored)
    grad_flow = cotangent
    weight_sums = [None] * layer_count
    gain_parts = [None] * layer_count
    for layer_index in reversed(range(layer_count)):
        gathered = kept_weights[layer_index]
        backward_stored = stored_layers[layer_index]
        query_full, key_full, value_full, output_full, gate_full, up_full, down_full = gathered
        (
            source,
            scale_one,
            normed,
            query_unit,
            query_scale,
            key_unit,
            key_scale,
            backward_query_groups,
            backward_key_groups,
            value_groups,
            log_total,
            attended,
            middle,
            scale_two,
            feed_normed,
            gate_linear,
            up_linear,
            activated,
        ) = backward_stored
        grad_half = grad_flow.astype(jnp.bfloat16)
        down_grad = contract_first(grad_half, activated)
        act_grad = jnp.dot(grad_half, down_full, preferred_element_type=jnp.float32)
        sigmoid_gate = jax.nn.sigmoid(gate_linear)
        gate_grad = (
            act_grad * up_linear * sigmoid_gate * (1.0 + gate_linear * (1.0 - sigmoid_gate))
        ).astype(jnp.bfloat16)
        up_grad = (act_grad * jax.nn.silu(gate_linear)).astype(jnp.bfloat16)
        gate_weight_grad = contract_first(feed_normed, gate_grad)
        up_weight_grad = contract_first(feed_normed, up_grad)
        feed_part = contract_last(gate_grad, gate_full) + contract_last(up_grad, up_full)
        feed_grad = tp_sum(feed_part)
        feed_unit = middle * scale_two
        feed_gain_grad = column_share(feed_grad, feed_unit)
        middle_grad = grad_flow + norm_back(
            feed_grad, feed_unit, scale_two, feedforward_gain[layer_index]
        )
        middle_half = middle_grad.astype(jnp.bfloat16)
        output_weight_grad = contract_first(middle_half, attended)
        attended_grad = jnp.dot(
            middle_half, output_full, preferred_element_type=jnp.float32
        ).astype(jnp.bfloat16)
        attended_grad = attended_grad.reshape(row_count, local_groups, per_group, head_size)
        scores = attention_scores(backward_query_groups, backward_key_groups)
        exact = jnp.where(allowed, jnp.exp(scores - log_total), 0.0)
        half_probs = exact.astype(jnp.bfloat16)
        value_grad = jnp.einsum(
            "grqk,qgrd->kgd", half_probs, attended_grad, preferred_element_type=jnp.float32
        )
        prob_grad = jnp.einsum(
            "qgrd,kgd->grqk", attended_grad, value_groups, preferred_element_type=jnp.float32
        )
        row_delta = jnp.sum(exact * prob_grad, axis=-1, keepdims=True)
        score_grad = (exact * (prob_grad - row_delta) * score_scale).astype(jnp.bfloat16)
        query_grad = jnp.einsum(
            "grqk,kgd->qgrd", score_grad, backward_key_groups, preferred_element_type=jnp.float32
        )
        query_grad = query_grad.reshape(row_count, local_heads, head_size)
        key_grad = jnp.einsum(
            "grqk,qgrd->kgd", score_grad, backward_query_groups, preferred_element_type=jnp.float32
        )
        key_own = ctx_scatter(key_grad.reshape(seq_length, local_groups * head_size))
        value_own = ctx_scatter(value_grad.reshape(seq_length, local_groups * head_size)).astype(
            jnp.bfloat16
        )
        query_turned = rotate(query_grad, cosine_table, -sine_table)
        key_turned = rotate(
            key_own.reshape(row_count, local_groups, head_size), cosine_table, -sine_table
        )
        query_gain_grad = jnp.sum(query_turned * query_unit, axis=(0, 1))
        key_gain_grad = jnp.sum(key_turned * key_unit, axis=(0, 1))
        query_pre = norm_back(
            query_turned, query_unit, query_scale, query_gain[layer_index]
        ).astype(jnp.bfloat16)
        query_pre = query_pre.reshape(row_count, local_heads * head_size)
        key_pre = norm_back(key_turned, key_unit, key_scale, key_gain[layer_index]).astype(
            jnp.bfloat16
        )
        key_pre = key_pre.reshape(row_count, local_groups * head_size)
        query_weight_grad = contract_first(normed, query_pre)
        key_weight_grad = contract_first(normed, key_pre)
        value_weight_grad = contract_first(normed, value_own)
        attention_part = (
            contract_last(query_pre, query_full)
            + contract_last(key_pre, key_full)
            + contract_last(value_own, value_full)
        )
        normed_grad = tp_sum(attention_part)
        source_unit = source * scale_one
        attention_gain_grad = column_share(normed_grad, source_unit)
        source_grad = middle_grad + norm_back(
            normed_grad, source_unit, scale_one, attention_norm_weight[layer_index]
        )
        weight_terms = (
            query_weight_grad,
            key_weight_grad,
            value_weight_grad,
            output_weight_grad,
            gate_weight_grad,
            up_weight_grad,
            down_grad,
        )
        gain_terms = (attention_gain_grad, query_gain_grad, key_gain_grad, feed_gain_grad)
        grad_flow, weight_terms, gain_terms = (source_grad, weight_terms, gain_terms)
        grad_query, grad_key, grad_value, grad_output, grad_gate, grad_up, grad_down = weight_terms
        weight_sums[layer_index] = scatter_layer(weight_terms, layer_index)
        gain_parts[layer_index] = gain_terms
    gain_stacks = [
        jnp.stack([member[which] for member in gain_parts]) for which in range(4)
    ]
    gain_edges = [0]
    for member in gain_stacks:
        gain_edges.append(gain_edges[-1] + member.shape[1])
    gain_joined = all_sum(jnp.concatenate(gain_stacks, axis=1))
    gain_totals = [
        gain_joined[:, gain_edges[which] : gain_edges[which + 1]] for which in range(4)
    ]
    stacked = [jnp.stack([member[which] for member in weight_sums]) for which in range(7)]
    return (
        hidden,
        grad_flow,
        gain_totals[0],
        gain_totals[1],
        gain_totals[2],
        gain_totals[3],
        stacked[0],
        stacked[1],
        stacked[2],
        stacked[3],
        stacked[4],
        stacked[5],
        stacked[6],
    )


def solution(mesh):
    in_specs = (
        P(("fsdp", "ctx"), None),
        P(("fsdp", "ctx"), None),
        P("fsdp", None),
        P(),
        P(),
        P(),
        P(),
        P(None, ("fsdp", "ctx"), "tp"),
        P(None, ("fsdp", "ctx"), "tp"),
        P(None, ("fsdp", "ctx"), "tp"),
        P(None, ("fsdp", "ctx"), "tp"),
        P(None, ("fsdp", "ctx"), "tp"),
        P(None, ("fsdp", "ctx"), "tp"),
        P(None, ("fsdp", "ctx"), "tp"),
    )
    out_specs = (
        P(("fsdp", "ctx"), None),
        P(("fsdp", "ctx"), None),
        P(),
        P(),
        P(),
        P(),
        P(None, ("fsdp", "ctx"), "tp"),
        P(None, ("fsdp", "ctx"), "tp"),
        P(None, ("fsdp", "ctx"), "tp"),
        P(None, ("fsdp", "ctx"), "tp"),
        P(None, ("fsdp", "ctx"), "tp"),
        P(None, ("fsdp", "ctx"), "tp"),
        P(None, ("fsdp", "ctx"), "tp"),
    )
    return jax.shard_map(
        per_device, mesh=mesh, in_specs=in_specs, out_specs=out_specs, check_vma=False
    )
```

```python
import jax
import jax.numpy as jnp
from jax import lax
from jax.sharding import PartitionSpec as P

eps = 1e-06
rope_base = 1000000.0


def contract_last(left_side, right_side):
    return lax.dot_general(
        left_side, right_side, (((1,), (1,)), ((), ())), preferred_element_type=jnp.float32
    )


def contract_first(left_side, right_side):
    return lax.dot_general(
        left_side, right_side, (((0,), (0,)), ((), ())), preferred_element_type=jnp.float32
    )


def row_scale(source):
    return lax.rsqrt(jnp.mean(source * source, axis=-1, keepdims=True) + eps)


def norm_back(grad_out, normalized, scaling, norm_gain):
    weighted = grad_out * norm_gain
    return scaling * (
        weighted - normalized * jnp.mean(weighted * normalized, axis=-1, keepdims=True)
    )


def rotary_tables(positions, head_size):
    halfway = head_size // 2
    frequency = rope_base ** (-2.0 * jnp.arange(halfway, dtype=jnp.float32) / head_size)
    angles = positions.astype(jnp.float32)[:, None] * frequency[None, :]
    return (jnp.cos(angles)[:, None, :], jnp.sin(angles)[:, None, :])


def rotate(source, cosine_table, sine_table):
    halfway = source.shape[-1] // 2
    leading = source[..., :halfway]
    trailing = source[..., halfway:]
    return jnp.concatenate(
        [
            leading * cosine_table - trailing * sine_table,
            trailing * cosine_table + leading * sine_table,
        ],
        axis=-1,
    )


def tp_sum(term):
    tp_count = lax.axis_size("tp")
    tp_index = lax.axis_index("tp")
    current = term.astype(jnp.bfloat16)
    half = current.shape[0] // 2
    upper = tp_index % 2
    core_pairs = [(device, device ^ 1) for device in range(tp_count)]
    kept = lax.dynamic_slice_in_dim(current, upper * half, half, 0)
    sent = lax.dynamic_slice_in_dim(current, (1 - upper) * half, half, 0)
    received = lax.ppermute(sent, "tp", core_pairs)
    total = kept.astype(jnp.float32) + received.astype(jnp.float32)
    step = 2
    while step < tp_count:
        mine = total.astype(jnp.bfloat16)
        pairs = [(device, device ^ step) for device in range(tp_count)]
        received = lax.ppermute(mine, "tp", pairs)
        total = mine.astype(jnp.float32) + received.astype(jnp.float32)
        step *= 2
    mine = total.astype(jnp.bfloat16)
    other = lax.ppermute(mine, "tp", core_pairs)
    joined = jnp.where(
        upper == 0,
        jnp.concatenate([mine, other], axis=0),
        jnp.concatenate([other, mine], axis=0),
    )
    return joined.astype(jnp.float32)


def swap_halves(local, axis_name):
    return lax.ppermute(local, axis_name, [(0, 1), (1, 0)])


def ctx_gather(local):
    other = swap_halves(local, "ctx")
    first = lax.axis_index("ctx") == 0
    return jnp.where(
        first, jnp.concatenate([local, other], axis=0), jnp.concatenate([other, local], axis=0)
    )


def ctx_scatter(full):
    rows = full.shape[0] // 2
    place = lax.axis_index("ctx")
    kept = lax.dynamic_slice_in_dim(full, place * rows, rows, 0)
    sent = lax.dynamic_slice_in_dim(full, (1 - place) * rows, rows, 0)
    received = swap_halves(sent.astype(jnp.bfloat16), "ctx")
    return kept.astype(jnp.bfloat16).astype(jnp.float32) + received.astype(jnp.float32)


def all_sum(value):
    total = value
    for axis_name in ("tp", "ctx", "fsdp"):
        count = lax.axis_size(axis_name)
        step = 1
        while step < count:
            pairs = [(device, device ^ step) for device in range(count)]
            total = total + lax.ppermute(total, axis_name, pairs)
            step *= 2
    return total


def shard_scatter(full):
    fsdp_count = lax.axis_size("fsdp")
    ctx_count = lax.axis_size("ctx")
    fsdp_bits = []
    step = 1
    while step < fsdp_count:
        fsdp_bits.append(step)
        step *= 2
    rows = full.shape[0] // (fsdp_count * ctx_count)
    current = full.astype(jnp.bfloat16).reshape((2,) * len(fsdp_bits) + (ctx_count, rows, -1))
    order = [("fsdp", 1), ("fsdp", 2), ("ctx", 1)] + [("fsdp", bit) for bit in fsdp_bits[2:]]
    for axis_name, bit in order:
        if axis_name == "fsdp":
            dim = len(fsdp_bits) - 1 - fsdp_bits.index(bit)
        else:
            dim = len(fsdp_bits)
        upper = (lax.axis_index(axis_name) // bit) % 2
        kept = lax.dynamic_slice_in_dim(current, upper, 1, dim)
        sent = lax.dynamic_slice_in_dim(current, 1 - upper, 1, dim)
        count = fsdp_count if axis_name == "fsdp" else ctx_count
        pairs = [(device, device ^ bit) for device in range(count)]
        received = lax.ppermute(sent.astype(jnp.bfloat16), axis_name, pairs)
        current = kept.astype(jnp.float32) + received.astype(jnp.float32)
    return current.reshape(rows, -1)


def shard_gather(local):
    fsdp_count = lax.axis_size("fsdp")
    ctx_count = lax.axis_size("ctx")
    fsdp_bits = []
    step = 1
    while step < fsdp_count:
        fsdp_bits.append(step)
        step *= 2
    current = local.reshape((1,) * (len(fsdp_bits) + 1) + local.shape)
    order = [("ctx", 1)] + [("fsdp", bit) for bit in fsdp_bits[2:]] + [("fsdp", 1), ("fsdp", 2)]
    for axis_name, bit in order:
        if axis_name == "fsdp":
            dim = len(fsdp_bits) - 1 - fsdp_bits.index(bit)
        else:
            dim = len(fsdp_bits)
        count = fsdp_count if axis_name == "fsdp" else ctx_count
        pairs = [(device, device ^ bit) for device in range(count)]
        received = lax.ppermute(current, axis_name, pairs)
        upper = (lax.axis_index(axis_name) // bit) % 2
        current = jnp.where(
            upper == 0,
            jnp.concatenate([current, received], axis=dim),
            jnp.concatenate([received, current], axis=dim),
        )
    return current.reshape(-1, local.shape[1])


def per_device(
    tokens,
    cotangent,
    segments,
    attention_norm_weight,
    query_gain,
    key_gain,
    feedforward_gain,
    query_weight,
    key_projection_matrix,
    value_projection_matrix,
    output_weight,
    gate_weight,
    up_weight,
    down_weight,
):
    row_count = tokens.shape[0]
    model_width = tokens.shape[1]
    head_size = query_gain.shape[1]
    local_heads = query_weight.shape[2] // head_size
    local_groups = key_projection_matrix.shape[2] // head_size
    per_group = local_heads // local_groups
    layer_count = query_weight.shape[0]
    seq_length = segments.shape[1]
    row_start = lax.axis_index("ctx") * row_count
    column_width = model_width // lax.axis_size("tp")
    column_start = lax.axis_index("tp") * column_width
    score_scale = head_size ** (-0.5)
    positions = row_start + jnp.arange(row_count, dtype=jnp.int32)
    segment_row = segments[0]
    query_ids = lax.dynamic_slice_in_dim(segment_row, row_start, row_count)
    key_positions = jnp.arange(seq_length, dtype=jnp.int32)
    allowed = (query_ids[:, None] == segment_row[None, :]) & (
        key_positions[None, :] <= positions[:, None]
    )
    cosine_table, sine_table = rotary_tables(positions, head_size)

    def column_share(grad_rows, normalized):
        gradient_portion = lax.dynamic_slice_in_dim(grad_rows, column_start, column_width, 1)
        unit_slice = lax.dynamic_slice_in_dim(normalized, column_start, column_width, 1)
        part_sum = jnp.sum(gradient_portion * unit_slice, axis=0)
        return lax.dynamic_update_slice_in_dim(
            jnp.zeros((model_width,), jnp.float32), part_sum, column_start, 0
        )

    def attention_scores(query_groups, key_groups):
        return (
            jnp.einsum(
                "qgrd,kgd->grqk", query_groups, key_groups, preferred_element_type=jnp.float32
            )
            * score_scale
        )

    weight_shards = (
        query_weight,
        key_projection_matrix,
        value_projection_matrix,
        output_weight,
        gate_weight,
        up_weight,
        down_weight,
    )
    widths = [member.shape[2] for member in weight_shards]
    edges = [0]
    for width in widths:
        edges.append(edges[-1] + width)

    def gather_layer(layer_index):
        if layer_index > 0:
            joined = jnp.concatenate([member[layer_index] for member in weight_shards], axis=1)
            full = lax.all_gather(joined, ("fsdp", "ctx"), axis=0, tiled=True)
            return tuple(full[:, edges[k] : edges[k + 1]] for k in range(len(widths)))
        early = jnp.concatenate([member[layer_index] for member in weight_shards[:3]], axis=1)
        early_full = shard_gather(early)
        late = jnp.concatenate([member[layer_index] for member in weight_shards[3:]], axis=1)
        late_full = lax.all_gather(late, ("fsdp", "ctx"), axis=0, tiled=True)
        pieces = []
        for k in range(len(widths)):
            if k < 3:
                pieces.append(early_full[:, edges[k] : edges[k + 1]])
            else:
                pieces.append(late_full[:, edges[k] - edges[3] : edges[k + 1] - edges[3]])
        return tuple(pieces)

    def scatter_terms(terms):
        joined = jnp.concatenate([term.astype(jnp.bfloat16) for term in terms], axis=1)
        owned = lax.psum_scatter(joined, ("fsdp", "ctx"), scatter_dimension=0, tiled=True)
        pieces = []
        start = 0
        for term in terms:
            pieces.append(owned[:, start : start + term.shape[1]].astype(jnp.float32))
            start += term.shape[1]
        return pieces

    def scatter_layer(terms, layer_index):
        if layer_index > 0:
            return tuple(scatter_terms(terms))
        early = scatter_terms(terms[4:])
        joined = shard_scatter(
            jnp.concatenate([term.astype(jnp.bfloat16) for term in terms[:4]], axis=1)
        )
        late = []
        start = 0
        for term in terms[:4]:
            late.append(joined[:, start : start + term.shape[1]])
            start += term.shape[1]
        return tuple(late + early)

    kept_weights = []
    stored_layers = []
    hidden = tokens
    for layer_index in range(layer_count):
        gathered = gather_layer(layer_index)
        kept_weights.append(gathered)
        (
            forward_query_full,
            forward_key_full,
            forward_value_full,
            forward_output_full,
            forward_gate_full,
            forward_up_full,
            forward_down_full,
        ) = gathered
        forward_scale_one = row_scale(hidden)
        forward_normed = (hidden * forward_scale_one * attention_norm_weight[layer_index]).astype(
            jnp.bfloat16
        )
        query_raw = jnp.dot(
            forward_normed, forward_query_full, preferred_element_type=jnp.float32
        ).reshape(row_count, local_heads, head_size)
        key_raw = jnp.dot(
            forward_normed, forward_key_full, preferred_element_type=jnp.float32
        ).reshape(row_count, local_groups, head_size)
        values = jnp.dot(
            forward_normed, forward_value_full, preferred_element_type=jnp.float32
        ).astype(jnp.bfloat16)
        forward_query_scale = row_scale(query_raw)
        forward_query_unit = query_raw * forward_query_scale
        forward_key_scale = row_scale(key_raw)
        forward_key_unit = key_raw * forward_key_scale
        queries = rotate(
            forward_query_unit * query_gain[layer_index], cosine_table, sine_table
        ).astype(jnp.bfloat16)
        keys = rotate(forward_key_unit * key_gain[layer_index], cosine_table, sine_table).astype(
            jnp.bfloat16
        )
        keys = keys.reshape(row_count, local_groups * head_size)
        all_keys = ctx_gather(keys)
        all_values = ctx_gather(values)
        forward_query_groups = queries.reshape(row_count, local_groups, per_group, head_size)
        forward_key_groups = all_keys.reshape(seq_length, local_groups, head_size)
        forward_value_groups = all_values.reshape(seq_length, local_groups, head_size)
        forward_scores = attention_scores(forward_query_groups, forward_key_groups)
        exponent = jnp.where(allowed, jnp.exp(forward_scores), 0.0)
        forward_log_total = jnp.log(jnp.sum(exponent, axis=-1, keepdims=True))
        attention_probs = jnp.where(
            allowed, jnp.exp(forward_scores - forward_log_total), 0.0
        ).astype(jnp.bfloat16)
        forward_attended = jnp.einsum(
            "grqk,kgd->qgrd",
            attention_probs,
            forward_value_groups,
            preferred_element_type=jnp.float32,
        )
        forward_attended = forward_attended.astype(jnp.bfloat16).reshape(
            row_count, local_heads * head_size
        )
        forward_middle = hidden + tp_sum(contract_last(forward_attended, forward_output_full))
        forward_scale_two = row_scale(forward_middle)
        forward_feed_normed = (
            forward_middle * forward_scale_two * feedforward_gain[layer_index]
        ).astype(jnp.bfloat16)
        forward_gate_linear = jnp.dot(
            forward_feed_normed, forward_gate_full, preferred_element_type=jnp.float32
        )
        forward_up_linear = jnp.dot(
            forward_feed_normed, forward_up_full, preferred_element_type=jnp.float32
        )
        forward_activated = (jax.nn.silu(forward_gate_linear) * forward_up_linear).astype(
            jnp.bfloat16
        )
        result = forward_middle + tp_sum(contract_last(forward_activated, forward_down_full))
        forward_stored = (
            hidden,
            forward_scale_one,
            forward_normed,
            forward_query_unit,
            forward_query_scale,
            forward_key_unit,
            forward_key_scale,
            forward_query_groups,
            forward_key_groups,
            forward_value_groups,
            forward_log_total,
            forward_attended,
            forward_middle,
            forward_scale_two,
            forward_feed_normed,
            forward_gate_linear,
            forward_up_linear,
            forward_activated,
        )
        hidden = result
        stored_layers.append(forward_stored)
    grad_flow = cotangent
    weight_sums = [None] * layer_count
    gain_parts = [None] * layer_count
    for layer_index in reversed(range(layer_count)):
        gathered = kept_weights[layer_index]
        backward_stored = stored_layers[layer_index]
        query_full, key_full, value_full, output_full, gate_full, up_full, down_full = gathered
        (
            source,
            scale_one,
            normed,
            query_unit,
            query_scale,
            key_unit,
            key_scale,
            backward_query_groups,
            backward_key_groups,
            value_groups,
            log_total,
            attended,
            middle,
            scale_two,
            feed_normed,
            gate_linear,
            up_linear,
            activated,
        ) = backward_stored
        grad_half = grad_flow.astype(jnp.bfloat16)
        down_grad = contract_first(grad_half, activated)
        act_grad = jnp.dot(grad_half, down_full, preferred_element_type=jnp.float32)
        sigmoid_gate = jax.nn.sigmoid(gate_linear)
        gate_grad = (
            act_grad * up_linear * sigmoid_gate * (1.0 + gate_linear * (1.0 - sigmoid_gate))
        ).astype(jnp.bfloat16)
        up_grad = (act_grad * jax.nn.silu(gate_linear)).astype(jnp.bfloat16)
        gate_weight_grad = contract_first(feed_normed, gate_grad)
        up_weight_grad = contract_first(feed_normed, up_grad)
        feed_part = contract_last(gate_grad, gate_full) + contract_last(up_grad, up_full)
        feed_grad = tp_sum(feed_part)
        feed_unit = middle * scale_two
        feed_gain_grad = column_share(feed_grad, feed_unit)
        middle_grad = grad_flow + norm_back(
            feed_grad, feed_unit, scale_two, feedforward_gain[layer_index]
        )
        middle_half = middle_grad.astype(jnp.bfloat16)
        output_weight_grad = contract_first(middle_half, attended)
        attended_grad = jnp.dot(
            middle_half, output_full, preferred_element_type=jnp.float32
        ).astype(jnp.bfloat16)
        attended_grad = attended_grad.reshape(row_count, local_groups, per_group, head_size)
        scores = attention_scores(backward_query_groups, backward_key_groups)
        exact = jnp.where(allowed, jnp.exp(scores - log_total), 0.0)
        half_probs = exact.astype(jnp.bfloat16)
        value_grad = jnp.einsum(
            "grqk,qgrd->kgd", half_probs, attended_grad, preferred_element_type=jnp.float32
        )
        prob_grad = jnp.einsum(
            "qgrd,kgd->grqk", attended_grad, value_groups, preferred_element_type=jnp.float32
        )
        row_delta = jnp.sum(exact * prob_grad, axis=-1, keepdims=True)
        score_grad = (exact * (prob_grad - row_delta) * score_scale).astype(jnp.bfloat16)
        query_grad = jnp.einsum(
            "grqk,kgd->qgrd", score_grad, backward_key_groups, preferred_element_type=jnp.float32
        )
        query_grad = query_grad.reshape(row_count, local_heads, head_size)
        key_grad = jnp.einsum(
            "grqk,qgrd->kgd", score_grad, backward_query_groups, preferred_element_type=jnp.float32
        )
        key_own = ctx_scatter(key_grad.reshape(seq_length, local_groups * head_size))
        value_own = ctx_scatter(value_grad.reshape(seq_length, local_groups * head_size)).astype(
            jnp.bfloat16
        )
        query_turned = rotate(query_grad, cosine_table, -sine_table)
        key_turned = rotate(
            key_own.reshape(row_count, local_groups, head_size), cosine_table, -sine_table
        )
        query_gain_grad = jnp.sum(query_turned * query_unit, axis=(0, 1))
        key_gain_grad = jnp.sum(key_turned * key_unit, axis=(0, 1))
        query_pre = norm_back(
            query_turned, query_unit, query_scale, query_gain[layer_index]
        ).astype(jnp.bfloat16)
        query_pre = query_pre.reshape(row_count, local_heads * head_size)
        key_pre = norm_back(key_turned, key_unit, key_scale, key_gain[layer_index]).astype(
            jnp.bfloat16
        )
        key_pre = key_pre.reshape(row_count, local_groups * head_size)
        query_weight_grad = contract_first(normed, query_pre)
        key_weight_grad = contract_first(normed, key_pre)
        value_weight_grad = contract_first(normed, value_own)
        attention_part = (
            contract_last(query_pre, query_full)
            + contract_last(key_pre, key_full)
            + contract_last(value_own, value_full)
        )
        normed_grad = tp_sum(attention_part)
        source_unit = source * scale_one
        attention_gain_grad = column_share(normed_grad, source_unit)
        source_grad = middle_grad + norm_back(
            normed_grad, source_unit, scale_one, attention_norm_weight[layer_index]
        )
        weight_terms = (
            query_weight_grad,
            key_weight_grad,
            value_weight_grad,
            output_weight_grad,
            gate_weight_grad,
            up_weight_grad,
            down_grad,
        )
        gain_terms = (attention_gain_grad, query_gain_grad, key_gain_grad, feed_gain_grad)
        grad_flow, weight_terms, gain_terms = (source_grad, weight_terms, gain_terms)
        grad_query, grad_key, grad_value, grad_output, grad_gate, grad_up, grad_down = weight_terms
        weight_sums[layer_index] = scatter_layer(weight_terms, layer_index)
        gain_parts[layer_index] = gain_terms
    gain_stacks = [
        jnp.stack([member[which] for member in gain_parts]) for which in range(4)
    ]
    gain_edges = [0]
    for member in gain_stacks:
        gain_edges.append(gain_edges[-1] + member.shape[1])
    gain_joined = all_sum(jnp.concatenate(gain_stacks, axis=1))
    gain_totals = [
        gain_joined[:, gain_edges[which] : gain_edges[which + 1]] for which in range(4)
    ]
    stacked = [jnp.stack([member[which] for member in weight_sums]) for which in range(7)]
    return (
        hidden,
        grad_flow,
        gain_totals[0],
        gain_totals[1],
        gain_totals[2],
        gain_totals[3],
        stacked[0],
        stacked[1],
        stacked[2],
        stacked[3],
        stacked[4],
        stacked[5],
        stacked[6],
    )


def solution(mesh):
    in_specs = (
        P(("fsdp", "ctx"), None),
        P(("fsdp", "ctx"), None),
        P("fsdp", None),
        P(),
        P(),
        P(),
        P(),
        P(None, ("fsdp", "ctx"), "tp"),
        P(None, ("fsdp", "ctx"), "tp"),
        P(None, ("fsdp", "ctx"), "tp"),
        P(None, ("fsdp", "ctx"), "tp"),
        P(None, ("fsdp", "ctx"), "tp"),
        P(None, ("fsdp", "ctx"), "tp"),
        P(None, ("fsdp", "ctx"), "tp"),
    )
    out_specs = (
        P(("fsdp", "ctx"), None),
        P(("fsdp", "ctx"), None),
        P(),
        P(),
        P(),
        P(),
        P(None, ("fsdp", "ctx"), "tp"),
        P(None, ("fsdp", "ctx"), "tp"),
        P(None, ("fsdp", "ctx"), "tp"),
        P(None, ("fsdp", "ctx"), "tp"),
        P(None, ("fsdp", "ctx"), "tp"),
        P(None, ("fsdp", "ctx"), "tp"),
        P(None, ("fsdp", "ctx"), "tp"),
    )
    return jax.shard_map(
        per_device, mesh=mesh, in_specs=in_specs, out_specs=out_specs, check_vma=False
    )
```

```python
import jax
import jax.numpy as jnp
from jax import lax
from jax.sharding import PartitionSpec as P

eps = 1e-06
rope_base = 1000000.0


def contract_last(left_side, right_side):
    return lax.dot_general(
        left_side, right_side, (((1,), (1,)), ((), ())), preferred_element_type=jnp.float32
    )


def contract_first(left_side, right_side):
    return lax.dot_general(
        left_side, right_side, (((0,), (0,)), ((), ())), preferred_element_type=jnp.float32
    )


def row_scale(source):
    return lax.rsqrt(jnp.mean(source * source, axis=-1, keepdims=True) + eps)


def norm_back(grad_out, normalized, scaling, norm_gain):
    weighted = grad_out * norm_gain
    return scaling * (
        weighted - normalized * jnp.mean(weighted * normalized, axis=-1, keepdims=True)
    )


def rotary_tables(positions, head_size):
    halfway = head_size // 2
    frequency = rope_base ** (-2.0 * jnp.arange(halfway, dtype=jnp.float32) / head_size)
    angles = positions.astype(jnp.float32)[:, None] * frequency[None, :]
    return (jnp.cos(angles)[:, None, :], jnp.sin(angles)[:, None, :])


def rotate(source, cosine_table, sine_table):
    halfway = source.shape[-1] // 2
    leading = source[..., :halfway]
    trailing = source[..., halfway:]
    return jnp.concatenate(
        [
            leading * cosine_table - trailing * sine_table,
            trailing * cosine_table + leading * sine_table,
        ],
        axis=-1,
    )


def tp_sum(term):
    tp_count = lax.axis_size("tp")
    tp_index = lax.axis_index("tp")
    current = term.astype(jnp.bfloat16)
    half = current.shape[0] // 2
    upper = tp_index % 2
    core_pairs = [(device, device ^ 1) for device in range(tp_count)]
    kept = lax.dynamic_slice_in_dim(current, upper * half, half, 0)
    sent = lax.dynamic_slice_in_dim(current, (1 - upper) * half, half, 0)
    received = lax.ppermute(sent, "tp", core_pairs)
    total = kept.astype(jnp.float32) + received.astype(jnp.float32)
    step = 2
    while step < tp_count:
        mine = total.astype(jnp.bfloat16)
        pairs = [(device, device ^ step) for device in range(tp_count)]
        received = lax.ppermute(mine, "tp", pairs)
        total = mine.astype(jnp.float32) + received.astype(jnp.float32)
        step *= 2
    mine = total.astype(jnp.bfloat16)
    other = lax.ppermute(mine, "tp", core_pairs)
    joined = jnp.where(
        upper == 0,
        jnp.concatenate([mine, other], axis=0),
        jnp.concatenate([other, mine], axis=0),
    )
    return joined.astype(jnp.float32)


def swap_halves(local, axis_name):
    return lax.ppermute(local, axis_name, [(0, 1), (1, 0)])


def ctx_gather(local):
    other = swap_halves(local, "ctx")
    first = lax.axis_index("ctx") == 0
    return jnp.where(
        first, jnp.concatenate([local, other], axis=0), jnp.concatenate([other, local], axis=0)
    )


def ctx_scatter(full):
    rows = full.shape[0] // 2
    place = lax.axis_index("ctx")
    kept = lax.dynamic_slice_in_dim(full, place * rows, rows, 0)
    sent = lax.dynamic_slice_in_dim(full, (1 - place) * rows, rows, 0)
    received = swap_halves(sent.astype(jnp.bfloat16), "ctx")
    return kept.astype(jnp.bfloat16).astype(jnp.float32) + received.astype(jnp.float32)


def all_sum(value):
    total = value
    for axis_name in ("tp", "ctx", "fsdp"):
        count = lax.axis_size(axis_name)
        step = 1
        while step < count:
            pairs = [(device, device ^ step) for device in range(count)]
            total = total + lax.ppermute(total, axis_name, pairs)
            step *= 2
    return total


def shard_scatter(full):
    fsdp_count = lax.axis_size("fsdp")
    ctx_count = lax.axis_size("ctx")
    fsdp_bits = []
    step = 1
    while step < fsdp_count:
        fsdp_bits.append(step)
        step *= 2
    rows = full.shape[0] // (fsdp_count * ctx_count)
    current = full.astype(jnp.bfloat16).reshape((2,) * len(fsdp_bits) + (ctx_count, rows, -1))
    order = [("fsdp", 1), ("fsdp", 2), ("ctx", 1)] + [("fsdp", bit) for bit in fsdp_bits[2:]]
    for axis_name, bit in order:
        if axis_name == "fsdp":
            dim = len(fsdp_bits) - 1 - fsdp_bits.index(bit)
        else:
            dim = len(fsdp_bits)
        upper = (lax.axis_index(axis_name) // bit) % 2
        kept = lax.dynamic_slice_in_dim(current, upper, 1, dim)
        sent = lax.dynamic_slice_in_dim(current, 1 - upper, 1, dim)
        count = fsdp_count if axis_name == "fsdp" else ctx_count
        pairs = [(device, device ^ bit) for device in range(count)]
        received = lax.ppermute(sent.astype(jnp.bfloat16), axis_name, pairs)
        current = kept.astype(jnp.float32) + received.astype(jnp.float32)
    return current.reshape(rows, -1)


def shard_gather(local):
    fsdp_count = lax.axis_size("fsdp")
    ctx_count = lax.axis_size("ctx")
    fsdp_bits = []
    step = 1
    while step < fsdp_count:
        fsdp_bits.append(step)
        step *= 2
    current = local.reshape((1,) * (len(fsdp_bits) + 1) + local.shape)
    order = [("ctx", 1)] + [("fsdp", bit) for bit in fsdp_bits[2:]] + [("fsdp", 1), ("fsdp", 2)]
    for axis_name, bit in order:
        if axis_name == "fsdp":
            dim = len(fsdp_bits) - 1 - fsdp_bits.index(bit)
        else:
            dim = len(fsdp_bits)
        count = fsdp_count if axis_name == "fsdp" else ctx_count
        pairs = [(device, device ^ bit) for device in range(count)]
        received = lax.ppermute(current, axis_name, pairs)
        upper = (lax.axis_index(axis_name) // bit) % 2
        current = jnp.where(
            upper == 0,
            jnp.concatenate([current, received], axis=dim),
            jnp.concatenate([received, current], axis=dim),
        )
    return current.reshape(-1, local.shape[1])


def per_device(
    tokens,
    cotangent,
    segments,
    attention_norm_weight,
    query_gain,
    key_gain,
    feedforward_gain,
    query_weight,
    key_projection_matrix,
    value_projection_matrix,
    output_weight,
    gate_weight,
    up_weight,
    down_weight,
):
    row_count = tokens.shape[0]
    model_width = tokens.shape[1]
    head_size = query_gain.shape[1]
    local_heads = query_weight.shape[2] // head_size
    local_groups = key_projection_matrix.shape[2] // head_size
    per_group = local_heads // local_groups
    layer_count = query_weight.shape[0]
    seq_length = segments.shape[1]
    row_start = lax.axis_index("ctx") * row_count
    column_width = model_width // lax.axis_size("tp")
    column_start = lax.axis_index("tp") * column_width
    score_scale = head_size ** (-0.5)
    positions = row_start + jnp.arange(row_count, dtype=jnp.int32)
    segment_row = segments[0]
    query_ids = lax.dynamic_slice_in_dim(segment_row, row_start, row_count)
    key_positions = jnp.arange(seq_length, dtype=jnp.int32)
    allowed = (query_ids[:, None] == segment_row[None, :]) & (
        key_positions[None, :] <= positions[:, None]
    )
    cosine_table, sine_table = rotary_tables(positions, head_size)

    def column_share(grad_rows, normalized):
        gradient_portion = lax.dynamic_slice_in_dim(grad_rows, column_start, column_width, 1)
        unit_slice = lax.dynamic_slice_in_dim(normalized, column_start, column_width, 1)
        part_sum = jnp.sum(gradient_portion * unit_slice, axis=0)
        return lax.dynamic_update_slice_in_dim(
            jnp.zeros((model_width,), jnp.float32), part_sum, column_start, 0
        )

    def attention_scores(query_groups, key_groups):
        return (
            jnp.einsum(
                "qgrd,kgd->grqk", query_groups, key_groups, preferred_element_type=jnp.float32
            )
            * score_scale
        )

    weight_shards = (
        query_weight,
        key_projection_matrix,
        value_projection_matrix,
        output_weight,
        gate_weight,
        up_weight,
        down_weight,
    )
    widths = [member.shape[2] for member in weight_shards]
    edges = [0]
    for width in widths:
        edges.append(edges[-1] + width)

    def gather_layer(layer_index):
        if layer_index > 0:
            joined = jnp.concatenate([member[layer_index] for member in weight_shards], axis=1)
            full = lax.all_gather(joined, ("fsdp", "ctx"), axis=0, tiled=True)
            return tuple(full[:, edges[k] : edges[k + 1]] for k in range(len(widths)))
        early = jnp.concatenate([member[layer_index] for member in weight_shards[:3]], axis=1)
        early_full = shard_gather(early)
        late = jnp.concatenate([member[layer_index] for member in weight_shards[3:]], axis=1)
        late_full = lax.all_gather(late, ("fsdp", "ctx"), axis=0, tiled=True)
        pieces = []
        for k in range(len(widths)):
            if k < 3:
                pieces.append(early_full[:, edges[k] : edges[k + 1]])
            else:
                pieces.append(late_full[:, edges[k] - edges[3] : edges[k + 1] - edges[3]])
        return tuple(pieces)

    def scatter_terms(terms):
        joined = jnp.concatenate([term.astype(jnp.bfloat16) for term in terms], axis=1)
        owned = lax.psum_scatter(joined, ("fsdp", "ctx"), scatter_dimension=0, tiled=True)
        pieces = []
        start = 0
        for term in terms:
            pieces.append(owned[:, start : start + term.shape[1]].astype(jnp.float32))
            start += term.shape[1]
        return pieces

    def scatter_layer(terms, layer_index):
        if layer_index > 0:
            return tuple(scatter_terms(terms))
        early = scatter_terms(terms[4:6])
        joined = shard_scatter(
            jnp.concatenate([term.astype(jnp.bfloat16) for term in terms[:4] + terms[6:]], axis=1)
        )
        late = []
        start = 0
        for term in terms[:4] + terms[6:]:
            late.append(joined[:, start : start + term.shape[1]])
            start += term.shape[1]
        return tuple(late[:4] + early + late[4:])

    kept_weights = []
    stored_layers = []
    hidden = tokens
    for layer_index in range(layer_count):
        gathered = gather_layer(layer_index)
        kept_weights.append(gathered)
        (
            forward_query_full,
            forward_key_full,
            forward_value_full,
            forward_output_full,
            forward_gate_full,
            forward_up_full,
            forward_down_full,
        ) = gathered
        forward_scale_one = row_scale(hidden)
        forward_normed = (hidden * forward_scale_one * attention_norm_weight[layer_index]).astype(
            jnp.bfloat16
        )
        query_raw = jnp.dot(
            forward_normed, forward_query_full, preferred_element_type=jnp.float32
        ).reshape(row_count, local_heads, head_size)
        key_raw = jnp.dot(
            forward_normed, forward_key_full, preferred_element_type=jnp.float32
        ).reshape(row_count, local_groups, head_size)
        values = jnp.dot(
            forward_normed, forward_value_full, preferred_element_type=jnp.float32
        ).astype(jnp.bfloat16)
        forward_query_scale = row_scale(query_raw)
        forward_query_unit = query_raw * forward_query_scale
        forward_key_scale = row_scale(key_raw)
        forward_key_unit = key_raw * forward_key_scale
        queries = rotate(
            forward_query_unit * query_gain[layer_index], cosine_table, sine_table
        ).astype(jnp.bfloat16)
        keys = rotate(forward_key_unit * key_gain[layer_index], cosine_table, sine_table).astype(
            jnp.bfloat16
        )
        keys = keys.reshape(row_count, local_groups * head_size)
        all_keys = ctx_gather(keys)
        all_values = ctx_gather(values)
        forward_query_groups = queries.reshape(row_count, local_groups, per_group, head_size)
        forward_key_groups = all_keys.reshape(seq_length, local_groups, head_size)
        forward_value_groups = all_values.reshape(seq_length, local_groups, head_size)
        forward_scores = attention_scores(forward_query_groups, forward_key_groups)
        exponent = jnp.where(allowed, jnp.exp(forward_scores), 0.0)
        forward_log_total = jnp.log(jnp.sum(exponent, axis=-1, keepdims=True))
        attention_probs = jnp.where(
            allowed, jnp.exp(forward_scores - forward_log_total), 0.0
        ).astype(jnp.bfloat16)
        forward_attended = jnp.einsum(
            "grqk,kgd->qgrd",
            attention_probs,
            forward_value_groups,
            preferred_element_type=jnp.float32,
        )
        forward_attended = forward_attended.astype(jnp.bfloat16).reshape(
            row_count, local_heads * head_size
        )
        forward_middle = hidden + tp_sum(contract_last(forward_attended, forward_output_full))
        forward_scale_two = row_scale(forward_middle)
        forward_feed_normed = (
            forward_middle * forward_scale_two * feedforward_gain[layer_index]
        ).astype(jnp.bfloat16)
        forward_gate_linear = jnp.dot(
            forward_feed_normed, forward_gate_full, preferred_element_type=jnp.float32
        )
        forward_up_linear = jnp.dot(
            forward_feed_normed, forward_up_full, preferred_element_type=jnp.float32
        )
        forward_activated = (jax.nn.silu(forward_gate_linear) * forward_up_linear).astype(
            jnp.bfloat16
        )
        result = forward_middle + tp_sum(contract_last(forward_activated, forward_down_full))
        forward_stored = (
            hidden,
            forward_scale_one,
            forward_normed,
            forward_query_unit,
            forward_query_scale,
            forward_key_unit,
            forward_key_scale,
            forward_query_groups,
            forward_key_groups,
            forward_value_groups,
            forward_log_total,
            forward_attended,
            forward_middle,
            forward_scale_two,
            forward_feed_normed,
            forward_gate_linear,
            forward_up_linear,
            forward_activated,
        )
        hidden = result
        stored_layers.append(forward_stored)
    grad_flow = cotangent
    weight_sums = [None] * layer_count
    gain_parts = [None] * layer_count
    for layer_index in reversed(range(layer_count)):
        gathered = kept_weights[layer_index]
        backward_stored = stored_layers[layer_index]
        query_full, key_full, value_full, output_full, gate_full, up_full, down_full = gathered
        (
            source,
            scale_one,
            normed,
            query_unit,
            query_scale,
            key_unit,
            key_scale,
            backward_query_groups,
            backward_key_groups,
            value_groups,
            log_total,
            attended,
            middle,
            scale_two,
            feed_normed,
            gate_linear,
            up_linear,
            activated,
        ) = backward_stored
        grad_half = grad_flow.astype(jnp.bfloat16)
        down_grad = contract_first(grad_half, activated)
        act_grad = jnp.dot(grad_half, down_full, preferred_element_type=jnp.float32)
        sigmoid_gate = jax.nn.sigmoid(gate_linear)
        gate_grad = (
            act_grad * up_linear * sigmoid_gate * (1.0 + gate_linear * (1.0 - sigmoid_gate))
        ).astype(jnp.bfloat16)
        up_grad = (act_grad * jax.nn.silu(gate_linear)).astype(jnp.bfloat16)
        gate_weight_grad = contract_first(feed_normed, gate_grad)
        up_weight_grad = contract_first(feed_normed, up_grad)
        feed_part = contract_last(gate_grad, gate_full) + contract_last(up_grad, up_full)
        feed_grad = tp_sum(feed_part)
        feed_unit = middle * scale_two
        feed_gain_grad = column_share(feed_grad, feed_unit)
        middle_grad = grad_flow + norm_back(
            feed_grad, feed_unit, scale_two, feedforward_gain[layer_index]
        )
        middle_half = middle_grad.astype(jnp.bfloat16)
        output_weight_grad = contract_first(middle_half, attended)
        attended_grad = jnp.dot(
            middle_half, output_full, preferred_element_type=jnp.float32
        ).astype(jnp.bfloat16)
        attended_grad = attended_grad.reshape(row_count, local_groups, per_group, head_size)
        scores = attention_scores(backward_query_groups, backward_key_groups)
        exact = jnp.where(allowed, jnp.exp(scores - log_total), 0.0)
        half_probs = exact.astype(jnp.bfloat16)
        value_grad = jnp.einsum(
            "grqk,qgrd->kgd", half_probs, attended_grad, preferred_element_type=jnp.float32
        )
        prob_grad = jnp.einsum(
            "qgrd,kgd->grqk", attended_grad, value_groups, preferred_element_type=jnp.float32
        )
        row_delta = jnp.sum(exact * prob_grad, axis=-1, keepdims=True)
        score_grad = (exact * (prob_grad - row_delta) * score_scale).astype(jnp.bfloat16)
        query_grad = jnp.einsum(
            "grqk,kgd->qgrd", score_grad, backward_key_groups, preferred_element_type=jnp.float32
        )
        query_grad = query_grad.reshape(row_count, local_heads, head_size)
        key_grad = jnp.einsum(
            "grqk,qgrd->kgd", score_grad, backward_query_groups, preferred_element_type=jnp.float32
        )
        key_own = ctx_scatter(key_grad.reshape(seq_length, local_groups * head_size))
        value_own = ctx_scatter(value_grad.reshape(seq_length, local_groups * head_size)).astype(
            jnp.bfloat16
        )
        query_turned = rotate(query_grad, cosine_table, -sine_table)
        key_turned = rotate(
            key_own.reshape(row_count, local_groups, head_size), cosine_table, -sine_table
        )
        query_gain_grad = jnp.sum(query_turned * query_unit, axis=(0, 1))
        key_gain_grad = jnp.sum(key_turned * key_unit, axis=(0, 1))
        query_pre = norm_back(
            query_turned, query_unit, query_scale, query_gain[layer_index]
        ).astype(jnp.bfloat16)
        query_pre = query_pre.reshape(row_count, local_heads * head_size)
        key_pre = norm_back(key_turned, key_unit, key_scale, key_gain[layer_index]).astype(
            jnp.bfloat16
        )
        key_pre = key_pre.reshape(row_count, local_groups * head_size)
        query_weight_grad = contract_first(normed, query_pre)
        key_weight_grad = contract_first(normed, key_pre)
        value_weight_grad = contract_first(normed, value_own)
        attention_part = (
            contract_last(query_pre, query_full)
            + contract_last(key_pre, key_full)
            + contract_last(value_own, value_full)
        )
        normed_grad = tp_sum(attention_part)
        source_unit = source * scale_one
        attention_gain_grad = column_share(normed_grad, source_unit)
        source_grad = middle_grad + norm_back(
            normed_grad, source_unit, scale_one, attention_norm_weight[layer_index]
        )
        weight_terms = (
            query_weight_grad,
            key_weight_grad,
            value_weight_grad,
            output_weight_grad,
            gate_weight_grad,
            up_weight_grad,
            down_grad,
        )
        gain_terms = (attention_gain_grad, query_gain_grad, key_gain_grad, feed_gain_grad)
        grad_flow, weight_terms, gain_terms = (source_grad, weight_terms, gain_terms)
        grad_query, grad_key, grad_value, grad_output, grad_gate, grad_up, grad_down = weight_terms
        weight_sums[layer_index] = scatter_layer(weight_terms, layer_index)
        gain_parts[layer_index] = gain_terms
    gain_stacks = [
        jnp.stack([member[which] for member in gain_parts]) for which in range(4)
    ]
    gain_edges = [0]
    for member in gain_stacks:
        gain_edges.append(gain_edges[-1] + member.shape[1])
    gain_joined = all_sum(jnp.concatenate(gain_stacks, axis=1))
    gain_totals = [
        gain_joined[:, gain_edges[which] : gain_edges[which + 1]] for which in range(4)
    ]
    stacked = [jnp.stack([member[which] for member in weight_sums]) for which in range(7)]
    return (
        hidden,
        grad_flow,
        gain_totals[0],
        gain_totals[1],
        gain_totals[2],
        gain_totals[3],
        stacked[0],
        stacked[1],
        stacked[2],
        stacked[3],
        stacked[4],
        stacked[5],
        stacked[6],
    )


def solution(mesh):
    in_specs = (
        P(("fsdp", "ctx"), None),
        P(("fsdp", "ctx"), None),
        P("fsdp", None),
        P(),
        P(),
        P(),
        P(),
        P(None, ("fsdp", "ctx"), "tp"),
        P(None, ("fsdp", "ctx"), "tp"),
        P(None, ("fsdp", "ctx"), "tp"),
        P(None, ("fsdp", "ctx"), "tp"),
        P(None, ("fsdp", "ctx"), "tp"),
        P(None, ("fsdp", "ctx"), "tp"),
        P(None, ("fsdp", "ctx"), "tp"),
    )
    out_specs = (
        P(("fsdp", "ctx"), None),
        P(("fsdp", "ctx"), None),
        P(),
        P(),
        P(),
        P(),
        P(None, ("fsdp", "ctx"), "tp"),
        P(None, ("fsdp", "ctx"), "tp"),
        P(None, ("fsdp", "ctx"), "tp"),
        P(None, ("fsdp", "ctx"), "tp"),
        P(None, ("fsdp", "ctx"), "tp"),
        P(None, ("fsdp", "ctx"), "tp"),
        P(None, ("fsdp", "ctx"), "tp"),
    )
    return jax.shard_map(
        per_device, mesh=mesh, in_specs=in_specs, out_specs=out_specs, check_vma=False
    )
```

```python
import jax
import jax.numpy as jnp
from jax import lax
from jax.sharding import PartitionSpec as P

eps = 1e-06
rope_base = 1000000.0


def contract_last(left_side, right_side):
    return lax.dot_general(
        left_side, right_side, (((1,), (1,)), ((), ())), preferred_element_type=jnp.float32
    )


def contract_first(left_side, right_side):
    return lax.dot_general(
        left_side, right_side, (((0,), (0,)), ((), ())), preferred_element_type=jnp.float32
    )


def row_scale(source):
    return lax.rsqrt(jnp.mean(source * source, axis=-1, keepdims=True) + eps)


def norm_back(grad_out, normalized, scaling, norm_gain):
    weighted = grad_out * norm_gain
    return scaling * (
        weighted - normalized * jnp.mean(weighted * normalized, axis=-1, keepdims=True)
    )


def rotary_tables(positions, head_size):
    halfway = head_size // 2
    frequency = rope_base ** (-2.0 * jnp.arange(halfway, dtype=jnp.float32) / head_size)
    angles = positions.astype(jnp.float32)[:, None] * frequency[None, :]
    return (jnp.cos(angles)[:, None, :], jnp.sin(angles)[:, None, :])


def rotate(source, cosine_table, sine_table):
    halfway = source.shape[-1] // 2
    leading = source[..., :halfway]
    trailing = source[..., halfway:]
    return jnp.concatenate(
        [
            leading * cosine_table - trailing * sine_table,
            trailing * cosine_table + leading * sine_table,
        ],
        axis=-1,
    )


def tp_sum(term):
    tp_count = lax.axis_size("tp")
    tp_index = lax.axis_index("tp")
    current = term.astype(jnp.bfloat16)
    half = current.shape[0] // 2
    upper = tp_index % 2
    core_pairs = [(device, device ^ 1) for device in range(tp_count)]
    kept = lax.dynamic_slice_in_dim(current, upper * half, half, 0)
    sent = lax.dynamic_slice_in_dim(current, (1 - upper) * half, half, 0)
    received = lax.ppermute(sent, "tp", core_pairs)
    total = kept.astype(jnp.float32) + received.astype(jnp.float32)
    step = 2
    while step < tp_count:
        mine = total.astype(jnp.bfloat16)
        pairs = [(device, device ^ step) for device in range(tp_count)]
        received = lax.ppermute(mine, "tp", pairs)
        total = mine.astype(jnp.float32) + received.astype(jnp.float32)
        step *= 2
    mine = total.astype(jnp.bfloat16)
    other = lax.ppermute(mine, "tp", core_pairs)
    joined = jnp.where(
        upper == 0,
        jnp.concatenate([mine, other], axis=0),
        jnp.concatenate([other, mine], axis=0),
    )
    return joined.astype(jnp.float32)


def swap_halves(local, axis_name):
    return lax.ppermute(local, axis_name, [(0, 1), (1, 0)])


def ctx_gather(local):
    other = swap_halves(local, "ctx")
    first = lax.axis_index("ctx") == 0
    return jnp.where(
        first, jnp.concatenate([local, other], axis=0), jnp.concatenate([other, local], axis=0)
    )


def ctx_scatter(full):
    rows = full.shape[0] // 2
    place = lax.axis_index("ctx")
    kept = lax.dynamic_slice_in_dim(full, place * rows, rows, 0)
    sent = lax.dynamic_slice_in_dim(full, (1 - place) * rows, rows, 0)
    received = swap_halves(sent.astype(jnp.bfloat16), "ctx")
    return kept.astype(jnp.bfloat16).astype(jnp.float32) + received.astype(jnp.float32)


def all_sum(value):
    total = value
    for axis_name in ("tp", "ctx", "fsdp"):
        count = lax.axis_size(axis_name)
        step = 1
        while step < count:
            pairs = [(device, device ^ step) for device in range(count)]
            total = total + lax.ppermute(total, axis_name, pairs)
            step *= 2
    return total


def shard_scatter(full):
    fsdp_count = lax.axis_size("fsdp")
    ctx_count = lax.axis_size("ctx")
    fsdp_bits = []
    step = 1
    while step < fsdp_count:
        fsdp_bits.append(step)
        step *= 2
    rows = full.shape[0] // (fsdp_count * ctx_count)
    current = full.astype(jnp.bfloat16).reshape((2,) * len(fsdp_bits) + (ctx_count, rows, -1))
    order = [("fsdp", 1), ("fsdp", 2), ("ctx", 1)] + [("fsdp", bit) for bit in fsdp_bits[2:]]
    for axis_name, bit in order:
        if axis_name == "fsdp":
            dim = len(fsdp_bits) - 1 - fsdp_bits.index(bit)
        else:
            dim = len(fsdp_bits)
        upper = (lax.axis_index(axis_name) // bit) % 2
        kept = lax.dynamic_slice_in_dim(current, upper, 1, dim)
        sent = lax.dynamic_slice_in_dim(current, 1 - upper, 1, dim)
        count = fsdp_count if axis_name == "fsdp" else ctx_count
        pairs = [(device, device ^ bit) for device in range(count)]
        received = lax.ppermute(sent.astype(jnp.bfloat16), axis_name, pairs)
        current = kept.astype(jnp.float32) + received.astype(jnp.float32)
    return current.reshape(rows, -1)


def shard_gather(local):
    fsdp_count = lax.axis_size("fsdp")
    ctx_count = lax.axis_size("ctx")
    fsdp_bits = []
    step = 1
    while step < fsdp_count:
        fsdp_bits.append(step)
        step *= 2
    current = local.reshape((1,) * (len(fsdp_bits) + 1) + local.shape)
    order = [("ctx", 1)] + [("fsdp", bit) for bit in fsdp_bits[2:]] + [("fsdp", 1), ("fsdp", 2)]
    for axis_name, bit in order:
        if axis_name == "fsdp":
            dim = len(fsdp_bits) - 1 - fsdp_bits.index(bit)
        else:
            dim = len(fsdp_bits)
        count = fsdp_count if axis_name == "fsdp" else ctx_count
        pairs = [(device, device ^ bit) for device in range(count)]
        received = lax.ppermute(current, axis_name, pairs)
        upper = (lax.axis_index(axis_name) // bit) % 2
        current = jnp.where(
            upper == 0,
            jnp.concatenate([current, received], axis=dim),
            jnp.concatenate([received, current], axis=dim),
        )
    return current.reshape(-1, local.shape[1])


def per_device(
    tokens,
    cotangent,
    segments,
    attention_norm_weight,
    query_gain,
    key_gain,
    feedforward_gain,
    query_weight,
    key_projection_matrix,
    value_projection_matrix,
    output_weight,
    gate_weight,
    up_weight,
    down_weight,
):
    row_count = tokens.shape[0]
    model_width = tokens.shape[1]
    head_size = query_gain.shape[1]
    local_heads = query_weight.shape[2] // head_size
    local_groups = key_projection_matrix.shape[2] // head_size
    per_group = local_heads // local_groups
    layer_count = query_weight.shape[0]
    seq_length = segments.shape[1]
    row_start = lax.axis_index("ctx") * row_count
    column_width = model_width // lax.axis_size("tp")
    column_start = lax.axis_index("tp") * column_width
    score_scale = head_size ** (-0.5)
    positions = row_start + jnp.arange(row_count, dtype=jnp.int32)
    segment_row = segments[0]
    query_ids = lax.dynamic_slice_in_dim(segment_row, row_start, row_count)
    key_positions = jnp.arange(seq_length, dtype=jnp.int32)
    allowed = (query_ids[:, None] == segment_row[None, :]) & (
        key_positions[None, :] <= positions[:, None]
    )
    cosine_table, sine_table = rotary_tables(positions, head_size)

    def column_share(grad_rows, normalized):
        gradient_portion = lax.dynamic_slice_in_dim(grad_rows, column_start, column_width, 1)
        unit_slice = lax.dynamic_slice_in_dim(normalized, column_start, column_width, 1)
        part_sum = jnp.sum(gradient_portion * unit_slice, axis=0)
        return lax.dynamic_update_slice_in_dim(
            jnp.zeros((model_width,), jnp.float32), part_sum, column_start, 0
        )

    def attention_scores(query_groups, key_groups):
        return (
            jnp.einsum(
                "qgrd,kgd->grqk", query_groups, key_groups, preferred_element_type=jnp.float32
            )
            * score_scale
        )

    weight_shards = (
        query_weight,
        key_projection_matrix,
        value_projection_matrix,
        output_weight,
        gate_weight,
        up_weight,
        down_weight,
    )
    widths = [member.shape[2] for member in weight_shards]
    edges = [0]
    for width in widths:
        edges.append(edges[-1] + width)

    def gather_layer(layer_index):
        if layer_index > 0:
            joined = jnp.concatenate([member[layer_index] for member in weight_shards], axis=1)
            full = lax.all_gather(joined, ("fsdp", "ctx"), axis=0, tiled=True)
            return tuple(full[:, edges[k] : edges[k + 1]] for k in range(len(widths)))
        early = jnp.concatenate([member[layer_index] for member in weight_shards[:3]], axis=1)
        early_full = shard_gather(early)
        late = jnp.concatenate([member[layer_index] for member in weight_shards[3:]], axis=1)
        late_full = lax.all_gather(late, ("fsdp", "ctx"), axis=0, tiled=True)
        pieces = []
        for k in range(len(widths)):
            if k < 3:
                pieces.append(early_full[:, edges[k] : edges[k + 1]])
            else:
                pieces.append(late_full[:, edges[k] - edges[3] : edges[k + 1] - edges[3]])
        return tuple(pieces)

    def scatter_terms(terms):
        joined = jnp.concatenate([term.astype(jnp.bfloat16) for term in terms], axis=1)
        owned = lax.psum_scatter(joined, ("fsdp", "ctx"), scatter_dimension=0, tiled=True)
        pieces = []
        start = 0
        for term in terms:
            pieces.append(owned[:, start : start + term.shape[1]].astype(jnp.float32))
            start += term.shape[1]
        return pieces

    def scatter_layer(terms, layer_index):
        if layer_index > 0:
            return tuple(scatter_terms(terms))
        split = terms[6].shape[1] // 3
        early = scatter_terms(list(terms[4:6]) + [terms[6][:, split:]])
        moved = list(terms[:4]) + [terms[6][:, :split]]
        joined = shard_scatter(
            jnp.concatenate([term.astype(jnp.bfloat16) for term in moved], axis=1)
        )
        late = []
        start = 0
        for term in moved:
            late.append(joined[:, start : start + term.shape[1]])
            start += term.shape[1]
        down_owned = jnp.concatenate([late[4], early[2]], axis=1)
        return tuple(late[:4] + early[:2] + [down_owned])

    kept_weights = []
    stored_layers = []
    hidden = tokens
    for layer_index in range(layer_count):
        gathered = gather_layer(layer_index)
        kept_weights.append(gathered)
        (
            forward_query_full,
            forward_key_full,
            forward_value_full,
            forward_output_full,
            forward_gate_full,
            forward_up_full,
            forward_down_full,
        ) = gathered
        forward_scale_one = row_scale(hidden)
        forward_normed = (hidden * forward_scale_one * attention_norm_weight[layer_index]).astype(
            jnp.bfloat16
        )
        query_raw = jnp.dot(
            forward_normed, forward_query_full, preferred_element_type=jnp.float32
        ).reshape(row_count, local_heads, head_size)
        key_raw = jnp.dot(
            forward_normed, forward_key_full, preferred_element_type=jnp.float32
        ).reshape(row_count, local_groups, head_size)
        values = jnp.dot(
            forward_normed, forward_value_full, preferred_element_type=jnp.float32
        ).astype(jnp.bfloat16)
        forward_query_scale = row_scale(query_raw)
        forward_query_unit = query_raw * forward_query_scale
        forward_key_scale = row_scale(key_raw)
        forward_key_unit = key_raw * forward_key_scale
        queries = rotate(
            forward_query_unit * query_gain[layer_index], cosine_table, sine_table
        ).astype(jnp.bfloat16)
        keys = rotate(forward_key_unit * key_gain[layer_index], cosine_table, sine_table).astype(
            jnp.bfloat16
        )
        keys = keys.reshape(row_count, local_groups * head_size)
        all_keys = ctx_gather(keys)
        all_values = ctx_gather(values)
        forward_query_groups = queries.reshape(row_count, local_groups, per_group, head_size)
        forward_key_groups = all_keys.reshape(seq_length, local_groups, head_size)
        forward_value_groups = all_values.reshape(seq_length, local_groups, head_size)
        forward_scores = attention_scores(forward_query_groups, forward_key_groups)
        exponent = jnp.where(allowed, jnp.exp(forward_scores), 0.0)
        forward_log_total = jnp.log(jnp.sum(exponent, axis=-1, keepdims=True))
        attention_probs = jnp.where(
            allowed, jnp.exp(forward_scores - forward_log_total), 0.0
        ).astype(jnp.bfloat16)
        forward_attended = jnp.einsum(
            "grqk,kgd->qgrd",
            attention_probs,
            forward_value_groups,
            preferred_element_type=jnp.float32,
        )
        forward_attended = forward_attended.astype(jnp.bfloat16).reshape(
            row_count, local_heads * head_size
        )
        forward_middle = hidden + tp_sum(contract_last(forward_attended, forward_output_full))
        forward_scale_two = row_scale(forward_middle)
        forward_feed_normed = (
            forward_middle * forward_scale_two * feedforward_gain[layer_index]
        ).astype(jnp.bfloat16)
        forward_gate_linear = jnp.dot(
            forward_feed_normed, forward_gate_full, preferred_element_type=jnp.float32
        )
        forward_up_linear = jnp.dot(
            forward_feed_normed, forward_up_full, preferred_element_type=jnp.float32
        )
        forward_activated = (jax.nn.silu(forward_gate_linear) * forward_up_linear).astype(
            jnp.bfloat16
        )
        result = forward_middle + tp_sum(contract_last(forward_activated, forward_down_full))
        forward_stored = (
            hidden,
            forward_scale_one,
            forward_normed,
            forward_query_unit,
            forward_query_scale,
            forward_key_unit,
            forward_key_scale,
            forward_query_groups,
            forward_key_groups,
            forward_value_groups,
            forward_log_total,
            forward_attended,
            forward_middle,
            forward_scale_two,
            forward_feed_normed,
            forward_gate_linear,
            forward_up_linear,
            forward_activated,
        )
        hidden = result
        stored_layers.append(forward_stored)
    grad_flow = cotangent
    weight_sums = [None] * layer_count
    gain_parts = [None] * layer_count
    for layer_index in reversed(range(layer_count)):
        gathered = kept_weights[layer_index]
        backward_stored = stored_layers[layer_index]
        query_full, key_full, value_full, output_full, gate_full, up_full, down_full = gathered
        (
            source,
            scale_one,
            normed,
            query_unit,
            query_scale,
            key_unit,
            key_scale,
            backward_query_groups,
            backward_key_groups,
            value_groups,
            log_total,
            attended,
            middle,
            scale_two,
            feed_normed,
            gate_linear,
            up_linear,
            activated,
        ) = backward_stored
        grad_half = grad_flow.astype(jnp.bfloat16)
        down_grad = contract_first(grad_half, activated)
        act_grad = jnp.dot(grad_half, down_full, preferred_element_type=jnp.float32)
        sigmoid_gate = jax.nn.sigmoid(gate_linear)
        gate_grad = (
            act_grad * up_linear * sigmoid_gate * (1.0 + gate_linear * (1.0 - sigmoid_gate))
        ).astype(jnp.bfloat16)
        up_grad = (act_grad * jax.nn.silu(gate_linear)).astype(jnp.bfloat16)
        gate_weight_grad = contract_first(feed_normed, gate_grad)
        up_weight_grad = contract_first(feed_normed, up_grad)
        feed_part = contract_last(gate_grad, gate_full) + contract_last(up_grad, up_full)
        feed_grad = tp_sum(feed_part)
        feed_unit = middle * scale_two
        feed_gain_grad = column_share(feed_grad, feed_unit)
        middle_grad = grad_flow + norm_back(
            feed_grad, feed_unit, scale_two, feedforward_gain[layer_index]
        )
        middle_half = middle_grad.astype(jnp.bfloat16)
        output_weight_grad = contract_first(middle_half, attended)
        attended_grad = jnp.dot(
            middle_half, output_full, preferred_element_type=jnp.float32
        ).astype(jnp.bfloat16)
        attended_grad = attended_grad.reshape(row_count, local_groups, per_group, head_size)
        scores = attention_scores(backward_query_groups, backward_key_groups)
        exact = jnp.where(allowed, jnp.exp(scores - log_total), 0.0)
        half_probs = exact.astype(jnp.bfloat16)
        value_grad = jnp.einsum(
            "grqk,qgrd->kgd", half_probs, attended_grad, preferred_element_type=jnp.float32
        )
        prob_grad = jnp.einsum(
            "qgrd,kgd->grqk", attended_grad, value_groups, preferred_element_type=jnp.float32
        )
        row_delta = jnp.sum(exact * prob_grad, axis=-1, keepdims=True)
        score_grad = (exact * (prob_grad - row_delta) * score_scale).astype(jnp.bfloat16)
        query_grad = jnp.einsum(
            "grqk,kgd->qgrd", score_grad, backward_key_groups, preferred_element_type=jnp.float32
        )
        query_grad = query_grad.reshape(row_count, local_heads, head_size)
        key_grad = jnp.einsum(
            "grqk,qgrd->kgd", score_grad, backward_query_groups, preferred_element_type=jnp.float32
        )
        key_own = ctx_scatter(key_grad.reshape(seq_length, local_groups * head_size))
        value_own = ctx_scatter(value_grad.reshape(seq_length, local_groups * head_size)).astype(
            jnp.bfloat16
        )
        query_turned = rotate(query_grad, cosine_table, -sine_table)
        key_turned = rotate(
            key_own.reshape(row_count, local_groups, head_size), cosine_table, -sine_table
        )
        query_gain_grad = jnp.sum(query_turned * query_unit, axis=(0, 1))
        key_gain_grad = jnp.sum(key_turned * key_unit, axis=(0, 1))
        query_pre = norm_back(
            query_turned, query_unit, query_scale, query_gain[layer_index]
        ).astype(jnp.bfloat16)
        query_pre = query_pre.reshape(row_count, local_heads * head_size)
        key_pre = norm_back(key_turned, key_unit, key_scale, key_gain[layer_index]).astype(
            jnp.bfloat16
        )
        key_pre = key_pre.reshape(row_count, local_groups * head_size)
        query_weight_grad = contract_first(normed, query_pre)
        key_weight_grad = contract_first(normed, key_pre)
        value_weight_grad = contract_first(normed, value_own)
        attention_part = (
            contract_last(query_pre, query_full)
            + contract_last(key_pre, key_full)
            + contract_last(value_own, value_full)
        )
        normed_grad = tp_sum(attention_part)
        source_unit = source * scale_one
        attention_gain_grad = column_share(normed_grad, source_unit)
        source_grad = middle_grad + norm_back(
            normed_grad, source_unit, scale_one, attention_norm_weight[layer_index]
        )
        weight_terms = (
            query_weight_grad,
            key_weight_grad,
            value_weight_grad,
            output_weight_grad,
            gate_weight_grad,
            up_weight_grad,
            down_grad,
        )
        gain_terms = (attention_gain_grad, query_gain_grad, key_gain_grad, feed_gain_grad)
        grad_flow, weight_terms, gain_terms = (source_grad, weight_terms, gain_terms)
        grad_query, grad_key, grad_value, grad_output, grad_gate, grad_up, grad_down = weight_terms
        weight_sums[layer_index] = scatter_layer(weight_terms, layer_index)
        gain_parts[layer_index] = gain_terms
    gain_stacks = [
        jnp.stack([member[which] for member in gain_parts]) for which in range(4)
    ]
    gain_edges = [0]
    for member in gain_stacks:
        gain_edges.append(gain_edges[-1] + member.shape[1])
    gain_joined = all_sum(jnp.concatenate(gain_stacks, axis=1))
    gain_totals = [
        gain_joined[:, gain_edges[which] : gain_edges[which + 1]] for which in range(4)
    ]
    stacked = [jnp.stack([member[which] for member in weight_sums]) for which in range(7)]
    return (
        hidden,
        grad_flow,
        gain_totals[0],
        gain_totals[1],
        gain_totals[2],
        gain_totals[3],
        stacked[0],
        stacked[1],
        stacked[2],
        stacked[3],
        stacked[4],
        stacked[5],
        stacked[6],
    )


def solution(mesh):
    in_specs = (
        P(("fsdp", "ctx"), None),
        P(("fsdp", "ctx"), None),
        P("fsdp", None),
        P(),
        P(),
        P(),
        P(),
        P(None, ("fsdp", "ctx"), "tp"),
        P(None, ("fsdp", "ctx"), "tp"),
        P(None, ("fsdp", "ctx"), "tp"),
        P(None, ("fsdp", "ctx"), "tp"),
        P(None, ("fsdp", "ctx"), "tp"),
        P(None, ("fsdp", "ctx"), "tp"),
        P(None, ("fsdp", "ctx"), "tp"),
    )
    out_specs = (
        P(("fsdp", "ctx"), None),
        P(("fsdp", "ctx"), None),
        P(),
        P(),
        P(),
        P(),
        P(None, ("fsdp", "ctx"), "tp"),
        P(None, ("fsdp", "ctx"), "tp"),
        P(None, ("fsdp", "ctx"), "tp"),
        P(None, ("fsdp", "ctx"), "tp"),
        P(None, ("fsdp", "ctx"), "tp"),
        P(None, ("fsdp", "ctx"), "tp"),
        P(None, ("fsdp", "ctx"), "tp"),
    )
    return jax.shard_map(
        per_device, mesh=mesh, in_specs=in_specs, out_specs=out_specs, check_vma=False
    )
```
